32 devices in a mesh: seq: 4 (over y, x), ctx: 8 (over z, core).
Axes of the slice: x: 2, y: 2, z: 4, core: 2. Of those that a mesh axis runs over, the one named last changes fastest.
Arguments:
- block_input: bfloat16 [4, 1024, 2048], P('seq', 'ctx'), may hold values from -6 to 6
- positions: int32 [4, 1024], P('seq', 'ctx'), may hold values from 0 to 1023, as said below
- segments: int32 [4, 1024], P('seq'), may hold values from 0 to 1, as said below
- cotangent: bfloat16 [4, 1024, 2048], P('seq', 'ctx'), may hold values from -6 to 6
- attn_gain: bfloat16 [2048], P(('seq', 'ctx')), may hold values from 0.5 to 1.5
- query_weight: bfloat16 [2048, 2048], P(('seq', 'ctx')), may hold values from -0.125 to 0.125
- key_weight: bfloat16 [2048, 256], P(('seq', 'ctx')), may hold values from -0.125 to 0.125
- value_weight: bfloat16 [2048, 256], P(('seq', 'ctx')), may hold values from -0.125 to 0.125
- out_weight: bfloat16 [2048, 2048], P(('seq', 'ctx')), may hold values from -0.75 to 0.75
- mlp_gain: bfloat16 [2048], P(('seq', 'ctx')), may hold values from 0.5 to 1.5
- gate_weight: bfloat16 [2048, 5632], P(('seq', 'ctx')), may hold values from -0.125 to 0.125
- up_weight: bfloat16 [2048, 5632], P(('seq', 'ctx')), may hold values from -0.125 to 0.125
- down_weight: bfloat16 [2048, 5632], P(('seq', 'ctx')), may hold values from -0.078125 to 0.078125
Outputs:
- block_output: bfloat16 [4, 1024, 2048], P('seq', 'ctx')
- input_grad: float32 [4, 1024, 2048], P('seq', 'ctx')
- attn_gain_grad: float32 [2048], P(('seq', 'ctx'))
- query_grad: float32 [2048, 2048], P(('seq', 'ctx'))
- key_grad: float32 [2048, 256], P(('seq', 'ctx'))
- value_grad: float32 [2048, 256], P(('seq', 'ctx'))
- out_grad: float32 [2048, 2048], P(('seq', 'ctx'))
- mlp_gain_grad: float32 [2048], P(('seq', 'ctx'))
- gate_grad: float32 [2048, 5632], P(('seq', 'ctx'))
- up_grad: float32 [2048, 5632], P(('seq', 'ctx'))
- down_grad: float32 [2048, 5632], P(('seq', 'ctx'))
The draws below stay inside these ranges and needn't reach their ends.
Inputs may be any that keep to these rules, and one draw needn't show every extreme that they name: `segments`: in each sequence the ids are 0 before one boundary and 1 from it on; the boundary lies between 640 and 896. The first document's positions rise by one and end at 1023; the second document's rise by one from 0.
All inputs are finite; a program needn't handle non-finite values.
Results may differ from the reference program's by a relative error of at most 0.017.
Values may be sent and summed in bfloat16 or wider, within the bound.
No kernel may reach another device: no remote copies, remote signals or barrier semaphores. Data moves between devices by JAX's collectives and lax.ppermute only.
A program may use at most 448 MiB of HBM per device.

```python
import jax
import jax.numpy as jnp
from jax import lax

D = 2048
HEADS = 32
KV_HEADS = 4
HEAD = 64
FF = 5632
KV_WIDTH = 256
LENGTH = 1024
SEQS = 4


def boundary(key):
    return 5 * LENGTH // 8 + jax.random.randint(jax.random.fold_in(key, 11), (SEQS,), 0, LENGTH // 4)


def draw_segments(key, part):
    cut_point = boundary(key)
    token_index = jnp.arange(LENGTH, dtype=jnp.int32)
    return (token_index[None, :] >= cut_point[:, None]).astype(jnp.int32)


def draw_positions(key, part):
    cut_point = boundary(key)
    offset = LENGTH - cut_point
    token_index = jnp.arange(LENGTH, dtype=jnp.int32)[None, :]
    return jnp.where(token_index < cut_point[:, None], token_index + offset[:, None], token_index - cut_point[:, None]).astype(jnp.int32)


def levels(key, dims, cuts, low, high):
    loudness = 1.0
    for dim, blocks in cuts:
        draws = jax.random.uniform(jax.random.fold_in(jax.random.fold_in(key, 6), dim), (blocks,), jnp.float32, low / len(cuts), high / len(cuts))
        loudness = loudness * jnp.repeat(jnp.exp(draws), dims[dim] // blocks).reshape((-1,) + (1,) * (len(dims) - 1 - dim))
    return loudness


def scatter_about(own_key, shape, width, bound, cuts=(), kind=jnp.bfloat16):
    drawn = jax.random.normal(own_key, shape, jnp.float32) * width
    if len(cuts) > 0:
        drawn = levels(own_key, shape, cuts, -0.22, 0.18) * drawn
    return jnp.clip(drawn, min=-bound, max=bound).astype(kind)


def setup_inputs(seed: int = 0) -> dict:
    key_of = jax.random.split(jax.random.key(seed), 14)
    block_input = scatter_about(key_of[0], (SEQS, LENGTH, D), 1.0, 6.0, ((0, 4), (1, 8)))
    positions = draw_positions(jax.random.fold_in(key_of[13], 71), 0)
    segments = draw_segments(jax.random.fold_in(key_of[13], 71), 0)
    cotangent = scatter_about(key_of[3], (SEQS, LENGTH, D), 1.0, 6.0, ((0, 4), (1, 8)))
    attn_gain = jnp.clip(1.0 + 0.1 * jax.random.normal(key_of[4], (D,), jnp.float32), 0.5, 1.5).astype(jnp.bfloat16)
    query_weight = scatter_about(key_of[5], (D, D), D ** -0.5, 0.125, ((0, 32),))
    key_weight = scatter_about(key_of[6], (D, KV_WIDTH), D ** -0.5, 0.125, ((0, 32),))
    value_weight = scatter_about(key_of[7], (D, KV_WIDTH), D ** -0.5, 0.125, ((0, 32),))
    out_weight = scatter_about(key_of[8], (D, D), (D // 32) ** -0.5, 0.75, ((0, 32),))
    mlp_gain = jnp.clip(1.0 + 0.1 * jax.random.normal(key_of[9], (D,), jnp.float32), 0.5, 1.5).astype(jnp.bfloat16)
    gate_weight = scatter_about(key_of[10], (D, FF), D ** -0.5, 0.125, ((0, 32),))
    up_weight = scatter_about(key_of[11], (D, FF), D ** -0.5, 0.125, ((0, 32),))
    down_weight = scatter_about(key_of[12], (D, FF), FF ** -0.5, 0.078125, ((0, 32),))
    return {"block_input": block_input, "positions": positions, "segments": segments, "cotangent": cotangent, "attn_gain": attn_gain, "query_weight": query_weight, "key_weight": key_weight, "value_weight": value_weight, "out_weight": out_weight, "mlp_gain": mlp_gain, "gate_weight": gate_weight, "up_weight": up_weight, "down_weight": down_weight}


EPSILON = 1e-05
MASKED = -1e+30
HIGH = lax.Precision.HIGHEST

@jax.custom_vjp
def low(v):
    return lax.optimization_barrier(v.astype(jnp.bfloat16)).astype(jnp.float32)

@jax.custom_vjp
def low_back(v):
    return v

def low_keep(v):
    return (low(v), None)

def low_pass(kept, grad):
    return (grad,)

def back_keep(v):
    return (v, None)

def back_low(kept, grad):
    return (low(grad),)
low.defvjp(low_keep, low_pass)
low_back.defvjp(back_keep, back_low)

def matmul(left, right):
    return jnp.dot(left, right, precision=HIGH)

def rms_norm(inputs, gain):
    return inputs * lax.rsqrt(lax.optimization_barrier(jnp.mean(inputs * inputs, axis=-1, keepdims=True)) + EPSILON) * gain

def rope_tables(position, head_size):
    half_size = head_size // 2
    inverse = 1.0 / 10000.0 ** (jnp.arange(half_size, dtype=jnp.float32) * 2.0 / head_size)
    angles = position.astype(jnp.float32)[:, None] * inverse[None, :]
    cosine = jnp.cos(angles)
    sine_table = jnp.sin(angles)
    return (jnp.concatenate([cosine, cosine], -1), jnp.concatenate([sine_table, sine_table], -1))

def rotate(values, cosine, sine_table):
    half_size = values.shape[-1] // 2
    turned = jnp.concatenate([-values[..., half_size:], values[..., :half_size]], -1)
    return values * cosine[:, None, :] + turned * sine_table[:, None, :]

def attention(queries, keys, values, seg_row):
    length = queries.shape[0]
    block_size = min(512, length)
    block_count = length // block_size
    grouped = queries.reshape(block_count, block_size, KV_HEADS, HEADS // KV_HEADS, HEAD)
    seg_query = seg_row.reshape(block_count, block_size)
    starts = jnp.arange(block_count, dtype=jnp.int32) * block_size
    key_index = jnp.arange(length, dtype=jnp.int32)

    def one_block(pieces):
        query_block, seg_block, block_start = pieces
        scores = low_back(jnp.einsum('tkgd,jkd->kgtj', query_block, keys, precision=HIGH) * HEAD ** (-0.5))
        query_index = block_start + jnp.arange(block_size, dtype=jnp.int32)
        allowed = (seg_block[:, None] == seg_row[None, :]) & (key_index[None, :] <= query_index[:, None])
        scores = jnp.where(allowed[None, None], scores, MASKED)
        soft_low = low(jax.nn.softmax(scores, axis=-1))
        mixed_out = jnp.einsum('kgtj,jkd->tkgd', soft_low, values, precision=HIGH)
        return mixed_out.reshape(block_size, HEADS * HEAD)
    return lax.map(jax.checkpoint(one_block), (grouped, seg_query, starts)).reshape(length, HEADS * HEAD)

def layer(inputs, position, seg_row, params):
    attn_gain, query_weight, key_weight, value_weight, out_weight, mlp_gain, gate_weight, up_weight, down_weight = params
    length = inputs.shape[0]
    normed1 = low(rms_norm(inputs, attn_gain))
    cosine, sine_table = rope_tables(position, HEAD)
    queries = low(rotate(low_back(matmul(normed1, query_weight)).reshape(length, HEADS, HEAD), cosine, sine_table))
    keys = low(rotate(low_back(matmul(normed1, key_weight)).reshape(length, KV_HEADS, HEAD), cosine, sine_table))
    values = low(low_back(matmul(normed1, value_weight))).reshape(length, KV_HEADS, HEAD)
    attn_low = low(low_back(attention(queries, keys, values, seg_row)))
    residual = inputs + low_back(matmul(attn_low, out_weight))
    normed2 = low(rms_norm(residual, mlp_gain))
    gate_proj = low_back(matmul(normed2, gate_weight))
    up_proj = low_back(matmul(normed2, up_weight))
    hidden = low(jax.nn.silu(gate_proj) * up_proj)
    return residual + low_back(matmul(hidden, down_weight.T))

def reference(block_input, positions, segments, cotangent, attn_gain, query_weight, key_weight, value_weight, out_weight, mlp_gain, gate_weight, up_weight, down_weight):
    params = tuple((item.astype(jnp.float32) for item in (attn_gain, query_weight, key_weight, value_weight, out_weight, mlp_gain, gate_weight, up_weight, down_weight)))

    def forward(inputs, weights):

        def one_sequence(pieces):
            return layer(pieces[0], pieces[1], pieces[2], weights)
        return lax.map(jax.checkpoint(one_sequence), (inputs, positions, segments))
    output, pull_back = jax.vjp(forward, block_input.astype(jnp.float32), params)
    input_grad, grads = pull_back(cotangent.astype(jnp.float32))
    return (output.astype(jnp.bfloat16), input_grad, grads[0], grads[1], grads[2], grads[3], grads[4], grads[5], grads[6], grads[7], grads[8])
```

```python
import jax
import jax.numpy as jnp
from jax import lax
from jax.experimental import pallas as pl
from jax.experimental.pallas import tpu as pltpu
from jax.sharding import PartitionSpec as P

HEADS = 32
KV_HEADS = 4
HEAD = 64


EPSILON = 1e-05
MASKED = -1e30


def rope_tables(position, head_size):
    half_size = head_size // 2
    inverse = 1.0 / 10000.0 ** (jnp.arange(half_size, dtype=jnp.float32) * 2.0 / head_size)
    angles = position.astype(jnp.float32)[:, None] * inverse[None, :]
    cosine = jnp.cos(angles)
    sine_table = jnp.sin(angles)
    return (jnp.concatenate([cosine, cosine], -1), jnp.concatenate([sine_table, sine_table], -1))


def rotate(values, cosine, sine_table):
    half_size = values.shape[-1] // 2
    turned = jnp.concatenate([-values[..., half_size:], values[..., :half_size]], -1)
    return values * cosine[:, None, :] + turned * sine_table[:, None, :]


def rms_scale(inputs):
    return lax.rsqrt(jnp.mean(inputs * inputs, axis=-1, keepdims=True) + EPSILON)


def norm_back(inputs, row_scale, gain, upstream):
    shaped = inputs * row_scale
    weighted = upstream * gain
    gain_term = jnp.sum(upstream * shaped, axis=0)
    return (
        row_scale * (weighted - shaped * jnp.mean(weighted * shaped, axis=-1, keepdims=True)),
        gain_term,
    )


def contract_rows(left, right):
    return lax.dot_general(
        left, right, (((0,), (0,)), ((), ())), preferred_element_type=jnp.float32
    )


def contract_cols(left, right):
    return lax.dot_general(
        left, right, (((1,), (1,)), ((), ())), preferred_element_type=jnp.float32
    )


def local_rows(
    block_input,
    positions,
    segments,
    cotangent,
    attn_gain,
    query_weight,
    key_weight,
    value_weight,
    out_weight,
    mlp_gain,
    gate_weight,
    up_weight,
    down_weight,
):
    row_count = block_input.shape[1]
    group_size = HEADS // KV_HEADS
    score_scale = HEAD ** (-0.5)
    inputs = block_input[0].astype(jnp.float32)
    seg_all = segments[0]
    length = seg_all.shape[0]
    block_size = min(512, length)
    block_count = length // block_size
    first_row = lax.axis_index("ctx") * row_count
    query_index = first_row + jnp.arange(row_count, dtype=jnp.int32)
    seg_rows = lax.dynamic_slice_in_dim(seg_all, first_row, row_count)
    cosine, sine_table = rope_tables(positions[0], HEAD)
    starts = jnp.arange(block_count, dtype=jnp.int32) * block_size
    seg_blocks = seg_all.reshape(block_count, block_size)

    def key_mask(seg_block, block_start):
        key_index = block_start + jnp.arange(block_size, dtype=jnp.int32)
        return (seg_rows[:, None] == seg_block[None, :]) & (
            key_index[None, :] <= query_index[:, None]
        )

    def guarded(compute, running):
        result = compute(running)
        return result

    attn_params = (
        lax.all_gather(attn_gain, ("seq", "ctx"), axis=0, tiled=True),
        lax.all_gather(query_weight, ("seq", "ctx"), axis=0, tiled=True),
        lax.all_gather(key_weight, ("seq", "ctx"), axis=0, tiled=True),
        lax.all_gather(value_weight, ("seq", "ctx"), axis=0, tiled=True),
        lax.all_gather(out_weight, ("seq", "ctx"), axis=0, tiled=True),
    )
    gain_one = attn_params[0].astype(jnp.float32)
    scale_one = rms_scale(inputs)
    normed1 = (inputs * scale_one * gain_one).astype(jnp.bfloat16)
    query_raw = jnp.dot(normed1, attn_params[1], preferred_element_type=jnp.float32)
    key_raw = jnp.dot(normed1, attn_params[2], preferred_element_type=jnp.float32)
    value_raw = jnp.dot(normed1, attn_params[3], preferred_element_type=jnp.float32)
    queries = rotate(query_raw.reshape(row_count, HEADS, HEAD), cosine, sine_table).astype(
        jnp.bfloat16
    )
    keys_local = (
        rotate(key_raw.reshape(row_count, KV_HEADS, HEAD), cosine, sine_table)
        .astype(jnp.bfloat16)
        .reshape(row_count, KV_HEADS * HEAD)
    )
    values_local = value_raw.astype(jnp.bfloat16)
    keys_all, values_all = (
        lax.all_gather(keys_local, "ctx", axis=0, tiled=True),
        lax.all_gather(values_local, "ctx", axis=0, tiled=True),
    )
    key_blocks = keys_all.reshape(block_count, block_size, KV_HEADS, HEAD)
    value_blocks = values_all.reshape(block_count, block_size, KV_HEADS, HEAD)
    query_group = queries.reshape(row_count, KV_HEADS, group_size, HEAD)

    def block_scores(key_block, allowed):
        scores = (
            jnp.einsum("tkgd,jkd->kgtj", query_group, key_block, preferred_element_type=jnp.float32)
            * score_scale
        )
        return jnp.where(allowed[None, None], scores, MASKED)

    def max_step(carry, pieces):
        key_block, seg_block, block_start = pieces
        allowed = key_mask(seg_block, block_start)

        def compute(running):
            run_max, run_sum = running
            scores = block_scores(key_block, allowed)
            new_max = jnp.maximum(run_max, jnp.max(scores, axis=-1))
            exponents = jnp.where(allowed[None, None], jnp.exp(scores - new_max[..., None]), 0.0)
            return (new_max, run_sum * jnp.exp(run_max - new_max) + jnp.sum(exponents, axis=-1))

        return (guarded(compute, carry), None)

    start_max = jnp.full((KV_HEADS, group_size, row_count), MASKED, jnp.float32)
    start_sum = jnp.zeros((KV_HEADS, group_size, row_count), jnp.float32)
    (run_max, run_sum), unused = lax.scan(
        max_step, (start_max, start_sum), (key_blocks, seg_blocks, starts)
    )
    log_sum = run_max + jnp.log(run_sum)

    def block_soft(key_block, allowed):
        scores = block_scores(key_block, allowed)
        return jnp.where(allowed[None, None], jnp.exp(scores - log_sum[..., None]), 0.0)

    def value_step(carry, pieces):
        key_block, value_block, seg_block, block_start = pieces
        allowed = key_mask(seg_block, block_start)

        def compute(running):
            acc_out, acc_fix = running
            soft_weights = block_soft(key_block, allowed)
            rounded = soft_weights.astype(jnp.bfloat16)
            leftover = (soft_weights - rounded.astype(jnp.float32)).astype(jnp.bfloat16)
            acc_out = acc_out + jnp.einsum(
                "kgtj,jkd->tkgd", rounded, value_block, preferred_element_type=jnp.float32
            )
            acc_fix = acc_fix + jnp.einsum(
                "kgtj,jkd->tkgd", leftover, value_block, preferred_element_type=jnp.float32
            )
            return (acc_out, acc_fix)

        return (guarded(compute, carry), None)

    zero_mix = jnp.zeros((row_count, KV_HEADS, group_size, HEAD), jnp.float32)
    (acc_out, acc_fix), unused = lax.scan(
        value_step, (zero_mix, zero_mix), (key_blocks, value_blocks, seg_blocks, starts)
    )
    attn_low = acc_out.reshape(row_count, HEADS * HEAD).astype(jnp.bfloat16)
    full_mix = acc_out + acc_fix
    residual = inputs + jnp.dot(attn_low, attn_params[4], preferred_element_type=jnp.float32)
    mlp_params = (
        lax.all_gather(mlp_gain, ("seq", "ctx"), axis=0, tiled=True),
        lax.all_gather(gate_weight, ("seq", "ctx"), axis=0, tiled=True),
        lax.all_gather(up_weight, ("seq", "ctx"), axis=0, tiled=True),
        lax.all_gather(down_weight, ("seq", "ctx"), axis=0, tiled=True),
    )
    gain_two = mlp_params[0].astype(jnp.float32)
    scale_two = rms_scale(residual)
    normed2 = (residual * scale_two * gain_two).astype(jnp.bfloat16)
    gate_proj = jnp.dot(normed2, mlp_params[1], preferred_element_type=jnp.float32)
    up_proj = jnp.dot(normed2, mlp_params[2], preferred_element_type=jnp.float32)
    sigmoid_gate = jax.nn.sigmoid(gate_proj)
    silu_gate = gate_proj * sigmoid_gate
    hidden = (silu_gate * up_proj).astype(jnp.bfloat16)
    block_output = (residual + contract_cols(hidden, mlp_params[3])).astype(jnp.bfloat16)
    out_back = cotangent[0]
    out_float = out_back.astype(jnp.float32)
    mlp_again = (
        lax.all_gather(mlp_gain, ("seq", "ctx"), axis=0, tiled=True),
        lax.all_gather(gate_weight, ("seq", "ctx"), axis=0, tiled=True),
        lax.all_gather(up_weight, ("seq", "ctx"), axis=0, tiled=True),
        lax.all_gather(down_weight, ("seq", "ctx"), axis=0, tiled=True),
    )
    down_grad = lax.psum_scatter(
        contract_rows(out_back, hidden), ("seq", "ctx"), scatter_dimension=0, tiled=True
    )
    hidden_back = jnp.dot(out_back, mlp_again[3], preferred_element_type=jnp.float32)
    gate_back = (
        hidden_back * up_proj * sigmoid_gate * (1.0 + gate_proj * (1.0 - sigmoid_gate))
    ).astype(jnp.bfloat16)
    upper_back = (hidden_back * silu_gate).astype(jnp.bfloat16)
    gate_full_grad = contract_rows(normed2, gate_back)
    up_full_grad = contract_rows(normed2, upper_back)
    normed2_back = contract_cols(gate_back, mlp_again[1]) + contract_cols(upper_back, mlp_again[2])
    residual_norm, mlp_gain_term = norm_back(
        residual, scale_two, mlp_again[0].astype(jnp.float32), normed2_back
    )
    mlp_sums = (
        lax.psum_scatter(mlp_gain_term, ("seq", "ctx"), scatter_dimension=0, tiled=True),
        lax.psum_scatter(gate_full_grad, ("seq", "ctx"), scatter_dimension=0, tiled=True),
        lax.psum_scatter(up_full_grad, ("seq", "ctx"), scatter_dimension=0, tiled=True),
    )
    residual_back = out_float + residual_norm
    attn_again = (
        lax.all_gather(attn_gain, ("seq", "ctx"), axis=0, tiled=True),
        lax.all_gather(query_weight, ("seq", "ctx"), axis=0, tiled=True),
        lax.all_gather(key_weight, ("seq", "ctx"), axis=0, tiled=True),
        lax.all_gather(value_weight, ("seq", "ctx"), axis=0, tiled=True),
        lax.all_gather(out_weight, ("seq", "ctx"), axis=0, tiled=True),
    )
    residual_low = residual_back.astype(jnp.bfloat16)
    out_full_grad = contract_rows(attn_low, residual_low)
    attn_back = contract_cols(residual_low, attn_again[4]).astype(jnp.bfloat16)
    grad_mix = attn_back.reshape(row_count, KV_HEADS, group_size, HEAD)
    delta_rows = jnp.transpose(jnp.sum(grad_mix.astype(jnp.float32) * full_mix, axis=-1), (1, 2, 0))

    def grad_step(carry, pieces):
        key_block, value_block, seg_block, block_start = pieces
        allowed = key_mask(seg_block, block_start)

        def compute(acc_query):
            soft_weights = block_soft(key_block, allowed)
            rounded = soft_weights.astype(jnp.bfloat16)
            value_part = jnp.einsum(
                "kgtj,tkgd->jkd", rounded, grad_mix, preferred_element_type=jnp.float32
            )
            soft_back = jnp.einsum(
                "tkgd,jkd->kgtj", grad_mix, value_block, preferred_element_type=jnp.float32
            )
            score_back = (soft_weights * (soft_back - delta_rows[..., None])).astype(jnp.bfloat16)
            acc_query = acc_query + jnp.einsum(
                "kgtj,jkd->tkgd", score_back, key_block, preferred_element_type=jnp.float32
            )
            key_part = jnp.einsum(
                "kgtj,tkgd->jkd", score_back, query_group, preferred_element_type=jnp.float32
            )
            return (acc_query, (key_part, value_part))

        return guarded(compute, carry)

    acc_query, (key_parts, value_parts) = lax.scan(
        grad_step, zero_mix, (key_blocks, value_blocks, seg_blocks, starts)
    )
    key_sums, value_sums = (
        lax.psum_scatter(
            key_parts.reshape(length, KV_HEADS * HEAD).astype(jnp.bfloat16),
            "ctx",
            scatter_dimension=0,
            tiled=True,
        ).astype(jnp.float32),
        lax.psum_scatter(
            value_parts.reshape(length, KV_HEADS * HEAD).astype(jnp.bfloat16),
            "ctx",
            scatter_dimension=0,
            tiled=True,
        ).astype(jnp.float32),
    )
    query_low = (
        rotate((acc_query * score_scale).reshape(row_count, HEADS, HEAD), cosine, -sine_table)
        .astype(jnp.bfloat16)
        .reshape(row_count, HEADS * HEAD)
    )
    key_low = (
        rotate((key_sums * score_scale).reshape(row_count, KV_HEADS, HEAD), cosine, -sine_table)
        .astype(jnp.bfloat16)
        .reshape(row_count, KV_HEADS * HEAD)
    )
    value_low = value_sums.astype(jnp.bfloat16)
    query_full_grad = contract_rows(normed1, query_low)
    key_full_grad = contract_rows(normed1, key_low)
    value_full_grad = contract_rows(normed1, value_low)
    normed1_back = (
        contract_cols(query_low, attn_again[1])
        + contract_cols(key_low, attn_again[2])
        + contract_cols(value_low, attn_again[3])
    )
    input_norm, attn_gain_term = norm_back(
        inputs, scale_one, attn_again[0].astype(jnp.float32), normed1_back
    )
    attn_sums = (
        lax.psum_scatter(attn_gain_term, ("seq", "ctx"), scatter_dimension=0, tiled=True),
        lax.psum_scatter(query_full_grad, ("seq", "ctx"), scatter_dimension=0, tiled=True),
        lax.psum_scatter(key_full_grad, ("seq", "ctx"), scatter_dimension=0, tiled=True),
        lax.psum_scatter(value_full_grad, ("seq", "ctx"), scatter_dimension=0, tiled=True),
        lax.psum_scatter(out_full_grad, ("seq", "ctx"), scatter_dimension=0, tiled=True),
    )
    input_grad = residual_back + input_norm
    return (
        block_output[None],
        input_grad[None],
        attn_sums[0],
        attn_sums[1],
        attn_sums[2],
        attn_sums[3],
        attn_sums[4],
        mlp_sums[0],
        mlp_sums[1],
        mlp_sums[2],
        down_grad,
    )


SEQ_X = [(0, 1), (1, 0), (2, 3), (3, 2)]
SEQ_Y = [(0, 2), (2, 0), (1, 3), (3, 1)]


def gather_ctx(block):
    return lax.all_gather(block, "ctx", axis=0, tiled=True)


def reduce_ctx(partial):
    return lax.psum_scatter(partial, "ctx", scatter_dimension=0, tiled=True)


def exchange_ctx(pieces):
    return lax.all_to_all(pieces, "ctx", 0, 0, tiled=True)


def gather_seq(block):
    rows, width = block.shape
    half = rows // 2
    mine = lax.axis_index("seq")
    from_x = lax.ppermute(block, "seq", SEQ_X)
    from_y = lax.ppermute(block, "seq", SEQ_Y)
    far_top = lax.ppermute(from_x[:half], "seq", SEQ_Y)
    far_low = lax.ppermute(from_y[half:], "seq", SEQ_X)
    whole = jnp.zeros((4 * rows, width), block.dtype)
    for piece, start in (
        (block, mine * rows),
        (from_x, (mine ^ 1) * rows),
        (from_y, (mine ^ 2) * rows),
        (far_top, (mine ^ 3) * rows),
        (far_low, (mine ^ 3) * rows + half),
    ):
        whole = lax.dynamic_update_slice_in_dim(whole, piece, start, 0)
    return whole


def reduce_seq(partial):
    rows = partial.shape[0] // 4
    half = rows // 2
    mine = lax.axis_index("seq")

    def part(other, low):
        start = (mine ^ other) * rows + (half if low else 0)
        return lax.dynamic_slice_in_dim(partial, start, half, 0)

    def add(left, right):
        return left.astype(jnp.float32) + right.astype(jnp.float32)

    top_near = lax.ppermute(part(1, False), "seq", SEQ_X)
    top_far = lax.ppermute(part(3, False), "seq", SEQ_X)
    low_near = lax.ppermute(part(2, True), "seq", SEQ_Y)
    low_far = lax.ppermute(part(3, True), "seq", SEQ_Y)
    top_send = add(part(2, False), top_far).astype(jnp.bfloat16)
    low_send = add(part(1, True), low_far).astype(jnp.bfloat16)
    top_last = lax.ppermute(top_send, "seq", SEQ_Y)
    low_last = lax.ppermute(low_send, "seq", SEQ_X)
    return jnp.concatenate(
        [
            add(part(0, False), top_near) + top_last.astype(jnp.float32),
            add(part(0, True), low_near) + low_last.astype(jnp.float32),
        ],
        axis=0,
    ).astype(jnp.bfloat16)


def to_slices(weight):
    rows, width = weight.shape
    return jnp.transpose(weight.reshape(rows, 8, width // 8), (1, 0, 2))


def from_slices(pieces):
    count, rows, width = pieces.shape
    return jnp.transpose(pieces, (1, 0, 2)).reshape(rows, count * width)


def head_slices(weight):
    rows = weight.shape[0]
    split = weight.reshape(rows, KV_HEADS, 8, HEAD)
    return jnp.transpose(split, (2, 0, 1, 3)).reshape(8, rows, KV_HEADS * HEAD)


def from_head_slices(pieces):
    rows = pieces.shape[1]
    split = pieces.reshape(8, rows, KV_HEADS, HEAD)
    return jnp.transpose(split, (1, 2, 0, 3)).reshape(rows, HEADS * HEAD)


def attend_mask(edge, first_row, block, span):
    row = first_row + lax.broadcasted_iota(jnp.int32, (block, span), 0)
    column = lax.broadcasted_iota(jnp.int32, (block, span), 1)
    return (column <= row) & (column >= jnp.where(row >= edge, edge, 0))


def soft_rows(query, key, allowed):
    scores = lax.dot_general(
        query, key, (((1,), (1,)), ((), ())), preferred_element_type=jnp.float32
    )
    scores = jnp.where(allowed, scores, MASKED)
    exponents = jnp.exp(scores - jnp.max(scores, axis=-1, keepdims=True))
    return exponents * (1.0 / jnp.sum(exponents, axis=-1, keepdims=True))


def attend_kernel(edge_ref, query_ref, key_ref, value_ref, mix_ref, *, block, blocks):
    step = pl.program_id(1)
    for index in range(blocks):

        @pl.when(step == index)
        def _(index=index):
            span = (index + 1) * block
            allowed = attend_mask(edge_ref[0], index * block, block, span)
            mixed = []
            for head in range(2):
                cut = slice(head * HEAD, (head + 1) * HEAD)
                soft = soft_rows(query_ref[:, cut], key_ref[:span, cut], allowed)
                mixed.append(
                    jnp.dot(
                        soft.astype(jnp.bfloat16),
                        value_ref[:span, cut],
                        preferred_element_type=jnp.float32,
                    )
                )
            mix_ref[...] = jnp.concatenate(mixed, axis=-1).astype(mix_ref.dtype)


def attend_back_kernel(
    edge_ref,
    query_ref,
    key_ref,
    value_ref,
    back_ref,
    query_back_ref,
    key_back_ref,
    value_back_ref,
    *,
    block,
    blocks,
    score_scale,
):
    step = pl.program_id(1)

    @pl.when(step == 0)
    def _():
        key_back_ref[...] = jnp.zeros_like(key_back_ref)
        value_back_ref[...] = jnp.zeros_like(value_back_ref)

    for index in range(blocks):

        @pl.when(step == index)
        def _(index=index):
            span = (index + 1) * block
            allowed = attend_mask(edge_ref[0], index * block, block, span)
            query_parts, key_parts, value_parts = [], [], []
            for head in range(2):
                cut = slice(head * HEAD, (head + 1) * HEAD)
                query, key = query_ref[:, cut], key_ref[:span, cut]
                back = back_ref[:, cut]
                soft = soft_rows(query, key, allowed)
                soft_back = contract_cols(back, value_ref[:span, cut])
                delta = jnp.sum(soft * soft_back, axis=-1, keepdims=True)
                score_back = (soft * (soft_back - delta)).astype(jnp.bfloat16)
                query_parts.append(
                    jnp.dot(score_back, key, preferred_element_type=jnp.float32) * score_scale
                )
                key_parts.append(contract_rows(score_back, query))
                value_parts.append(contract_rows(soft.astype(jnp.bfloat16), back))
            query_back_ref[...] = jnp.concatenate(query_parts, axis=-1)
            key_back_ref[:span, :] += jnp.concatenate(key_parts, axis=-1)
            value_back_ref[:span, :] += jnp.concatenate(value_parts, axis=-1)


def attend_specs(length, block):
    rows = pl.BlockSpec((block, 2 * HEAD), lambda pair, step: (step, pair))
    whole = pl.BlockSpec((length, 2 * HEAD), lambda pair, step: (0, pair))
    edge = pl.BlockSpec(memory_space=pltpu.SMEM)
    return edge, rows, whole


def attend(edge, queries, keys, values):
    length, width = queries.shape
    block = 256
    blocks = length // block
    scalar, rows, whole = attend_specs(length, block)

    def body(*refs):
        attend_kernel(*refs, block=block, blocks=blocks)

    return pl.pallas_call(
        body,
        name="attend",
        grid=(width // (2 * HEAD), blocks),
        in_specs=[scalar, rows, whole, whole],
        out_specs=rows,
        out_shape=jax.ShapeDtypeStruct((length, width), jnp.bfloat16),
    )(edge, queries, keys, values)


def attend_back(edge, queries, keys, values, back, score_scale):
    length, width = queries.shape
    block = 256
    blocks = length // block
    scalar, rows, whole = attend_specs(length, block)

    def body(*refs):
        attend_back_kernel(*refs, block=block, blocks=blocks, score_scale=score_scale)

    shape = jax.ShapeDtypeStruct((length, width), jnp.float32)
    return pl.pallas_call(
        body,
        name="attend_back",
        grid=(width // (2 * HEAD), blocks),
        in_specs=[scalar, rows, whole, whole, rows],
        out_specs=(rows, whole, whole),
        out_shape=(shape, shape, shape),
    )(edge, queries, keys, values, back)


def turn(values, cosine, sine_table):
    half = HEAD // 2
    lane = lax.broadcasted_iota(jnp.int32, values.shape, 1) % HEAD
    turned = jnp.where(
        lane < half, -jnp.roll(values, -half, axis=1), jnp.roll(values, half, axis=1)
    )
    return values * cosine + turned * sine_table


def local_columns(
    block_input,
    positions,
    segments,
    cotangent,
    attn_gain,
    query_weight,
    key_weight,
    value_weight,
    out_weight,
    mlp_gain,
    gate_weight,
    up_weight,
    down_weight,
):
    f32, bf16 = jnp.float32, jnp.bfloat16
    score_scale = HEAD ** (-0.5)
    length = segments.shape[1]
    rows = query_weight.shape[0]
    head_width = KV_HEADS * HEAD
    inputs = block_input[0].astype(f32)
    out_back = cotangent[0]
    gain_one = attn_gain.astype(f32)[:, None]
    gain_two = mlp_gain.astype(f32)[:, None]

    def fold(weight, gain):
        return (weight.astype(f32) * gain).astype(bf16)

    inputs_all = gather_ctx(block_input[0])
    key_value = jnp.concatenate([fold(key_weight, gain_one), fold(value_weight, gain_one)], axis=1)
    attn_pieces = jnp.concatenate(
        [
            head_slices(fold(query_weight, gain_one)),
            jnp.broadcast_to(key_value[None], (8,) + key_value.shape),
        ],
        axis=2,
    )
    attn_cols = gather_seq(exchange_ctx(attn_pieces).reshape(8 * rows, 3 * head_width))
    out_rows = gather_seq(out_weight)
    gate_cols = gather_seq(
        exchange_ctx(to_slices(fold(gate_weight, gain_two))).reshape(8 * rows, -1)
    )
    up_cols = gather_seq(exchange_ctx(to_slices(fold(up_weight, gain_two))).reshape(8 * rows, -1))
    down_cols = gather_seq(exchange_ctx(to_slices(down_weight)).reshape(8 * rows, -1))
    back_all = gather_ctx(out_back)

    edge = jnp.sum((segments[0] == 0).astype(jnp.int32))
    token = jnp.arange(length, dtype=jnp.int32)
    position = jnp.where(token < edge, token + (length - edge), token - edge)
    cosine, sine_table = rope_tables(position, HEAD)
    cosine = jnp.tile(cosine, (1, KV_HEADS))
    sine_table = jnp.tile(sine_table, (1, KV_HEADS))
    edge = edge[None]

    wide = inputs_all.astype(f32)
    shaped_all = (wide * rms_scale(wide)).astype(bf16)
    raw = jnp.dot(shaped_all, attn_cols, preferred_element_type=f32)
    queries = turn(raw[:, :head_width], cosine, sine_table).astype(bf16)
    keys = turn(raw[:, head_width : 2 * head_width], cosine, sine_table).astype(bf16)
    values = raw[:, 2 * head_width :].astype(bf16)
    queries = queries * jnp.asarray(score_scale, bf16)
    attn_low = attend(edge, queries, keys, values)
    mixed = jnp.dot(attn_low, out_rows, preferred_element_type=f32).astype(bf16)
    residual = inputs + reduce_ctx(mixed).astype(f32)
    scale_two = rms_scale(residual)
    shaped_two = residual * scale_two
    normed_all = gather_ctx(shaped_two.astype(bf16))
    gate_proj = jnp.dot(normed_all, gate_cols, preferred_element_type=f32)
    up_proj = jnp.dot(normed_all, up_cols, preferred_element_type=f32)
    sigmoid_gate = jax.nn.sigmoid(gate_proj)
    silu_gate = gate_proj * sigmoid_gate
    hidden = (silu_gate * up_proj).astype(bf16)
    hidden_back = jnp.dot(back_all, down_cols, preferred_element_type=f32)
    gate_back = (
        hidden_back * up_proj * sigmoid_gate * (1.0 + gate_proj * (1.0 - sigmoid_gate))
    ).astype(bf16)
    upper_back = (hidden_back * silu_gate).astype(bf16)
    weighted = reduce_ctx(
        (contract_cols(gate_back, gate_cols) + contract_cols(upper_back, up_cols)).astype(bf16)
    ).astype(f32)
    residual_back = out_back.astype(f32) + scale_two * (
        weighted - shaped_two * jnp.mean(weighted * shaped_two, axis=-1, keepdims=True)
    )
    low_all = gather_ctx(residual_back.astype(bf16))
    attn_back = contract_cols(low_all, out_rows).astype(bf16)
    query_back, key_back, value_back = attend_back(
        edge, queries, keys, values, attn_back, score_scale
    )
    heads_back = jnp.concatenate(
        [
            turn(query_back, cosine, -sine_table).astype(bf16),
            turn(key_back, cosine, -sine_table).astype(bf16),
            value_back.astype(bf16),
        ],
        axis=1,
    )
    weighted_one = reduce_ctx(contract_cols(heads_back, attn_cols).astype(bf16)).astype(f32)
    scale_one = rms_scale(inputs)
    shaped_one = inputs * scale_one
    input_grad = residual_back + scale_one * (
        weighted_one - shaped_one * jnp.mean(weighted_one * shaped_one, axis=-1, keepdims=True)
    )
    block_output = (
        residual + reduce_ctx(contract_cols(hidden, down_cols).astype(bf16)).astype(f32)
    ).astype(bf16)

    def column_grad(left, right):
        slices = reduce_seq(contract_rows(left, right).astype(bf16))
        return exchange_ctx(slices.reshape(8, rows, -1)).astype(f32)

    down_grad = from_slices(column_grad(back_all, hidden))
    gate_rows = from_slices(column_grad(normed_all, gate_back))
    up_rows = from_slices(column_grad(normed_all, upper_back))
    out_grad = reduce_seq(contract_rows(attn_low, low_all).astype(bf16)).astype(f32)
    attn_grad = column_grad(shaped_all, heads_back)
    query_rows = from_head_slices(attn_grad[:, :, :head_width])
    pair_rows = jnp.sum(attn_grad[:, :, head_width:], axis=0)
    key_rows, value_rows = pair_rows[:, :head_width], pair_rows[:, head_width:]

    def row_sum(weight, grad):
        return jnp.sum(weight.astype(f32) * grad, axis=1)

    attn_gain_grad = (
        row_sum(query_weight, query_rows)
        + row_sum(key_weight, key_rows)
        + row_sum(value_weight, value_rows)
    )
    mlp_gain_grad = row_sum(gate_weight, gate_rows) + row_sum(up_weight, up_rows)
    return (
        block_output[None],
        input_grad[None],
        attn_gain_grad,
        query_rows * gain_one,
        key_rows * gain_one,
        value_rows * gain_one,
        out_grad,
        mlp_gain_grad,
        gate_rows * gain_two,
        up_rows * gain_two,
        down_grad,
    )


def solution(mesh):
    placed = (
        P("seq", "ctx", None),
        P("seq", "ctx"),
        P("seq", None),
        P("seq", "ctx", None),
        P(("seq", "ctx")),
        P(("seq", "ctx"), None),
        P(("seq", "ctx"), None),
        P(("seq", "ctx"), None),
        P(("seq", "ctx"), None),
        P(("seq", "ctx")),
        P(("seq", "ctx"), None),
        P(("seq", "ctx"), None),
        P(("seq", "ctx"), None),
    )
    seq_count, ctx_count = mesh.shape["seq"], mesh.shape["ctx"]

    def run(*args):
        width = args[0].shape[2]
        fits = (
            seq_count == KV_HEADS == 4
            and ctx_count == HEADS // KV_HEADS == 8
            and width == seq_count * ctx_count * HEAD
        )
        return jax.shard_map(
            local_columns if fits else local_rows,
            mesh=mesh,
            in_specs=placed,
            out_specs=(
                P("seq", "ctx", None),
                P("seq", "ctx", None),
                P(("seq", "ctx")),
                P(("seq", "ctx"), None),
                P(("seq", "ctx"), None),
                P(("seq", "ctx"), None),
                P(("seq", "ctx"), None),
                P(("seq", "ctx")),
                P(("seq", "ctx"), None),
                P(("seq", "ctx"), None),
                P(("seq", "ctx"), None),
            ),
            check_vma=False,
        )(*args)

    return run
```

```python
import jax
import jax.numpy as jnp
from jax import lax
from jax.experimental import pallas as pl
from jax.experimental.pallas import tpu as pltpu
from jax.sharding import PartitionSpec as P

HEADS = 32
KV_HEADS = 4
HEAD = 64


EPSILON = 1e-05
MASKED = -1e30


def rope_tables(position, head_size):
    half_size = head_size // 2
    inverse = 1.0 / 10000.0 ** (jnp.arange(half_size, dtype=jnp.float32) * 2.0 / head_size)
    angles = position.astype(jnp.float32)[:, None] * inverse[None, :]
    cosine = jnp.cos(angles)
    sine_table = jnp.sin(angles)
    return (jnp.concatenate([cosine, cosine], -1), jnp.concatenate([sine_table, sine_table], -1))


def rotate(values, cosine, sine_table):
    half_size = values.shape[-1] // 2
    turned = jnp.concatenate([-values[..., half_size:], values[..., :half_size]], -1)
    return values * cosine[:, None, :] + turned * sine_table[:, None, :]


def rms_scale(inputs):
    return lax.rsqrt(jnp.mean(inputs * inputs, axis=-1, keepdims=True) + EPSILON)


def norm_back(inputs, row_scale, gain, upstream):
    shaped = inputs * row_scale
    weighted = upstream * gain
    gain_term = jnp.sum(upstream * shaped, axis=0)
    return (
        row_scale * (weighted - shaped * jnp.mean(weighted * shaped, axis=-1, keepdims=True)),
        gain_term,
    )


def contract_rows(left, right):
    return lax.dot_general(
        left, right, (((0,), (0,)), ((), ())), preferred_element_type=jnp.float32
    )


def contract_cols(left, right):
    return lax.dot_general(
        left, right, (((1,), (1,)), ((), ())), preferred_element_type=jnp.float32
    )


def local_rows(
    block_input,
    positions,
    segments,
    cotangent,
    attn_gain,
    query_weight,
    key_weight,
    value_weight,
    out_weight,
    mlp_gain,
    gate_weight,
    up_weight,
    down_weight,
):
    row_count = block_input.shape[1]
    group_size = HEADS // KV_HEADS
    score_scale = HEAD ** (-0.5)
    inputs = block_input[0].astype(jnp.float32)
    seg_all = segments[0]
    length = seg_all.shape[0]
    block_size = min(512, length)
    block_count = length // block_size
    first_row = lax.axis_index("ctx") * row_count
    query_index = first_row + jnp.arange(row_count, dtype=jnp.int32)
    seg_rows = lax.dynamic_slice_in_dim(seg_all, first_row, row_count)
    cosine, sine_table = rope_tables(positions[0], HEAD)
    starts = jnp.arange(block_count, dtype=jnp.int32) * block_size
    seg_blocks = seg_all.reshape(block_count, block_size)

    def key_mask(seg_block, block_start):
        key_index = block_start + jnp.arange(block_size, dtype=jnp.int32)
        return (seg_rows[:, None] == seg_block[None, :]) & (
            key_index[None, :] <= query_index[:, None]
        )

    def guarded(compute, running):
        result = compute(running)
        return result

    attn_params = (
        lax.all_gather(attn_gain, ("seq", "ctx"), axis=0, tiled=True),
        lax.all_gather(query_weight, ("seq", "ctx"), axis=0, tiled=True),
        lax.all_gather(key_weight, ("seq", "ctx"), axis=0, tiled=True),
        lax.all_gather(value_weight, ("seq", "ctx"), axis=0, tiled=True),
        lax.all_gather(out_weight, ("seq", "ctx"), axis=0, tiled=True),
    )
    gain_one = attn_params[0].astype(jnp.float32)
    scale_one = rms_scale(inputs)
    normed1 = (inputs * scale_one * gain_one).astype(jnp.bfloat16)
    query_raw = jnp.dot(normed1, attn_params[1], preferred_element_type=jnp.float32)
    key_raw = jnp.dot(normed1, attn_params[2], preferred_element_type=jnp.float32)
    value_raw = jnp.dot(normed1, attn_params[3], preferred_element_type=jnp.float32)
    queries = rotate(query_raw.reshape(row_count, HEADS, HEAD), cosine, sine_table).astype(
        jnp.bfloat16
    )
    keys_local = (
        rotate(key_raw.reshape(row_count, KV_HEADS, HEAD), cosine, sine_table)
        .astype(jnp.bfloat16)
        .reshape(row_count, KV_HEADS * HEAD)
    )
    values_local = value_raw.astype(jnp.bfloat16)
    keys_all, values_all = (
        lax.all_gather(keys_local, "ctx", axis=0, tiled=True),
        lax.all_gather(values_local, "ctx", axis=0, tiled=True),
    )
    key_blocks = keys_all.reshape(block_count, block_size, KV_HEADS, HEAD)
    value_blocks = values_all.reshape(block_count, block_size, KV_HEADS, HEAD)
    query_group = queries.reshape(row_count, KV_HEADS, group_size, HEAD)

    def block_scores(key_block, allowed):
        scores = (
            jnp.einsum("tkgd,jkd->kgtj", query_group, key_block, preferred_element_type=jnp.float32)
            * score_scale
        )
        return jnp.where(allowed[None, None], scores, MASKED)

    def max_step(carry, pieces):
        key_block, seg_block, block_start = pieces
        allowed = key_mask(seg_block, block_start)

        def compute(running):
            run_max, run_sum = running
            scores = block_scores(key_block, allowed)
            new_max = jnp.maximum(run_max, jnp.max(scores, axis=-1))
            exponents = jnp.where(allowed[None, None], jnp.exp(scores - new_max[..., None]), 0.0)
            return (new_max, run_sum * jnp.exp(run_max - new_max) + jnp.sum(exponents, axis=-1))

        return (guarded(compute, carry), None)

    start_max = jnp.full((KV_HEADS, group_size, row_count), MASKED, jnp.float32)
    start_sum = jnp.zeros((KV_HEADS, group_size, row_count), jnp.float32)
    (run_max, run_sum), unused = lax.scan(
        max_step, (start_max, start_sum), (key_blocks, seg_blocks, starts)
    )
    log_sum = run_max + jnp.log(run_sum)

    def block_soft(key_block, allowed):
        scores = block_scores(key_block, allowed)
        return jnp.where(allowed[None, None], jnp.exp(scores - log_sum[..., None]), 0.0)

    def value_step(carry, pieces):
        key_block, value_block, seg_block, block_start = pieces
        allowed = key_mask(seg_block, block_start)

        def compute(running):
            acc_out, acc_fix = running
            soft_weights = block_soft(key_block, allowed)
            rounded = soft_weights.astype(jnp.bfloat16)
            leftover = (soft_weights - rounded.astype(jnp.float32)).astype(jnp.bfloat16)
            acc_out = acc_out + jnp.einsum(
                "kgtj,jkd->tkgd", rounded, value_block, preferred_element_type=jnp.float32
            )
            acc_fix = acc_fix + jnp.einsum(
                "kgtj,jkd->tkgd", leftover, value_block, preferred_element_type=jnp.float32
            )
            return (acc_out, acc_fix)

        return (guarded(compute, carry), None)

    zero_mix = jnp.zeros((row_count, KV_HEADS, group_size, HEAD), jnp.float32)
    (acc_out, acc_fix), unused = lax.scan(
        value_step, (zero_mix, zero_mix), (key_blocks, value_blocks, seg_blocks, starts)
    )
    attn_low = acc_out.reshape(row_count, HEADS * HEAD).astype(jnp.bfloat16)
    full_mix = acc_out + acc_fix
    residual = inputs + jnp.dot(attn_low, attn_params[4], preferred_element_type=jnp.float32)
    mlp_params = (
        lax.all_gather(mlp_gain, ("seq", "ctx"), axis=0, tiled=True),
        lax.all_gather(gate_weight, ("seq", "ctx"), axis=0, tiled=True),
        lax.all_gather(up_weight, ("seq", "ctx"), axis=0, tiled=True),
        lax.all_gather(down_weight, ("seq", "ctx"), axis=0, tiled=True),
    )
    gain_two = mlp_params[0].astype(jnp.float32)
    scale_two = rms_scale(residual)
    normed2 = (residual * scale_two * gain_two).astype(jnp.bfloat16)
    gate_proj = jnp.dot(normed2, mlp_params[1], preferred_element_type=jnp.float32)
    up_proj = jnp.dot(normed2, mlp_params[2], preferred_element_type=jnp.float32)
    sigmoid_gate = jax.nn.sigmoid(gate_proj)
    silu_gate = gate_proj * sigmoid_gate
    hidden = (silu_gate * up_proj).astype(jnp.bfloat16)
    block_output = (residual + contract_cols(hidden, mlp_params[3])).astype(jnp.bfloat16)
    out_back = cotangent[0]
    out_float = out_back.astype(jnp.float32)
    mlp_again = (
        lax.all_gather(mlp_gain, ("seq", "ctx"), axis=0, tiled=True),
        lax.all_gather(gate_weight, ("seq", "ctx"), axis=0, tiled=True),
        lax.all_gather(up_weight, ("seq", "ctx"), axis=0, tiled=True),
        lax.all_gather(down_weight, ("seq", "ctx"), axis=0, tiled=True),
    )
    down_grad = lax.psum_scatter(
        contract_rows(out_back, hidden), ("seq", "ctx"), scatter_dimension=0, tiled=True
    )
    hidden_back = jnp.dot(out_back, mlp_again[3], preferred_element_type=jnp.float32)
    gate_back = (
        hidden_back * up_proj * sigmoid_gate * (1.0 + gate_proj * (1.0 - sigmoid_gate))
    ).astype(jnp.bfloat16)
    upper_back = (hidden_back * silu_gate).astype(jnp.bfloat16)
    gate_full_grad = contract_rows(normed2, gate_back)
    up_full_grad = contract_rows(normed2, upper_back)
    normed2_back = contract_cols(gate_back, mlp_again[1]) + contract_cols(upper_back, mlp_again[2])
    residual_norm, mlp_gain_term = norm_back(
        residual, scale_two, mlp_again[0].astype(jnp.float32), normed2_back
    )
    mlp_sums = (
        lax.psum_scatter(mlp_gain_term, ("seq", "ctx"), scatter_dimension=0, tiled=True),
        lax.psum_scatter(gate_full_grad, ("seq", "ctx"), scatter_dimension=0, tiled=True),
        lax.psum_scatter(up_full_grad, ("seq", "ctx"), scatter_dimension=0, tiled=True),
    )
    residual_back = out_float + residual_norm
    attn_again = (
        lax.all_gather(attn_gain, ("seq", "ctx"), axis=0, tiled=True),
        lax.all_gather(query_weight, ("seq", "ctx"), axis=0, tiled=True),
        lax.all_gather(key_weight, ("seq", "ctx"), axis=0, tiled=True),
        lax.all_gather(value_weight, ("seq", "ctx"), axis=0, tiled=True),
        lax.all_gather(out_weight, ("seq", "ctx"), axis=0, tiled=True),
    )
    residual_low = residual_back.astype(jnp.bfloat16)
    out_full_grad = contract_rows(attn_low, residual_low)
    attn_back = contract_cols(residual_low, attn_again[4]).astype(jnp.bfloat16)
    grad_mix = attn_back.reshape(row_count, KV_HEADS, group_size, HEAD)
    delta_rows = jnp.transpose(jnp.sum(grad_mix.astype(jnp.float32) * full_mix, axis=-1), (1, 2, 0))

    def grad_step(carry, pieces):
        key_block, value_block, seg_block, block_start = pieces
        allowed = key_mask(seg_block, block_start)

        def compute(acc_query):
            soft_weights = block_soft(key_block, allowed)
            rounded = soft_weights.astype(jnp.bfloat16)
            value_part = jnp.einsum(
                "kgtj,tkgd->jkd", rounded, grad_mix, preferred_element_type=jnp.float32
            )
            soft_back = jnp.einsum(
                "tkgd,jkd->kgtj", grad_mix, value_block, preferred_element_type=jnp.float32
            )
            score_back = (soft_weights * (soft_back - delta_rows[..., None])).astype(jnp.bfloat16)
            acc_query = acc_query + jnp.einsum(
                "kgtj,jkd->tkgd", score_back, key_block, preferred_element_type=jnp.float32
            )
            key_part = jnp.einsum(
                "kgtj,tkgd->jkd", score_back, query_group, preferred_element_type=jnp.float32
            )
            return (acc_query, (key_part, value_part))

        return guarded(compute, carry)

    acc_query, (key_parts, value_parts) = lax.scan(
        grad_step, zero_mix, (key_blocks, value_blocks, seg_blocks, starts)
    )
    key_sums, value_sums = (
        lax.psum_scatter(
            key_parts.reshape(length, KV_HEADS * HEAD).astype(jnp.bfloat16),
            "ctx",
            scatter_dimension=0,
            tiled=True,
        ).astype(jnp.float32),
        lax.psum_scatter(
            value_parts.reshape(length, KV_HEADS * HEAD).astype(jnp.bfloat16),
            "ctx",
            scatter_dimension=0,
            tiled=True,
        ).astype(jnp.float32),
    )
    query_low = (
        rotate((acc_query * score_scale).reshape(row_count, HEADS, HEAD), cosine, -sine_table)
        .astype(jnp.bfloat16)
        .reshape(row_count, HEADS * HEAD)
    )
    key_low = (
        rotate((key_sums * score_scale).reshape(row_count, KV_HEADS, HEAD), cosine, -sine_table)
        .astype(jnp.bfloat16)
        .reshape(row_count, KV_HEADS * HEAD)
    )
    value_low = value_sums.astype(jnp.bfloat16)
    query_full_grad = contract_rows(normed1, query_low)
    key_full_grad = contract_rows(normed1, key_low)
    value_full_grad = contract_rows(normed1, value_low)
    normed1_back = (
        contract_cols(query_low, attn_again[1])
        + contract_cols(key_low, attn_again[2])
        + contract_cols(value_low, attn_again[3])
    )
    input_norm, attn_gain_term = norm_back(
        inputs, scale_one, attn_again[0].astype(jnp.float32), normed1_back
    )
    attn_sums = (
        lax.psum_scatter(attn_gain_term, ("seq", "ctx"), scatter_dimension=0, tiled=True),
        lax.psum_scatter(query_full_grad, ("seq", "ctx"), scatter_dimension=0, tiled=True),
        lax.psum_scatter(key_full_grad, ("seq", "ctx"), scatter_dimension=0, tiled=True),
        lax.psum_scatter(value_full_grad, ("seq", "ctx"), scatter_dimension=0, tiled=True),
        lax.psum_scatter(out_full_grad, ("seq", "ctx"), scatter_dimension=0, tiled=True),
    )
    input_grad = residual_back + input_norm
    return (
        block_output[None],
        input_grad[None],
        attn_sums[0],
        attn_sums[1],
        attn_sums[2],
        attn_sums[3],
        attn_sums[4],
        mlp_sums[0],
        mlp_sums[1],
        mlp_sums[2],
        down_grad,
    )


SEQ_X = [(0, 1), (1, 0), (2, 3), (3, 2)]
SEQ_Y = [(0, 2), (2, 0), (1, 3), (3, 1)]


def gather_ctx(block):
    return lax.all_gather(block, "ctx", axis=0, tiled=True)


def reduce_ctx(partial):
    return lax.psum_scatter(partial, "ctx", scatter_dimension=0, tiled=True)


def exchange_ctx(pieces):
    return lax.all_to_all(pieces, "ctx", 0, 0, tiled=True)


def gather_seq_near(block):
    return lax.ppermute(block, "seq", SEQ_X), lax.ppermute(block, "seq", SEQ_Y)


def gather_seq_far(block, from_x, from_y):
    rows, width = block.shape
    half = rows // 2
    mine = lax.axis_index("seq")
    far_top = lax.ppermute(from_x[:half], "seq", SEQ_Y)
    far_low = lax.ppermute(from_y[half:], "seq", SEQ_X)
    whole = jnp.zeros((4 * rows, width), block.dtype)
    for piece, start in (
        (block, mine * rows),
        (from_x, (mine ^ 1) * rows),
        (from_y, (mine ^ 2) * rows),
        (far_top, (mine ^ 3) * rows),
        (far_low, (mine ^ 3) * rows + half),
    ):
        whole = lax.dynamic_update_slice_in_dim(whole, piece, start, 0)
    return whole


def gather_seq(block):
    return gather_seq_far(block, *gather_seq_near(block))


def seq_part(partials, other, low):
    rows = partials[0].shape[0] // 4
    half = rows // 2
    start = (lax.axis_index("seq") ^ other) * rows + (half if low else 0)
    return jnp.concatenate(
        [lax.dynamic_slice_in_dim(partial, start, half, 0) for partial in partials], axis=1
    )


def reduce_seq_near(partials):
    return (
        lax.ppermute(seq_part(partials, 3, False), "seq", SEQ_X),
        lax.ppermute(seq_part(partials, 3, True), "seq", SEQ_Y),
        lax.ppermute(seq_part(partials, 1, False), "seq", SEQ_X),
        lax.ppermute(seq_part(partials, 2, True), "seq", SEQ_Y),
    )


def add_wide(*terms):
    total = terms[0].astype(jnp.float32)
    for term in terms[1:]:
        total = total + term.astype(jnp.float32)
    return total


def reduce_seq_far(partials, top_far, low_far, top_near, low_near):
    top_send = add_wide(seq_part(partials, 2, False), top_far).astype(jnp.bfloat16)
    low_send = add_wide(seq_part(partials, 1, True), low_far).astype(jnp.bfloat16)
    top_last = lax.ppermute(top_send, "seq", SEQ_Y)
    low_last = lax.ppermute(low_send, "seq", SEQ_X)
    return jnp.concatenate(
        [
            add_wide(seq_part(partials, 0, False), top_near, top_last),
            add_wide(seq_part(partials, 0, True), low_near, low_last),
        ],
        axis=0,
    ).astype(jnp.bfloat16)


def reduce_seq(partials):
    return reduce_seq_far(partials, *reduce_seq_near(partials))


def tie(*values):
    return lax.optimization_barrier(values)


def ff_split(width):
    main = width // 8 // 128 * 128
    return main, width // 8 - main


def ff_slices(weight):
    rows, width = weight.shape
    main, tail = ff_split(width)
    return (
        jnp.transpose(weight[:, : 8 * main].reshape(rows, 8, main), (1, 0, 2)),
        jnp.transpose(weight[:, 8 * main :].reshape(rows, 8, tail), (1, 0, 2)),
    )


def ff_rows(main, tail):
    count, rows, width = main.shape
    return jnp.concatenate(
        [
            jnp.transpose(main, (1, 0, 2)).reshape(rows, count * width),
            jnp.transpose(tail, (1, 0, 2)).reshape(rows, count * tail.shape[2]),
        ],
        axis=1,
    )


def head_slices(weight):
    rows = weight.shape[0]
    split = weight.reshape(rows, KV_HEADS, 8, HEAD)
    return jnp.transpose(split, (2, 0, 1, 3)).reshape(8, rows, KV_HEADS * HEAD)


def from_head_slices(pieces):
    rows = pieces.shape[1]
    split = pieces.reshape(8, rows, KV_HEADS, HEAD)
    return jnp.transpose(split, (1, 2, 0, 3)).reshape(rows, HEADS * HEAD)


def attend_mask(edge, first_row, block, span):
    row = first_row + lax.broadcasted_iota(jnp.int32, (block, span), 0)
    column = lax.broadcasted_iota(jnp.int32, (block, span), 1)
    return (column <= row) & (column >= jnp.where(row >= edge, edge, 0))


def soft_rows(query, key, allowed):
    scores = lax.dot_general(
        query, key, (((1,), (1,)), ((), ())), preferred_element_type=jnp.float32
    )
    scores = jnp.where(allowed, scores, MASKED)
    exponents = jnp.exp(scores - jnp.max(scores, axis=-1, keepdims=True))
    return exponents * (1.0 / jnp.sum(exponents, axis=-1, keepdims=True))


def attend_kernel(edge_ref, query_ref, key_ref, value_ref, mix_ref, *, block, blocks):
    step = pl.program_id(1)
    for index in range(blocks):

        @pl.when(step == index)
        def _(index=index):
            span = (index + 1) * block
            allowed = attend_mask(edge_ref[0], index * block, block, span)
            mixed = []
            for head in range(2):
                cut = slice(head * HEAD, (head + 1) * HEAD)
                soft = soft_rows(query_ref[:, cut], key_ref[:span, cut], allowed)
                mixed.append(
                    jnp.dot(
                        soft.astype(jnp.bfloat16),
                        value_ref[:span, cut],
                        preferred_element_type=jnp.float32,
                    )
                )
            mix_ref[...] = jnp.concatenate(mixed, axis=-1).astype(mix_ref.dtype)


def attend_back_kernel(
    edge_ref,
    query_ref,
    key_ref,
    value_ref,
    back_ref,
    query_back_ref,
    key_back_ref,
    value_back_ref,
    *,
    block,
    blocks,
    score_scale,
):
    step = pl.program_id(1)

    @pl.when(step == 0)
    def _():
        key_back_ref[...] = jnp.zeros_like(key_back_ref)
        value_back_ref[...] = jnp.zeros_like(value_back_ref)

    for index in range(blocks):

        @pl.when(step == index)
        def _(index=index):
            span = (index + 1) * block
            allowed = attend_mask(edge_ref[0], index * block, block, span)
            query_parts, key_parts, value_parts = [], [], []
            for head in range(2):
                cut = slice(head * HEAD, (head + 1) * HEAD)
                query, key = query_ref[:, cut], key_ref[:span, cut]
                back = back_ref[:, cut]
                soft = soft_rows(query, key, allowed)
                soft_back = contract_cols(back, value_ref[:span, cut])
                delta = jnp.sum(soft * soft_back, axis=-1, keepdims=True)
                score_back = (soft * (soft_back - delta)).astype(jnp.bfloat16)
                query_parts.append(
                    jnp.dot(score_back, key, preferred_element_type=jnp.float32) * score_scale
                )
                key_parts.append(contract_rows(score_back, query))
                value_parts.append(contract_rows(soft.astype(jnp.bfloat16), back))
            query_back_ref[...] = jnp.concatenate(query_parts, axis=-1)
            key_back_ref[:span, :] += jnp.concatenate(key_parts, axis=-1)
            value_back_ref[:span, :] += jnp.concatenate(value_parts, axis=-1)


def attend_specs(length, block):
    rows = pl.BlockSpec((block, 2 * HEAD), lambda pair, step: (step, pair))
    whole = pl.BlockSpec((length, 2 * HEAD), lambda pair, step: (0, pair))
    edge = pl.BlockSpec(memory_space=pltpu.SMEM)
    return edge, rows, whole


def attend(edge, queries, keys, values):
    length, width = queries.shape
    block = 256
    blocks = length // block
    scalar, rows, whole = attend_specs(length, block)

    def body(*refs):
        attend_kernel(*refs, block=block, blocks=blocks)

    return pl.pallas_call(
        body,
        name="attend",
        grid=(width // (2 * HEAD), blocks),
        in_specs=[scalar, rows, whole, whole],
        out_specs=rows,
        out_shape=jax.ShapeDtypeStruct((length, width), jnp.bfloat16),
    )(edge, queries, keys, values)


def attend_back(edge, queries, keys, values, back, score_scale):
    length, width = queries.shape
    block = 256
    blocks = length // block
    scalar, rows, whole = attend_specs(length, block)

    def body(*refs):
        attend_back_kernel(*refs, block=block, blocks=blocks, score_scale=score_scale)

    shape = jax.ShapeDtypeStruct((length, width), jnp.float32)
    return pl.pallas_call(
        body,
        name="attend_back",
        grid=(width // (2 * HEAD), blocks),
        in_specs=[scalar, rows, whole, whole, rows],
        out_specs=(rows, whole, whole),
        out_shape=(shape, shape, shape),
    )(edge, queries, keys, values, back)


def turn(values, cosine, sine_table):
    half = HEAD // 2
    lane = lax.broadcasted_iota(jnp.int32, values.shape, 1) % HEAD
    turned = jnp.where(
        lane < half, -jnp.roll(values, -half, axis=1), jnp.roll(values, half, axis=1)
    )
    return values * cosine + turned * sine_table


def local_columns(
    block_input,
    positions,
    segments,
    cotangent,
    attn_gain,
    query_weight,
    key_weight,
    value_weight,
    out_weight,
    mlp_gain,
    gate_weight,
    up_weight,
    down_weight,
):
    f32, bf16 = jnp.float32, jnp.bfloat16
    score_scale = HEAD ** (-0.5)
    length = segments.shape[1]
    rows = query_weight.shape[0]
    head_width = KV_HEADS * HEAD
    inputs = block_input[0].astype(f32)
    out_back = cotangent[0]
    gain_one = attn_gain.astype(f32)[:, None]
    gain_two = mlp_gain.astype(f32)[:, None]

    def fold(weight, gain):
        return (weight.astype(f32) * gain).astype(bf16)

    inputs_all = gather_ctx(block_input[0])
    back_all = gather_ctx(out_back)
    key_value = jnp.concatenate([fold(key_weight, gain_one), fold(value_weight, gain_one)], axis=1)
    attn_pieces = jnp.concatenate(
        [
            head_slices(fold(query_weight, gain_one)),
            jnp.broadcast_to(key_value[None], (8,) + key_value.shape),
        ],
        axis=2,
    )
    main, tail = ff_split(gate_weight.shape[1])
    both = 2 * (main + tail)
    gate_main, gate_tail = ff_slices(fold(gate_weight, gain_two))
    up_main, up_tail = ff_slices(fold(up_weight, gain_two))
    mlp_pieces = jnp.concatenate(
        [gate_main, up_main, gate_tail, up_tail, *ff_slices(down_weight)], axis=2
    )
    attn_own = exchange_ctx(attn_pieces).reshape(8 * rows, 3 * head_width)
    attn_own, mlp_pieces = tie(attn_own, mlp_pieces)
    attn_cols = gather_seq(attn_own)
    out_rows = gather_seq(out_weight)
    mlp_own = exchange_ctx(mlp_pieces).reshape(8 * rows, -1)

    edge = jnp.sum((segments[0] == 0).astype(jnp.int32))
    token = jnp.arange(length, dtype=jnp.int32)
    position = jnp.where(token < edge, token + (length - edge), token - edge)
    cosine, sine_table = rope_tables(position, HEAD)
    cosine = jnp.tile(cosine, (1, KV_HEADS))
    sine_table = jnp.tile(sine_table, (1, KV_HEADS))
    edge = edge[None]

    wide = inputs_all.astype(f32)
    shaped_all = (wide * rms_scale(wide)).astype(bf16)
    raw = jnp.dot(shaped_all, attn_cols, preferred_element_type=f32)
    queries = turn(raw[:, :head_width], cosine, sine_table).astype(bf16)
    keys = turn(raw[:, head_width : 2 * head_width], cosine, sine_table).astype(bf16)
    values = raw[:, 2 * head_width :].astype(bf16)
    queries = queries * jnp.asarray(score_scale, bf16)
    attn_low = attend(edge, queries, keys, values)
    attn_low, out_rows, mlp_own, back_all = tie(attn_low, out_rows, mlp_own, back_all)
    mixed = jnp.dot(attn_low, out_rows, preferred_element_type=f32).astype(bf16)
    mixed_own = reduce_ctx(mixed)
    mlp_near = gather_seq_near(mlp_own)
    mixed_own, *mlp_near = tie(mixed_own, *mlp_near)
    residual = inputs + mixed_own.astype(f32)
    scale_two = rms_scale(residual)
    shaped_two = residual * scale_two
    normed_all = gather_ctx(shaped_two.astype(bf16))
    mlp_cols = gather_seq_far(mlp_own, *mlp_near)
    gate_up, down_cols = mlp_cols[:, :both], mlp_cols[:, both:]
    hidden_back = jnp.dot(back_all, down_cols, preferred_element_type=f32)
    normed_all, hidden_back = tie(normed_all, hidden_back)
    proj = jnp.dot(normed_all, gate_up, preferred_element_type=f32)

    def halves(left_tail, right_tail, left, right):
        return jnp.concatenate([left, left_tail], axis=1), jnp.concatenate([right, right_tail], axis=1)

    gate_proj, up_proj = halves(
        proj[:, 2 * main : 2 * main + tail],
        proj[:, 2 * main + tail :],
        proj[:, :main],
        proj[:, main : 2 * main],
    )
    sigmoid_gate = jax.nn.sigmoid(gate_proj)
    silu_gate = gate_proj * sigmoid_gate
    hidden = (silu_gate * up_proj).astype(bf16)
    gate_back = (
        hidden_back * up_proj * sigmoid_gate * (1.0 + gate_proj * (1.0 - sigmoid_gate))
    ).astype(bf16)
    upper_back = (hidden_back * silu_gate).astype(bf16)
    gate_up_back = jnp.concatenate(
        [gate_back[:, :main], upper_back[:, :main], gate_back[:, main:], upper_back[:, main:]],
        axis=1,
    )
    weighted = reduce_ctx(contract_cols(gate_up_back, gate_up).astype(bf16))
    gate_up_grad = contract_rows(normed_all, gate_up_back).astype(bf16)
    down_grad = contract_rows(back_all, hidden).astype(bf16)
    mixed_out = contract_cols(hidden, down_cols).astype(bf16)
    weighted, gate_up_grad, down_grad, mixed_out = tie(weighted, gate_up_grad, down_grad, mixed_out)
    mlp_grads = [gate_up_grad, down_grad]
    weighted = weighted.astype(f32)
    residual_back = out_back.astype(f32) + scale_two * (
        weighted - shaped_two * jnp.mean(weighted * shaped_two, axis=-1, keepdims=True)
    )
    low_all = gather_ctx(residual_back.astype(bf16))
    mlp_grads_near = reduce_seq_near(mlp_grads)
    low_all, mixed_out, *mlp_grads_near = tie(low_all, mixed_out, *mlp_grads_near)
    out_own = reduce_ctx(mixed_out)
    mlp_grads_own = reduce_seq_far(mlp_grads, *mlp_grads_near)
    attn_back = contract_cols(low_all, out_rows).astype(bf16)
    query_back, key_back, value_back = attend_back(
        edge, queries, keys, values, attn_back, score_scale
    )
    out_grad = reduce_seq([contract_rows(attn_low, low_all).astype(bf16)]).astype(f32)
    query_back, mlp_grads_own, out_own = tie(query_back, mlp_grads_own, out_own)
    heads_back = jnp.concatenate(
        [
            turn(query_back, cosine, -sine_table).astype(bf16),
            turn(key_back, cosine, -sine_table).astype(bf16),
            value_back.astype(bf16),
        ],
        axis=1,
    )
    weighted_one = reduce_ctx(contract_cols(heads_back, attn_cols).astype(bf16)).astype(f32)
    scale_one = rms_scale(inputs)
    shaped_one = inputs * scale_one
    input_grad = residual_back + scale_one * (
        weighted_one - shaped_one * jnp.mean(weighted_one * shaped_one, axis=-1, keepdims=True)
    )
    block_output = (residual + out_own.astype(f32)).astype(bf16)

    mlp_grad = exchange_ctx(mlp_grads_own.reshape(8, rows, -1)).astype(f32)
    attn_grad_own = reduce_seq([contract_rows(shaped_all, heads_back).astype(bf16)])
    attn_grad = exchange_ctx(attn_grad_own.reshape(8, rows, -1)).astype(f32)
    gate_rows = ff_rows(mlp_grad[:, :, :main], mlp_grad[:, :, 2 * main : 2 * main + tail])
    up_rows = ff_rows(mlp_grad[:, :, main : 2 * main], mlp_grad[:, :, 2 * main + tail : both])
    down_grad = ff_rows(mlp_grad[:, :, both : both + main], mlp_grad[:, :, both + main :])
    query_rows = from_head_slices(attn_grad[:, :, :head_width])
    pair_rows = jnp.sum(attn_grad[:, :, head_width:], axis=0)
    key_rows, value_rows = pair_rows[:, :head_width], pair_rows[:, head_width:]

    def row_sum(weight, grad):
        return jnp.sum(weight.astype(f32) * grad, axis=1)

    attn_gain_grad = (
        row_sum(query_weight, query_rows)
        + row_sum(key_weight, key_rows)
        + row_sum(value_weight, value_rows)
    )
    mlp_gain_grad = row_sum(gate_weight, gate_rows) + row_sum(up_weight, up_rows)
    return (
        block_output[None],
        input_grad[None],
        attn_gain_grad,
        query_rows * gain_one,
        key_rows * gain_one,
        value_rows * gain_one,
        out_grad,
        mlp_gain_grad,
        gate_rows * gain_two,
        up_rows * gain_two,
        down_grad,
    )


def solution(mesh):
    placed = (
        P("seq", "ctx", None),
        P("seq", "ctx"),
        P("seq", None),
        P("seq", "ctx", None),
        P(("seq", "ctx")),
        P(("seq", "ctx"), None),
        P(("seq", "ctx"), None),
        P(("seq", "ctx"), None),
        P(("seq", "ctx"), None),
        P(("seq", "ctx")),
        P(("seq", "ctx"), None),
        P(("seq", "ctx"), None),
        P(("seq", "ctx"), None),
    )
    seq_count, ctx_count = mesh.shape["seq"], mesh.shape["ctx"]

    def run(*args):
        width = args[0].shape[2]
        fits = (
            seq_count == KV_HEADS == 4
            and ctx_count == HEADS // KV_HEADS == 8
            and width == seq_count * ctx_count * HEAD
        )
        return jax.shard_map(
            local_columns if fits else local_rows,
            mesh=mesh,
            in_specs=placed,
            out_specs=(
                P("seq", "ctx", None),
                P("seq", "ctx", None),
                P(("seq", "ctx")),
                P(("seq", "ctx"), None),
                P(("seq", "ctx"), None),
                P(("seq", "ctx"), None),
                P(("seq", "ctx"), None),
                P(("seq", "ctx")),
                P(("seq", "ctx"), None),
                P(("seq", "ctx"), None),
                P(("seq", "ctx"), None),
            ),
            check_vma=False,
        )(*args)

    return run
```

```python
import jax
import jax.numpy as jnp
from jax import lax
from jax.experimental import pallas as pl
from jax.experimental.pallas import tpu as pltpu
from jax.sharding import PartitionSpec as P

HEADS = 32
KV_HEADS = 4
HEAD = 64


EPSILON = 1e-05
MASKED = -1e30


def rope_tables(position, head_size):
    half_size = head_size // 2
    inverse = 1.0 / 10000.0 ** (jnp.arange(half_size, dtype=jnp.float32) * 2.0 / head_size)
    angles = position.astype(jnp.float32)[:, None] * inverse[None, :]
    cosine = jnp.cos(angles)
    sine_table = jnp.sin(angles)
    return (jnp.concatenate([cosine, cosine], -1), jnp.concatenate([sine_table, sine_table], -1))


def rotate(values, cosine, sine_table):
    half_size = values.shape[-1] // 2
    turned = jnp.concatenate([-values[..., half_size:], values[..., :half_size]], -1)
    return values * cosine[:, None, :] + turned * sine_table[:, None, :]


def rms_scale(inputs):
    return lax.rsqrt(jnp.mean(inputs * inputs, axis=-1, keepdims=True) + EPSILON)


def norm_back(inputs, row_scale, gain, upstream):
    shaped = inputs * row_scale
    weighted = upstream * gain
    gain_term = jnp.sum(upstream * shaped, axis=0)
    return (
        row_scale * (weighted - shaped * jnp.mean(weighted * shaped, axis=-1, keepdims=True)),
        gain_term,
    )


def contract_rows(left, right):
    return lax.dot_general(
        left, right, (((0,), (0,)), ((), ())), preferred_element_type=jnp.float32
    )


def contract_cols(left, right):
    return lax.dot_general(
        left, right, (((1,), (1,)), ((), ())), preferred_element_type=jnp.float32
    )


def local_rows(
    block_input,
    positions,
    segments,
    cotangent,
    attn_gain,
    query_weight,
    key_weight,
    value_weight,
    out_weight,
    mlp_gain,
    gate_weight,
    up_weight,
    down_weight,
):
    row_count = block_input.shape[1]
    group_size = HEADS // KV_HEADS
    score_scale = HEAD ** (-0.5)
    inputs = block_input[0].astype(jnp.float32)
    seg_all = segments[0]
    length = seg_all.shape[0]
    block_size = min(512, length)
    block_count = length // block_size
    first_row = lax.axis_index("ctx") * row_count
    query_index = first_row + jnp.arange(row_count, dtype=jnp.int32)
    seg_rows = lax.dynamic_slice_in_dim(seg_all, first_row, row_count)
    cosine, sine_table = rope_tables(positions[0], HEAD)
    starts = jnp.arange(block_count, dtype=jnp.int32) * block_size
    seg_blocks = seg_all.reshape(block_count, block_size)

    def key_mask(seg_block, block_start):
        key_index = block_start + jnp.arange(block_size, dtype=jnp.int32)
        return (seg_rows[:, None] == seg_block[None, :]) & (
            key_index[None, :] <= query_index[:, None]
        )

    def guarded(compute, running):
        result = compute(running)
        return result

    attn_params = (
        lax.all_gather(attn_gain, ("seq", "ctx"), axis=0, tiled=True),
        lax.all_gather(query_weight, ("seq", "ctx"), axis=0, tiled=True),
        lax.all_gather(key_weight, ("seq", "ctx"), axis=0, tiled=True),
        lax.all_gather(value_weight, ("seq", "ctx"), axis=0, tiled=True),
        lax.all_gather(out_weight, ("seq", "ctx"), axis=0, tiled=True),
    )
    gain_one = attn_params[0].astype(jnp.float32)
    scale_one = rms_scale(inputs)
    normed1 = (inputs * scale_one * gain_one).astype(jnp.bfloat16)
    query_raw = jnp.dot(normed1, attn_params[1], preferred_element_type=jnp.float32)
    key_raw = jnp.dot(normed1, attn_params[2], preferred_element_type=jnp.float32)
    value_raw = jnp.dot(normed1, attn_params[3], preferred_element_type=jnp.float32)
    queries = rotate(query_raw.reshape(row_count, HEADS, HEAD), cosine, sine_table).astype(
        jnp.bfloat16
    )
    keys_local = (
        rotate(key_raw.reshape(row_count, KV_HEADS, HEAD), cosine, sine_table)
        .astype(jnp.bfloat16)
        .reshape(row_count, KV_HEADS * HEAD)
    )
    values_local = value_raw.astype(jnp.bfloat16)
    keys_all, values_all = (
        lax.all_gather(keys_local, "ctx", axis=0, tiled=True),
        lax.all_gather(values_local, "ctx", axis=0, tiled=True),
    )
    key_blocks = keys_all.reshape(block_count, block_size, KV_HEADS, HEAD)
    value_blocks = values_all.reshape(block_count, block_size, KV_HEADS, HEAD)
    query_group = queries.reshape(row_count, KV_HEADS, group_size, HEAD)

    def block_scores(key_block, allowed):
        scores = (
            jnp.einsum("tkgd,jkd->kgtj", query_group, key_block, preferred_element_type=jnp.float32)
            * score_scale
        )
        return jnp.where(allowed[None, None], scores, MASKED)

    def max_step(carry, pieces):
        key_block, seg_block, block_start = pieces
        allowed = key_mask(seg_block, block_start)

        def compute(running):
            run_max, run_sum = running
            scores = block_scores(key_block, allowed)
            new_max = jnp.maximum(run_max, jnp.max(scores, axis=-1))
            exponents = jnp.where(allowed[None, None], jnp.exp(scores - new_max[..., None]), 0.0)
            return (new_max, run_sum * jnp.exp(run_max - new_max) + jnp.sum(exponents, axis=-1))

        return (guarded(compute, carry), None)

    start_max = jnp.full((KV_HEADS, group_size, row_count), MASKED, jnp.float32)
    start_sum = jnp.zeros((KV_HEADS, group_size, row_count), jnp.float32)
    (run_max, run_sum), unused = lax.scan(
        max_step, (start_max, start_sum), (key_blocks, seg_blocks, starts)
    )
    log_sum = run_max + jnp.log(run_sum)

    def block_soft(key_block, allowed):
        scores = block_scores(key_block, allowed)
        return jnp.where(allowed[None, None], jnp.exp(scores - log_sum[..., None]), 0.0)

    def value_step(carry, pieces):
        key_block, value_block, seg_block, block_start = pieces
        allowed = key_mask(seg_block, block_start)

        def compute(running):
            acc_out, acc_fix = running
            soft_weights = block_soft(key_block, allowed)
            rounded = soft_weights.astype(jnp.bfloat16)
            leftover = (soft_weights - rounded.astype(jnp.float32)).astype(jnp.bfloat16)
            acc_out = acc_out + jnp.einsum(
                "kgtj,jkd->tkgd", rounded, value_block, preferred_element_type=jnp.float32
            )
            acc_fix = acc_fix + jnp.einsum(
                "kgtj,jkd->tkgd", leftover, value_block, preferred_element_type=jnp.float32
            )
            return (acc_out, acc_fix)

        return (guarded(compute, carry), None)

    zero_mix = jnp.zeros((row_count, KV_HEADS, group_size, HEAD), jnp.float32)
    (acc_out, acc_fix), unused = lax.scan(
        value_step, (zero_mix, zero_mix), (key_blocks, value_blocks, seg_blocks, starts)
    )
    attn_low = acc_out.reshape(row_count, HEADS * HEAD).astype(jnp.bfloat16)
    full_mix = acc_out + acc_fix
    residual = inputs + jnp.dot(attn_low, attn_params[4], preferred_element_type=jnp.float32)
    mlp_params = (
        lax.all_gather(mlp_gain, ("seq", "ctx"), axis=0, tiled=True),
        lax.all_gather(gate_weight, ("seq", "ctx"), axis=0, tiled=True),
        lax.all_gather(up_weight, ("seq", "ctx"), axis=0, tiled=True),
        lax.all_gather(down_weight, ("seq", "ctx"), axis=0, tiled=True),
    )
    gain_two = mlp_params[0].astype(jnp.float32)
    scale_two = rms_scale(residual)
    normed2 = (residual * scale_two * gain_two).astype(jnp.bfloat16)
    gate_proj = jnp.dot(normed2, mlp_params[1], preferred_element_type=jnp.float32)
    up_proj = jnp.dot(normed2, mlp_params[2], preferred_element_type=jnp.float32)
    sigmoid_gate = jax.nn.sigmoid(gate_proj)
    silu_gate = gate_proj * sigmoid_gate
    hidden = (silu_gate * up_proj).astype(jnp.bfloat16)
    block_output = (residual + contract_cols(hidden, mlp_params[3])).astype(jnp.bfloat16)
    out_back = cotangent[0]
    out_float = out_back.astype(jnp.float32)
    mlp_again = (
        lax.all_gather(mlp_gain, ("seq", "ctx"), axis=0, tiled=True),
        lax.all_gather(gate_weight, ("seq", "ctx"), axis=0, tiled=True),
        lax.all_gather(up_weight, ("seq", "ctx"), axis=0, tiled=True),
        lax.all_gather(down_weight, ("seq", "ctx"), axis=0, tiled=True),
    )
    down_grad = lax.psum_scatter(
        contract_rows(out_back, hidden), ("seq", "ctx"), scatter_dimension=0, tiled=True
    )
    hidden_back = jnp.dot(out_back, mlp_again[3], preferred_element_type=jnp.float32)
    gate_back = (
        hidden_back * up_proj * sigmoid_gate * (1.0 + gate_proj * (1.0 - sigmoid_gate))
    ).astype(jnp.bfloat16)
    upper_back = (hidden_back * silu_gate).astype(jnp.bfloat16)
    gate_full_grad = contract_rows(normed2, gate_back)
    up_full_grad = contract_rows(normed2, upper_back)
    normed2_back = contract_cols(gate_back, mlp_again[1]) + contract_cols(upper_back, mlp_again[2])
    residual_norm, mlp_gain_term = norm_back(
        residual, scale_two, mlp_again[0].astype(jnp.float32), normed2_back
    )
    mlp_sums = (
        lax.psum_scatter(mlp_gain_term, ("seq", "ctx"), scatter_dimension=0, tiled=True),
        lax.psum_scatter(gate_full_grad, ("seq", "ctx"), scatter_dimension=0, tiled=True),
        lax.psum_scatter(up_full_grad, ("seq", "ctx"), scatter_dimension=0, tiled=True),
    )
    residual_back = out_float + residual_norm
    attn_again = (
        lax.all_gather(attn_gain, ("seq", "ctx"), axis=0, tiled=True),
        lax.all_gather(query_weight, ("seq", "ctx"), axis=0, tiled=True),
        lax.all_gather(key_weight, ("seq", "ctx"), axis=0, tiled=True),
        lax.all_gather(value_weight, ("seq", "ctx"), axis=0, tiled=True),
        lax.all_gather(out_weight, ("seq", "ctx"), axis=0, tiled=True),
    )
    residual_low = residual_back.astype(jnp.bfloat16)
    out_full_grad = contract_rows(attn_low, residual_low)
    attn_back = contract_cols(residual_low, attn_again[4]).astype(jnp.bfloat16)
    grad_mix = attn_back.reshape(row_count, KV_HEADS, group_size, HEAD)
    delta_rows = jnp.transpose(jnp.sum(grad_mix.astype(jnp.float32) * full_mix, axis=-1), (1, 2, 0))

    def grad_step(carry, pieces):
        key_block, value_block, seg_block, block_start = pieces
        allowed = key_mask(seg_block, block_start)

        def compute(acc_query):
            soft_weights = block_soft(key_block, allowed)
            rounded = soft_weights.astype(jnp.bfloat16)
            value_part = jnp.einsum(
                "kgtj,tkgd->jkd", rounded, grad_mix, preferred_element_type=jnp.float32
            )
            soft_back = jnp.einsum(
                "tkgd,jkd->kgtj", grad_mix, value_block, preferred_element_type=jnp.float32
            )
            score_back = (soft_weights * (soft_back - delta_rows[..., None])).astype(jnp.bfloat16)
            acc_query = acc_query + jnp.einsum(
                "kgtj,jkd->tkgd", score_back, key_block, preferred_element_type=jnp.float32
            )
            key_part = jnp.einsum(
                "kgtj,tkgd->jkd", score_back, query_group, preferred_element_type=jnp.float32
            )
            return (acc_query, (key_part, value_part))

        return guarded(compute, carry)

    acc_query, (key_parts, value_parts) = lax.scan(
        grad_step, zero_mix, (key_blocks, value_blocks, seg_blocks, starts)
    )
    key_sums, value_sums = (
        lax.psum_scatter(
            key_parts.reshape(length, KV_HEADS * HEAD).astype(jnp.bfloat16),
            "ctx",
            scatter_dimension=0,
            tiled=True,
        ).astype(jnp.float32),
        lax.psum_scatter(
            value_parts.reshape(length, KV_HEADS * HEAD).astype(jnp.bfloat16),
            "ctx",
            scatter_dimension=0,
            tiled=True,
        ).astype(jnp.float32),
    )
    query_low = (
        rotate((acc_query * score_scale).reshape(row_count, HEADS, HEAD), cosine, -sine_table)
        .astype(jnp.bfloat16)
        .reshape(row_count, HEADS * HEAD)
    )
    key_low = (
        rotate((key_sums * score_scale).reshape(row_count, KV_HEADS, HEAD), cosine, -sine_table)
        .astype(jnp.bfloat16)
        .reshape(row_count, KV_HEADS * HEAD)
    )
    value_low = value_sums.astype(jnp.bfloat16)
    query_full_grad = contract_rows(normed1, query_low)
    key_full_grad = contract_rows(normed1, key_low)
    value_full_grad = contract_rows(normed1, value_low)
    normed1_back = (
        contract_cols(query_low, attn_again[1])
        + contract_cols(key_low, attn_again[2])
        + contract_cols(value_low, attn_again[3])
    )
    input_norm, attn_gain_term = norm_back(
        inputs, scale_one, attn_again[0].astype(jnp.float32), normed1_back
    )
    attn_sums = (
        lax.psum_scatter(attn_gain_term, ("seq", "ctx"), scatter_dimension=0, tiled=True),
        lax.psum_scatter(query_full_grad, ("seq", "ctx"), scatter_dimension=0, tiled=True),
        lax.psum_scatter(key_full_grad, ("seq", "ctx"), scatter_dimension=0, tiled=True),
        lax.psum_scatter(value_full_grad, ("seq", "ctx"), scatter_dimension=0, tiled=True),
        lax.psum_scatter(out_full_grad, ("seq", "ctx"), scatter_dimension=0, tiled=True),
    )
    input_grad = residual_back + input_norm
    return (
        block_output[None],
        input_grad[None],
        attn_sums[0],
        attn_sums[1],
        attn_sums[2],
        attn_sums[3],
        attn_sums[4],
        mlp_sums[0],
        mlp_sums[1],
        mlp_sums[2],
        down_grad,
    )


SEQ_X = [(0, 1), (1, 0), (2, 3), (3, 2)]
SEQ_Y = [(0, 2), (2, 0), (1, 3), (3, 1)]


def gather_ctx(block):
    return lax.all_gather(block, "ctx", axis=0, tiled=True)


def reduce_ctx(partial):
    return lax.psum_scatter(partial, "ctx", scatter_dimension=0, tiled=True)


def exchange_ctx(pieces):
    return lax.all_to_all(pieces, "ctx", 0, 0, tiled=True)


def gather_seq_near(block):
    return lax.ppermute(block, "seq", SEQ_X), lax.ppermute(block, "seq", SEQ_Y)


def gather_seq_far(block, from_x, from_y):
    rows, width = block.shape
    half = rows // 2
    mine = lax.axis_index("seq")
    far_top = lax.ppermute(from_x[:half], "seq", SEQ_Y)
    far_low = lax.ppermute(from_y[half:], "seq", SEQ_X)
    whole = jnp.zeros((4 * rows, width), block.dtype)
    for piece, start in (
        (block, mine * rows),
        (from_x, (mine ^ 1) * rows),
        (from_y, (mine ^ 2) * rows),
        (far_top, (mine ^ 3) * rows),
        (far_low, (mine ^ 3) * rows + half),
    ):
        whole = lax.dynamic_update_slice_in_dim(whole, piece, start, 0)
    return whole


def gather_seq(block):
    return gather_seq_far(block, *gather_seq_near(block))


def seq_part(partials, other, low):
    rows = partials[0].shape[0] // 4
    half = rows // 2
    start = (lax.axis_index("seq") ^ other) * rows + (half if low else 0)
    return jnp.concatenate(
        [lax.dynamic_slice_in_dim(partial, start, half, 0) for partial in partials], axis=1
    )


def seq_parts(partials):
    return (
        seq_part(partials, 3, False),
        seq_part(partials, 3, True),
        seq_part(partials, 1, False),
        seq_part(partials, 2, True),
    )


def send_parts(parts):
    return tuple(
        lax.ppermute(part, "seq", axis) for part, axis in zip(parts, (SEQ_X, SEQ_Y) * 2)
    )


def reduce_seq_near(partials):
    return send_parts(seq_parts(partials))


def add_wide(*terms):
    total = terms[0].astype(jnp.float32)
    for term in terms[1:]:
        total = total + term.astype(jnp.float32)
    return total


def far_sums(partials, top_far, low_far):
    return (
        add_wide(seq_part(partials, 2, False), top_far).astype(jnp.bfloat16),
        add_wide(seq_part(partials, 1, True), low_far).astype(jnp.bfloat16),
    )


def reduce_seq_far(partials, sums, top_near, low_near):
    top_send, low_send = sums
    top_last = lax.ppermute(top_send, "seq", SEQ_Y)
    low_last = lax.ppermute(low_send, "seq", SEQ_X)
    return jnp.concatenate(
        [
            add_wide(seq_part(partials, 0, False), top_near, top_last),
            add_wide(seq_part(partials, 0, True), low_near, low_last),
        ],
        axis=0,
    ).astype(jnp.bfloat16)


def reduce_seq(partials):
    top_far, low_far, *nears = reduce_seq_near(partials)
    return reduce_seq_far(partials, far_sums(partials, top_far, low_far), *nears)


def tie(*values):
    return lax.optimization_barrier(values)


def swap_cores(block):
    return lax.ppermute(block, "ctx", [(device, device ^ 1) for device in range(8)])


def ff_split(width):
    main = width // 8 // 128 * 128
    return main, width // 8 - main


def ff_slices(weight):
    rows, width = weight.shape
    main, tail = ff_split(width)
    return (
        jnp.transpose(weight[:, : 8 * main].reshape(rows, 8, main), (1, 0, 2)),
        jnp.transpose(weight[:, 8 * main :].reshape(rows, 8, tail), (1, 0, 2)),
    )


def ff_rows(main, tail):
    count, rows, width = main.shape
    return jnp.concatenate(
        [
            jnp.transpose(main, (1, 0, 2)).reshape(rows, count * width),
            jnp.transpose(tail, (1, 0, 2)).reshape(rows, count * tail.shape[2]),
        ],
        axis=1,
    )


def head_slices(weight):
    rows = weight.shape[0]
    split = weight.reshape(rows, KV_HEADS, 8, HEAD)
    return jnp.transpose(split, (2, 0, 1, 3)).reshape(8, rows, KV_HEADS * HEAD)


def from_head_slices(pieces):
    rows = pieces.shape[1]
    split = pieces.reshape(8, rows, KV_HEADS, HEAD)
    return jnp.transpose(split, (1, 2, 0, 3)).reshape(rows, HEADS * HEAD)


def attend_mask(edge, first_row, block, span):
    row = first_row + lax.broadcasted_iota(jnp.int32, (block, span), 0)
    column = lax.broadcasted_iota(jnp.int32, (block, span), 1)
    return (column <= row) & (column >= jnp.where(row >= edge, edge, 0))


def soft_rows(query, key, allowed):
    scores = lax.dot_general(
        query, key, (((1,), (1,)), ((), ())), preferred_element_type=jnp.float32
    )
    scores = jnp.where(allowed, scores, MASKED)
    exponents = jnp.exp(scores - jnp.max(scores, axis=-1, keepdims=True))
    return exponents * (1.0 / jnp.sum(exponents, axis=-1, keepdims=True))


def attend_kernel(edge_ref, query_ref, key_ref, value_ref, mix_ref, *, block, blocks):
    step = pl.program_id(1)
    for index in range(blocks):

        @pl.when(step == index)
        def _(index=index):
            span = (index + 1) * block
            allowed = attend_mask(edge_ref[0], index * block, block, span)
            mixed = []
            for head in range(2):
                cut = slice(head * HEAD, (head + 1) * HEAD)
                soft = soft_rows(query_ref[:, cut], key_ref[:span, cut], allowed)
                mixed.append(
                    jnp.dot(
                        soft.astype(jnp.bfloat16),
                        value_ref[:span, cut],
                        preferred_element_type=jnp.float32,
                    )
                )
            mix_ref[...] = jnp.concatenate(mixed, axis=-1).astype(mix_ref.dtype)


def attend_back_kernel(
    edge_ref,
    query_ref,
    key_ref,
    value_ref,
    back_ref,
    query_back_ref,
    key_back_ref,
    value_back_ref,
    *,
    block,
    blocks,
    score_scale,
):
    step = pl.program_id(1)

    @pl.when(step == 0)
    def _():
        key_back_ref[...] = jnp.zeros_like(key_back_ref)
        value_back_ref[...] = jnp.zeros_like(value_back_ref)

    for index in range(blocks):

        @pl.when(step == index)
        def _(index=index):
            span = (index + 1) * block
            allowed = attend_mask(edge_ref[0], index * block, block, span)
            query_parts, key_parts, value_parts = [], [], []
            for head in range(2):
                cut = slice(head * HEAD, (head + 1) * HEAD)
                query, key = query_ref[:, cut], key_ref[:span, cut]
                back = back_ref[:, cut]
                soft = soft_rows(query, key, allowed)
                soft_back = contract_cols(back, value_ref[:span, cut])
                delta = jnp.sum(soft * soft_back, axis=-1, keepdims=True)
                score_back = (soft * (soft_back - delta)).astype(jnp.bfloat16)
                query_parts.append(
                    jnp.dot(score_back, key, preferred_element_type=jnp.float32) * score_scale
                )
                key_parts.append(contract_rows(score_back, query))
                value_parts.append(contract_rows(soft.astype(jnp.bfloat16), back))
            query_back_ref[...] = jnp.concatenate(query_parts, axis=-1)
            key_back_ref[:span, :] += jnp.concatenate(key_parts, axis=-1)
            value_back_ref[:span, :] += jnp.concatenate(value_parts, axis=-1)


def attend_specs(length, block):
    rows = pl.BlockSpec((block, 2 * HEAD), lambda pair, step: (step, pair))
    whole = pl.BlockSpec((length, 2 * HEAD), lambda pair, step: (0, pair))
    edge = pl.BlockSpec(memory_space=pltpu.SMEM)
    return edge, rows, whole


def attend_cost(length, width, products):
    return pl.CostEstimate(
        flops=8 * products * length * length * width,
        transcendentals=length * length * width // HEAD,
        bytes_accessed=(2 * products + 4) * length * width,
    )


def attend(edge, queries, keys, values):
    length, width = queries.shape
    block = 256
    blocks = length // block
    scalar, rows, whole = attend_specs(length, block)

    def body(*refs):
        attend_kernel(*refs, block=block, blocks=blocks)

    return pl.pallas_call(
        body,
        name="attend",
        grid=(width // (2 * HEAD), blocks),
        in_specs=[scalar, rows, whole, whole],
        out_specs=rows,
        out_shape=jax.ShapeDtypeStruct((length, width), jnp.bfloat16),
        cost_estimate=attend_cost(length, width, 2),
    )(edge, queries, keys, values)


def attend_back(edge, queries, keys, values, back, score_scale):
    length, width = queries.shape
    block = 256
    blocks = length // block
    scalar, rows, whole = attend_specs(length, block)

    def body(*refs):
        attend_back_kernel(*refs, block=block, blocks=blocks, score_scale=score_scale)

    shape = jax.ShapeDtypeStruct((length, width), jnp.float32)
    return pl.pallas_call(
        body,
        name="attend_back",
        grid=(width // (2 * HEAD), blocks),
        in_specs=[scalar, rows, whole, whole, rows],
        out_specs=(rows, whole, whole),
        out_shape=(shape, shape, shape),
        cost_estimate=attend_cost(length, width, 5),
    )(edge, queries, keys, values, back)


def turn(values, cosine, sine_table):
    half = HEAD // 2
    lane = lax.broadcasted_iota(jnp.int32, values.shape, 1) % HEAD
    turned = jnp.where(
        lane < half, -jnp.roll(values, -half, axis=1), jnp.roll(values, half, axis=1)
    )
    return values * cosine + turned * sine_table


def local_columns(
    block_input,
    positions,
    segments,
    cotangent,
    attn_gain,
    query_weight,
    key_weight,
    value_weight,
    out_weight,
    mlp_gain,
    gate_weight,
    up_weight,
    down_weight,
):
    f32, bf16 = jnp.float32, jnp.bfloat16
    score_scale = HEAD ** (-0.5)
    length = segments.shape[1]
    rows = query_weight.shape[0]
    head_width = KV_HEADS * HEAD
    inputs = block_input[0].astype(f32)
    out_back = cotangent[0]
    gain_one = attn_gain.astype(f32)[:, None]
    gain_two = mlp_gain.astype(f32)[:, None]

    def fold(weight, gain):
        return (weight.astype(f32) * gain).astype(bf16)

    inputs_all = gather_ctx(block_input[0])
    key_value = jnp.stack([fold(key_weight, gain_one), fold(value_weight, gain_one)])
    attn_pieces = jnp.concatenate(
        [
            head_slices(fold(query_weight, gain_one)),
            jnp.tile(key_value, (4, 1, 1)),
        ],
        axis=2,
    )
    main, tail = ff_split(gate_weight.shape[1])
    both = 2 * (main + tail)
    gate_main, gate_tail = ff_slices(fold(gate_weight, gain_two))
    up_main, up_tail = ff_slices(fold(up_weight, gain_two))
    mlp_pieces = jnp.concatenate(
        [gate_main, up_main, gate_tail, up_tail, *ff_slices(down_weight)], axis=2
    )
    attn_own = exchange_ctx(attn_pieces).reshape(8 * rows, 2 * head_width)
    attn_own, mlp_pieces = tie(attn_own, mlp_pieces)
    attn_cols = gather_seq(attn_own)
    core = lax.axis_index("ctx") % 2
    own_cols = attn_cols[:, head_width:]
    other_cols = swap_cores(own_cols)
    attn_cols = jnp.concatenate(
        [
            attn_cols[:, :head_width],
            jnp.where(core == 0, own_cols, other_cols),
            jnp.where(core == 0, other_cols, own_cols),
        ],
        axis=1,
    )
    out_rows = gather_seq(out_weight)
    mlp_own = exchange_ctx(mlp_pieces).reshape(8 * rows, -1)

    edge = jnp.sum((segments[0] == 0).astype(jnp.int32))
    token = jnp.arange(length, dtype=jnp.int32)
    position = jnp.where(token < edge, token + (length - edge), token - edge)
    cosine, sine_table = rope_tables(position, HEAD)
    cosine = jnp.tile(cosine, (1, KV_HEADS))
    sine_table = jnp.tile(sine_table, (1, KV_HEADS))
    edge = edge[None]

    wide = inputs_all.astype(f32)
    shaped_all = (wide * rms_scale(wide)).astype(bf16)
    raw = jnp.dot(shaped_all, attn_cols, preferred_element_type=f32)
    raw, mlp_own = tie(raw, mlp_own)
    mlp_near = gather_seq_near(mlp_own)
    queries = turn(raw[:, :head_width], cosine, sine_table).astype(bf16)
    keys = turn(raw[:, head_width : 2 * head_width], cosine, sine_table).astype(bf16)
    values = raw[:, 2 * head_width :].astype(bf16)
    queries = queries * jnp.asarray(score_scale, bf16)
    attn_low = attend(edge, queries, keys, values)
    attn_low, out_rows, back_late = tie(attn_low, out_rows, out_back)
    mixed = jnp.dot(attn_low, out_rows, preferred_element_type=f32).astype(bf16)
    mixed_own = reduce_ctx(mixed)
    mixed_own, *mlp_near = tie(mixed_own, *mlp_near)
    residual = inputs + mixed_own.astype(f32)
    scale_two = rms_scale(residual)
    shaped_two = residual * scale_two
    shaped_low = shaped_two.astype(bf16)
    normed_all = gather_ctx(shaped_low)
    shaped_two, back_late = tie(shaped_two, back_late)
    mlp_cols = gather_seq_far(mlp_own, *mlp_near)
    back_all = gather_ctx(back_late)
    gate_up, down_cols = mlp_cols[:, :both], mlp_cols[:, both:]
    proj = jnp.dot(normed_all, gate_up, preferred_element_type=f32)

    def halves(left_tail, right_tail, left, right):
        return jnp.concatenate([left, left_tail], axis=1), jnp.concatenate([right, right_tail], axis=1)

    gate_proj, up_proj = halves(
        proj[:, 2 * main : 2 * main + tail],
        proj[:, 2 * main + tail :],
        proj[:, :main],
        proj[:, main : 2 * main],
    )
    sigmoid_gate = jax.nn.sigmoid(gate_proj)
    silu_gate = gate_proj * sigmoid_gate
    hidden = (silu_gate * up_proj).astype(bf16)
    mixed_out = contract_cols(hidden, down_cols).astype(bf16)
    mixed_out, back_all = tie(mixed_out, back_all)
    out_own = reduce_ctx(mixed_out)
    hidden_back = jnp.dot(back_all, down_cols, preferred_element_type=f32)
    gate_back = (
        hidden_back * up_proj * sigmoid_gate * (1.0 + gate_proj * (1.0 - sigmoid_gate))
    ).astype(bf16)
    upper_back = (hidden_back * silu_gate).astype(bf16)
    gate_up_back = jnp.concatenate(
        [gate_back[:, :main], upper_back[:, :main], gate_back[:, main:], upper_back[:, main:]],
        axis=1,
    )
    weighted = reduce_ctx(contract_cols(gate_up_back, gate_up).astype(bf16))
    gate_up_back, hidden, out_own = tie(gate_up_back, hidden, out_own)
    gate_up_grad = contract_rows(normed_all, gate_up_back).astype(bf16)
    down_grad = contract_rows(back_all, hidden).astype(bf16)
    mlp_grads = [gate_up_grad, down_grad]
    mlp_parts = seq_parts(mlp_grads)
    mlp_first = send_parts(mlp_parts[:2])
    weighted, *mlp_first = tie(weighted, *mlp_first)
    weighted = weighted.astype(f32)
    residual_back = out_back.astype(f32) + scale_two * (
        weighted - shaped_two * jnp.mean(weighted * shaped_two, axis=-1, keepdims=True)
    )
    residual_low = residual_back.astype(bf16)
    low_all = gather_ctx(residual_low)
    residual_back, *mlp_first = tie(residual_back, *mlp_first)
    mlp_near = send_parts(mlp_parts[2:])
    mlp_sums = far_sums(mlp_grads, *mlp_first)
    mlp_grads_own = reduce_seq_far(mlp_grads, mlp_sums, *mlp_near)
    low_all, mlp_grads_own = tie(low_all, mlp_grads_own)
    mlp_grad = exchange_ctx(mlp_grads_own.reshape(8, rows, -1))
    attn_back = contract_cols(low_all, out_rows).astype(bf16)
    query_back, key_back, value_back = attend_back(
        edge, queries, keys, values, attn_back, score_scale
    )
    heads_back = jnp.concatenate(
        [
            turn(query_back, cosine, -sine_table).astype(bf16),
            turn(key_back, cosine, -sine_table).astype(bf16),
            value_back.astype(bf16),
        ],
        axis=1,
    )
    weighted_part = contract_cols(heads_back, attn_cols).astype(bf16)
    weighted_part, mlp_grad, heads_back, low_all = tie(weighted_part, mlp_grad, heads_back, low_all)
    weighted_one = reduce_ctx(weighted_part).astype(f32)
    attn_full_grad = contract_rows(shaped_all, heads_back)
    key_part = attn_full_grad[:, head_width : 2 * head_width]
    value_part = attn_full_grad[:, 2 * head_width :]
    other_part = swap_cores(jnp.where(core == 0, value_part, key_part).astype(bf16))
    own_part = jnp.where(core == 0, key_part, value_part) + other_part.astype(f32)
    attn_grad_own = reduce_seq(
        [jnp.concatenate([attn_full_grad[:, :head_width].astype(bf16), own_part.astype(bf16)], axis=1)]
    )
    out_grad = reduce_seq([contract_rows(attn_low, low_all).astype(bf16)]).astype(f32)
    mlp_grad = mlp_grad.astype(f32)
    attn_grad = exchange_ctx(attn_grad_own.reshape(8, rows, -1)).astype(f32)

    scale_one = rms_scale(inputs)
    shaped_one = inputs * scale_one
    input_grad = residual_back + scale_one * (
        weighted_one - shaped_one * jnp.mean(weighted_one * shaped_one, axis=-1, keepdims=True)
    )
    block_output = (residual + out_own.astype(f32)).astype(bf16)
    gate_rows = ff_rows(mlp_grad[:, :, :main], mlp_grad[:, :, 2 * main : 2 * main + tail])
    up_rows = ff_rows(mlp_grad[:, :, main : 2 * main], mlp_grad[:, :, 2 * main + tail : both])
    down_grad = ff_rows(mlp_grad[:, :, both : both + main], mlp_grad[:, :, both + main :])
    query_rows = from_head_slices(attn_grad[:, :, :head_width])
    pair_rows = jnp.sum(attn_grad[:, :, head_width:].reshape(4, 2, rows, head_width), axis=0)
    key_rows, value_rows = pair_rows[0], pair_rows[1]

    def row_sum(weight, grad):
        return jnp.sum(weight.astype(f32) * grad, axis=1)

    attn_gain_grad = (
        row_sum(query_weight, query_rows)
        + row_sum(key_weight, key_rows)
        + row_sum(value_weight, value_rows)
    )
    mlp_gain_grad = row_sum(gate_weight, gate_rows) + row_sum(up_weight, up_rows)
    return (
        block_output[None],
        input_grad[None],
        attn_gain_grad,
        query_rows * gain_one,
        key_rows * gain_one,
        value_rows * gain_one,
        out_grad,
        mlp_gain_grad,
        gate_rows * gain_two,
        up_rows * gain_two,
        down_grad,
    )


def solution(mesh):
    placed = (
        P("seq", "ctx", None),
        P("seq", "ctx"),
        P("seq", None),
        P("seq", "ctx", None),
        P(("seq", "ctx")),
        P(("seq", "ctx"), None),
        P(("seq", "ctx"), None),
        P(("seq", "ctx"), None),
        P(("seq", "ctx"), None),
        P(("seq", "ctx")),
        P(("seq", "ctx"), None),
        P(("seq", "ctx"), None),
        P(("seq", "ctx"), None),
    )
    seq_count, ctx_count = mesh.shape["seq"], mesh.shape["ctx"]

    def run(*args):
        width = args[0].shape[2]
        fits = (
            seq_count == KV_HEADS == 4
            and ctx_count == HEADS // KV_HEADS == 8
            and width == seq_count * ctx_count * HEAD
        )
        return jax.shard_map(
            local_columns if fits else local_rows,
            mesh=mesh,
            in_specs=placed,
            out_specs=(
                P("seq", "ctx", None),
                P("seq", "ctx", None),
                P(("seq", "ctx")),
                P(("seq", "ctx"), None),
                P(("seq", "ctx"), None),
                P(("seq", "ctx"), None),
                P(("seq", "ctx"), None),
                P(("seq", "ctx")),
                P(("seq", "ctx"), None),
                P(("seq", "ctx"), None),
                P(("seq", "ctx"), None),
            ),
            check_vma=False,
        )(*args)

    return run
```

```python
import jax
import jax.numpy as jnp
from jax import lax
from jax.experimental import pallas as pl
from jax.experimental.pallas import tpu as pltpu
from jax.sharding import PartitionSpec as P

HEADS = 32
KV_HEADS = 4
HEAD = 64


EPSILON = 1e-05
MASKED = -1e30


def rope_tables(position, head_size):
    half_size = head_size // 2
    inverse = 1.0 / 10000.0 ** (jnp.arange(half_size, dtype=jnp.float32) * 2.0 / head_size)
    angles = position.astype(jnp.float32)[:, None] * inverse[None, :]
    cosine = jnp.cos(angles)
    sine_table = jnp.sin(angles)
    return (jnp.concatenate([cosine, cosine], -1), jnp.concatenate([sine_table, sine_table], -1))


def rotate(values, cosine, sine_table):
    half_size = values.shape[-1] // 2
    turned = jnp.concatenate([-values[..., half_size:], values[..., :half_size]], -1)
    return values * cosine[:, None, :] + turned * sine_table[:, None, :]


def rms_scale(inputs):
    return lax.rsqrt(jnp.mean(inputs * inputs, axis=-1, keepdims=True) + EPSILON)


def norm_back(inputs, row_scale, gain, upstream):
    shaped = inputs * row_scale
    weighted = upstream * gain
    gain_term = jnp.sum(upstream * shaped, axis=0)
    return (
        row_scale * (weighted - shaped * jnp.mean(weighted * shaped, axis=-1, keepdims=True)),
        gain_term,
    )


def contract_rows(left, right):
    return lax.dot_general(
        left, right, (((0,), (0,)), ((), ())), preferred_element_type=jnp.float32
    )


def contract_cols(left, right):
    return lax.dot_general(
        left, right, (((1,), (1,)), ((), ())), preferred_element_type=jnp.float32
    )


def local_rows(
    block_input,
    positions,
    segments,
    cotangent,
    attn_gain,
    query_weight,
    key_weight,
    value_weight,
    out_weight,
    mlp_gain,
    gate_weight,
    up_weight,
    down_weight,
):
    row_count = block_input.shape[1]
    group_size = HEADS // KV_HEADS
    score_scale = HEAD ** (-0.5)
    inputs = block_input[0].astype(jnp.float32)
    seg_all = segments[0]
    length = seg_all.shape[0]
    block_size = min(512, length)
    block_count = length // block_size
    first_row = lax.axis_index("ctx") * row_count
    query_index = first_row + jnp.arange(row_count, dtype=jnp.int32)
    seg_rows = lax.dynamic_slice_in_dim(seg_all, first_row, row_count)
    cosine, sine_table = rope_tables(positions[0], HEAD)
    starts = jnp.arange(block_count, dtype=jnp.int32) * block_size
    seg_blocks = seg_all.reshape(block_count, block_size)

    def key_mask(seg_block, block_start):
        key_index = block_start + jnp.arange(block_size, dtype=jnp.int32)
        return (seg_rows[:, None] == seg_block[None, :]) & (
            key_index[None, :] <= query_index[:, None]
        )

    def guarded(compute, running):
        result = compute(running)
        return result

    attn_params = (
        lax.all_gather(attn_gain, ("seq", "ctx"), axis=0, tiled=True),
        lax.all_gather(query_weight, ("seq", "ctx"), axis=0, tiled=True),
        lax.all_gather(key_weight, ("seq", "ctx"), axis=0, tiled=True),
        lax.all_gather(value_weight, ("seq", "ctx"), axis=0, tiled=True),
        lax.all_gather(out_weight, ("seq", "ctx"), axis=0, tiled=True),
    )
    gain_one = attn_params[0].astype(jnp.float32)
    scale_one = rms_scale(inputs)
    normed1 = (inputs * scale_one * gain_one).astype(jnp.bfloat16)
    query_raw = jnp.dot(normed1, attn_params[1], preferred_element_type=jnp.float32)
    key_raw = jnp.dot(normed1, attn_params[2], preferred_element_type=jnp.float32)
    value_raw = jnp.dot(normed1, attn_params[3], preferred_element_type=jnp.float32)
    queries = rotate(query_raw.reshape(row_count, HEADS, HEAD), cosine, sine_table).astype(
        jnp.bfloat16
    )
    keys_local = (
        rotate(key_raw.reshape(row_count, KV_HEADS, HEAD), cosine, sine_table)
        .astype(jnp.bfloat16)
        .reshape(row_count, KV_HEADS * HEAD)
    )
    values_local = value_raw.astype(jnp.bfloat16)
    keys_all, values_all = (
        lax.all_gather(keys_local, "ctx", axis=0, tiled=True),
        lax.all_gather(values_local, "ctx", axis=0, tiled=True),
    )
    key_blocks = keys_all.reshape(block_count, block_size, KV_HEADS, HEAD)
    value_blocks = values_all.reshape(block_count, block_size, KV_HEADS, HEAD)
    query_group = queries.reshape(row_count, KV_HEADS, group_size, HEAD)

    def block_scores(key_block, allowed):
        scores = (
            jnp.einsum("tkgd,jkd->kgtj", query_group, key_block, preferred_element_type=jnp.float32)
            * score_scale
        )
        return jnp.where(allowed[None, None], scores, MASKED)

    def max_step(carry, pieces):
        key_block, seg_block, block_start = pieces
        allowed = key_mask(seg_block, block_start)

        def compute(running):
            run_max, run_sum = running
            scores = block_scores(key_block, allowed)
            new_max = jnp.maximum(run_max, jnp.max(scores, axis=-1))
            exponents = jnp.where(allowed[None, None], jnp.exp(scores - new_max[..., None]), 0.0)
            return (new_max, run_sum * jnp.exp(run_max - new_max) + jnp.sum(exponents, axis=-1))

        return (guarded(compute, carry), None)

    start_max = jnp.full((KV_HEADS, group_size, row_count), MASKED, jnp.float32)
    start_sum = jnp.zeros((KV_HEADS, group_size, row_count), jnp.float32)
    (run_max, run_sum), unused = lax.scan(
        max_step, (start_max, start_sum), (key_blocks, seg_blocks, starts)
    )
    log_sum = run_max + jnp.log(run_sum)

    def block_soft(key_block, allowed):
        scores = block_scores(key_block, allowed)
        return jnp.where(allowed[None, None], jnp.exp(scores - log_sum[..., None]), 0.0)

    def value_step(carry, pieces):
        key_block, value_block, seg_block, block_start = pieces
        allowed = key_mask(seg_block, block_start)

        def compute(running):
            acc_out, acc_fix = running
            soft_weights = block_soft(key_block, allowed)
            rounded = soft_weights.astype(jnp.bfloat16)
            leftover = (soft_weights - rounded.astype(jnp.float32)).astype(jnp.bfloat16)
            acc_out = acc_out + jnp.einsum(
                "kgtj,jkd->tkgd", rounded, value_block, preferred_element_type=jnp.float32
            )
            acc_fix = acc_fix + jnp.einsum(
                "kgtj,jkd->tkgd", leftover, value_block, preferred_element_type=jnp.float32
            )
            return (acc_out, acc_fix)

        return (guarded(compute, carry), None)

    zero_mix = jnp.zeros((row_count, KV_HEADS, group_size, HEAD), jnp.float32)
    (acc_out, acc_fix), unused = lax.scan(
        value_step, (zero_mix, zero_mix), (key_blocks, value_blocks, seg_blocks, starts)
    )
    attn_low = acc_out.reshape(row_count, HEADS * HEAD).astype(jnp.bfloat16)
    full_mix = acc_out + acc_fix
    residual = inputs + jnp.dot(attn_low, attn_params[4], preferred_element_type=jnp.float32)
    mlp_params = (
        lax.all_gather(mlp_gain, ("seq", "ctx"), axis=0, tiled=True),
        lax.all_gather(gate_weight, ("seq", "ctx"), axis=0, tiled=True),
        lax.all_gather(up_weight, ("seq", "ctx"), axis=0, tiled=True),
        lax.all_gather(down_weight, ("seq", "ctx"), axis=0, tiled=True),
    )
    gain_two = mlp_params[0].astype(jnp.float32)
    scale_two = rms_scale(residual)
    normed2 = (residual * scale_two * gain_two).astype(jnp.bfloat16)
    gate_proj = jnp.dot(normed2, mlp_params[1], preferred_element_type=jnp.float32)
    up_proj = jnp.dot(normed2, mlp_params[2], preferred_element_type=jnp.float32)
    sigmoid_gate = jax.nn.sigmoid(gate_proj)
    silu_gate = gate_proj * sigmoid_gate
    hidden = (silu_gate * up_proj).astype(jnp.bfloat16)
    block_output = (residual + contract_cols(hidden, mlp_params[3])).astype(jnp.bfloat16)
    out_back = cotangent[0]
    out_float = out_back.astype(jnp.float32)
    mlp_again = (
        lax.all_gather(mlp_gain, ("seq", "ctx"), axis=0, tiled=True),
        lax.all_gather(gate_weight, ("seq", "ctx"), axis=0, tiled=True),
        lax.all_gather(up_weight, ("seq", "ctx"), axis=0, tiled=True),
        lax.all_gather(down_weight, ("seq", "ctx"), axis=0, tiled=True),
    )
    down_grad = lax.psum_scatter(
        contract_rows(out_back, hidden), ("seq", "ctx"), scatter_dimension=0, tiled=True
    )
    hidden_back = jnp.dot(out_back, mlp_again[3], preferred_element_type=jnp.float32)
    gate_back = (
        hidden_back * up_proj * sigmoid_gate * (1.0 + gate_proj * (1.0 - sigmoid_gate))
    ).astype(jnp.bfloat16)
    upper_back = (hidden_back * silu_gate).astype(jnp.bfloat16)
    gate_full_grad = contract_rows(normed2, gate_back)
    up_full_grad = contract_rows(normed2, upper_back)
    normed2_back = contract_cols(gate_back, mlp_again[1]) + contract_cols(upper_back, mlp_again[2])
    residual_norm, mlp_gain_term = norm_back(
        residual, scale_two, mlp_again[0].astype(jnp.float32), normed2_back
    )
    mlp_sums = (
        lax.psum_scatter(mlp_gain_term, ("seq", "ctx"), scatter_dimension=0, tiled=True),
        lax.psum_scatter(gate_full_grad, ("seq", "ctx"), scatter_dimension=0, tiled=True),
        lax.psum_scatter(up_full_grad, ("seq", "ctx"), scatter_dimension=0, tiled=True),
    )
    residual_back = out_float + residual_norm
    attn_again = (
        lax.all_gather(attn_gain, ("seq", "ctx"), axis=0, tiled=True),
        lax.all_gather(query_weight, ("seq", "ctx"), axis=0, tiled=True),
        lax.all_gather(key_weight, ("seq", "ctx"), axis=0, tiled=True),
        lax.all_gather(value_weight, ("seq", "ctx"), axis=0, tiled=True),
        lax.all_gather(out_weight, ("seq", "ctx"), axis=0, tiled=True),
    )
    residual_low = residual_back.astype(jnp.bfloat16)
    out_full_grad = contract_rows(attn_low, residual_low)
    attn_back = contract_cols(residual_low, attn_again[4]).astype(jnp.bfloat16)
    grad_mix = attn_back.reshape(row_count, KV_HEADS, group_size, HEAD)
    delta_rows = jnp.transpose(jnp.sum(grad_mix.astype(jnp.float32) * full_mix, axis=-1), (1, 2, 0))

    def grad_step(carry, pieces):
        key_block, value_block, seg_block, block_start = pieces
        allowed = key_mask(seg_block, block_start)

        def compute(acc_query):
            soft_weights = block_soft(key_block, allowed)
            rounded = soft_weights.astype(jnp.bfloat16)
            value_part = jnp.einsum(
                "kgtj,tkgd->jkd", rounded, grad_mix, preferred_element_type=jnp.float32
            )
            soft_back = jnp.einsum(
                "tkgd,jkd->kgtj", grad_mix, value_block, preferred_element_type=jnp.float32
            )
            score_back = (soft_weights * (soft_back - delta_rows[..., None])).astype(jnp.bfloat16)
            acc_query = acc_query + jnp.einsum(
                "kgtj,jkd->tkgd", score_back, key_block, preferred_element_type=jnp.float32
            )
            key_part = jnp.einsum(
                "kgtj,tkgd->jkd", score_back, query_group, preferred_element_type=jnp.float32
            )
            return (acc_query, (key_part, value_part))

        return guarded(compute, carry)

    acc_query, (key_parts, value_parts) = lax.scan(
        grad_step, zero_mix, (key_blocks, value_blocks, seg_blocks, starts)
    )
    key_sums, value_sums = (
        lax.psum_scatter(
            key_parts.reshape(length, KV_HEADS * HEAD).astype(jnp.bfloat16),
            "ctx",
            scatter_dimension=0,
            tiled=True,
        ).astype(jnp.float32),
        lax.psum_scatter(
            value_parts.reshape(length, KV_HEADS * HEAD).astype(jnp.bfloat16),
            "ctx",
            scatter_dimension=0,
            tiled=True,
        ).astype(jnp.float32),
    )
    query_low = (
        rotate((acc_query * score_scale).reshape(row_count, HEADS, HEAD), cosine, -sine_table)
        .astype(jnp.bfloat16)
        .reshape(row_count, HEADS * HEAD)
    )
    key_low = (
        rotate((key_sums * score_scale).reshape(row_count, KV_HEADS, HEAD), cosine, -sine_table)
        .astype(jnp.bfloat16)
        .reshape(row_count, KV_HEADS * HEAD)
    )
    value_low = value_sums.astype(jnp.bfloat16)
    query_full_grad = contract_rows(normed1, query_low)
    key_full_grad = contract_rows(normed1, key_low)
    value_full_grad = contract_rows(normed1, value_low)
    normed1_back = (
        contract_cols(query_low, attn_again[1])
        + contract_cols(key_low, attn_again[2])
        + contract_cols(value_low, attn_again[3])
    )
    input_norm, attn_gain_term = norm_back(
        inputs, scale_one, attn_again[0].astype(jnp.float32), normed1_back
    )
    attn_sums = (
        lax.psum_scatter(attn_gain_term, ("seq", "ctx"), scatter_dimension=0, tiled=True),
        lax.psum_scatter(query_full_grad, ("seq", "ctx"), scatter_dimension=0, tiled=True),
        lax.psum_scatter(key_full_grad, ("seq", "ctx"), scatter_dimension=0, tiled=True),
        lax.psum_scatter(value_full_grad, ("seq", "ctx"), scatter_dimension=0, tiled=True),
        lax.psum_scatter(out_full_grad, ("seq", "ctx"), scatter_dimension=0, tiled=True),
    )
    input_grad = residual_back + input_norm
    return (
        block_output[None],
        input_grad[None],
        attn_sums[0],
        attn_sums[1],
        attn_sums[2],
        attn_sums[3],
        attn_sums[4],
        mlp_sums[0],
        mlp_sums[1],
        mlp_sums[2],
        down_grad,
    )


SEQ_X = [(0, 1), (1, 0), (2, 3), (3, 2)]
SEQ_Y = [(0, 2), (2, 0), (1, 3), (3, 1)]


def gather_ctx(block):
    return lax.all_gather(block, "ctx", axis=0, tiled=True)


def reduce_ctx(partial):
    return lax.psum_scatter(partial, "ctx", scatter_dimension=0, tiled=True)


def exchange_ctx(pieces):
    return lax.all_to_all(pieces, "ctx", 0, 0, tiled=True)


def gather_seq_near(block):
    return lax.ppermute(block, "seq", SEQ_X), lax.ppermute(block, "seq", SEQ_Y)


def gather_seq_far(block, from_x, from_y):
    rows, width = block.shape
    half = rows // 2
    mine = lax.axis_index("seq")
    far_top = lax.ppermute(from_x[:half], "seq", SEQ_Y)
    far_low = lax.ppermute(from_y[half:], "seq", SEQ_X)
    whole = jnp.zeros((4 * rows, width), block.dtype)
    for piece, start in (
        (block, mine * rows),
        (from_x, (mine ^ 1) * rows),
        (from_y, (mine ^ 2) * rows),
        (far_top, (mine ^ 3) * rows),
        (far_low, (mine ^ 3) * rows + half),
    ):
        whole = lax.dynamic_update_slice_in_dim(whole, piece, start, 0)
    return whole


def gather_seq(block):
    return gather_seq_far(block, *gather_seq_near(block))


def seq_part(partials, other, low):
    rows = partials[0].shape[0] // 4
    half = rows // 2
    start = (lax.axis_index("seq") ^ other) * rows + (half if low else 0)
    return jnp.concatenate(
        [lax.dynamic_slice_in_dim(partial, start, half, 0) for partial in partials], axis=1
    )


def seq_parts(partials):
    return (
        seq_part(partials, 3, False),
        seq_part(partials, 3, True),
        seq_part(partials, 1, False),
        seq_part(partials, 2, True),
    )


def send_parts(parts):
    return tuple(
        lax.ppermute(part, "seq", axis) for part, axis in zip(parts, (SEQ_X, SEQ_Y) * 2)
    )


def reduce_seq_near(partials):
    return send_parts(seq_parts(partials))


def add_wide(*terms):
    total = terms[0].astype(jnp.float32)
    for term in terms[1:]:
        total = total + term.astype(jnp.float32)
    return total


def far_sums(partials, top_far, low_far):
    return (
        add_wide(seq_part(partials, 2, False), top_far).astype(jnp.bfloat16),
        add_wide(seq_part(partials, 1, True), low_far).astype(jnp.bfloat16),
    )


def reduce_seq_far(partials, sums, top_near, low_near):
    top_send, low_send = sums
    top_last = lax.ppermute(top_send, "seq", SEQ_Y)
    low_last = lax.ppermute(low_send, "seq", SEQ_X)
    return jnp.concatenate(
        [
            add_wide(seq_part(partials, 0, False), top_near, top_last),
            add_wide(seq_part(partials, 0, True), low_near, low_last),
        ],
        axis=0,
    ).astype(jnp.bfloat16)


def reduce_seq(partials):
    top_far, low_far, *nears = reduce_seq_near(partials)
    return reduce_seq_far(partials, far_sums(partials, top_far, low_far), *nears)


def tie(*values):
    return lax.optimization_barrier(values)


def swap_cores(block):
    return lax.ppermute(block, "ctx", [(device, device ^ 1) for device in range(8)])


def ff_split(width):
    main = width // 8 // 128 * 128
    return main, width // 8 - main


def ff_slices(weight):
    rows, width = weight.shape
    main, tail = ff_split(width)
    return (
        jnp.transpose(weight[:, : 8 * main].reshape(rows, 8, main), (1, 0, 2)),
        jnp.transpose(weight[:, 8 * main :].reshape(rows, 8, tail), (1, 0, 2)),
    )


def ff_rows(main, tail):
    count, rows, width = main.shape
    return jnp.concatenate(
        [
            jnp.transpose(main, (1, 0, 2)).reshape(rows, count * width),
            jnp.transpose(tail, (1, 0, 2)).reshape(rows, count * tail.shape[2]),
        ],
        axis=1,
    )


def head_slices(weight):
    rows = weight.shape[0]
    split = weight.reshape(rows, KV_HEADS, 8, HEAD)
    return jnp.transpose(split, (2, 0, 1, 3)).reshape(8, rows, KV_HEADS * HEAD)


def from_head_slices(pieces):
    rows = pieces.shape[1]
    split = pieces.reshape(8, rows, KV_HEADS, HEAD)
    return jnp.transpose(split, (1, 2, 0, 3)).reshape(rows, HEADS * HEAD)


def attend_mask(edge, first_row, block, span):
    row = first_row + lax.broadcasted_iota(jnp.int32, (block, span), 0)
    column = lax.broadcasted_iota(jnp.int32, (block, span), 1)
    return (column <= row) & (column >= jnp.where(row >= edge, edge, 0))


def soft_rows(query, key, allowed):
    scores = lax.dot_general(
        query, key, (((1,), (1,)), ((), ())), preferred_element_type=jnp.float32
    )
    scores = jnp.where(allowed, scores, MASKED)
    exponents = jnp.exp(scores - jnp.max(scores, axis=-1, keepdims=True))
    return exponents * (1.0 / jnp.sum(exponents, axis=-1, keepdims=True))


def attend_kernel(edge_ref, query_ref, key_ref, value_ref, mix_ref, *, block, blocks):
    step = pl.program_id(1)
    for index in range(blocks):

        @pl.when(step == index)
        def _(index=index):
            span = (index + 1) * block
            allowed = attend_mask(edge_ref[0], index * block, block, span)
            mixed = []
            for head in range(2):
                cut = slice(head * HEAD, (head + 1) * HEAD)
                soft = soft_rows(query_ref[:, cut], key_ref[:span, cut], allowed)
                mixed.append(
                    jnp.dot(
                        soft.astype(jnp.bfloat16),
                        value_ref[:span, cut],
                        preferred_element_type=jnp.float32,
                    )
                )
            mix_ref[...] = jnp.concatenate(mixed, axis=-1).astype(mix_ref.dtype)


def attend_back_kernel(
    edge_ref,
    query_ref,
    key_ref,
    value_ref,
    back_ref,
    query_back_ref,
    key_back_ref,
    value_back_ref,
    *,
    block,
    blocks,
    score_scale,
):
    step = pl.program_id(1)

    @pl.when(step == 0)
    def _():
        key_back_ref[...] = jnp.zeros_like(key_back_ref)
        value_back_ref[...] = jnp.zeros_like(value_back_ref)

    for index in range(blocks):

        @pl.when(step == index)
        def _(index=index):
            span = (index + 1) * block
            allowed = attend_mask(edge_ref[0], index * block, block, span)
            query_parts, key_parts, value_parts = [], [], []
            for head in range(2):
                cut = slice(head * HEAD, (head + 1) * HEAD)
                query, key = query_ref[:, cut], key_ref[:span, cut]
                back = back_ref[:, cut]
                soft = soft_rows(query, key, allowed)
                soft_back = contract_cols(back, value_ref[:span, cut])
                delta = jnp.sum(soft * soft_back, axis=-1, keepdims=True)
                score_back = (soft * (soft_back - delta)).astype(jnp.bfloat16)
                query_parts.append(
                    jnp.dot(score_back, key, preferred_element_type=jnp.float32) * score_scale
                )
                key_parts.append(contract_rows(score_back, query))
                value_parts.append(contract_rows(soft.astype(jnp.bfloat16), back))
            query_back_ref[...] = jnp.concatenate(query_parts, axis=-1)
            key_back_ref[:span, :] += jnp.concatenate(key_parts, axis=-1)
            value_back_ref[:span, :] += jnp.concatenate(value_parts, axis=-1)


def attend_specs(length, block):
    rows = pl.BlockSpec((block, 2 * HEAD), lambda pair, step: (step, pair))
    whole = pl.BlockSpec((length, 2 * HEAD), lambda pair, step: (0, pair))
    edge = pl.BlockSpec(memory_space=pltpu.SMEM)
    return edge, rows, whole


def attend_cost(length, width, products):
    return pl.CostEstimate(
        flops=8 * products * length * length * width,
        transcendentals=length * length * width // HEAD,
        bytes_accessed=(2 * products + 4) * length * width,
    )


def attend(edge, queries, keys, values):
    length, width = queries.shape
    block = 256
    blocks = length // block
    scalar, rows, whole = attend_specs(length, block)

    def body(*refs):
        attend_kernel(*refs, block=block, blocks=blocks)

    return pl.pallas_call(
        body,
        name="attend",
        grid=(width // (2 * HEAD), blocks),
        in_specs=[scalar, rows, whole, whole],
        out_specs=rows,
        out_shape=jax.ShapeDtypeStruct((length, width), jnp.bfloat16),
        cost_estimate=attend_cost(length, width, 2),
    )(edge, queries, keys, values)


def attend_back(edge, queries, keys, values, back, score_scale):
    length, width = queries.shape
    block = 256
    blocks = length // block
    scalar, rows, whole = attend_specs(length, block)

    def body(*refs):
        attend_back_kernel(*refs, block=block, blocks=blocks, score_scale=score_scale)

    shape = jax.ShapeDtypeStruct((length, width), jnp.float32)
    return pl.pallas_call(
        body,
        name="attend_back",
        grid=(width // (2 * HEAD), blocks),
        in_specs=[scalar, rows, whole, whole, rows],
        out_specs=(rows, whole, whole),
        out_shape=(shape, shape, shape),
        cost_estimate=attend_cost(length, width, 5),
    )(edge, queries, keys, values, back)


def turn(values, cosine, sine_table):
    half = HEAD // 2
    lane = lax.broadcasted_iota(jnp.int32, values.shape, 1) % HEAD
    turned = jnp.where(
        lane < half, -jnp.roll(values, -half, axis=1), jnp.roll(values, half, axis=1)
    )
    return values * cosine + turned * sine_table


def local_columns(
    block_input,
    positions,
    segments,
    cotangent,
    attn_gain,
    query_weight,
    key_weight,
    value_weight,
    out_weight,
    mlp_gain,
    gate_weight,
    up_weight,
    down_weight,
):
    f32, bf16 = jnp.float32, jnp.bfloat16
    score_scale = HEAD ** (-0.5)
    length = segments.shape[1]
    rows = query_weight.shape[0]
    head_width = KV_HEADS * HEAD
    inputs = block_input[0].astype(f32)
    out_back = cotangent[0]
    gain_one = attn_gain.astype(f32)[:, None]
    gain_two = mlp_gain.astype(f32)[:, None]

    def fold(weight, gain):
        return (weight.astype(f32) * gain).astype(bf16)

    inputs_all = gather_ctx(block_input[0])
    key_value = jnp.stack([fold(key_weight, gain_one), fold(value_weight, gain_one)])
    attn_pieces = jnp.concatenate(
        [
            head_slices(fold(query_weight, gain_one)),
            jnp.tile(key_value, (4, 1, 1)),
        ],
        axis=2,
    )
    main, tail = ff_split(gate_weight.shape[1])
    both = 2 * (main + tail)
    gate_main, gate_tail = ff_slices(fold(gate_weight, gain_two))
    up_main, up_tail = ff_slices(fold(up_weight, gain_two))
    down_pieces = jnp.concatenate(ff_slices(down_weight), axis=2)
    gate_up_pieces = jnp.concatenate([gate_main, up_main, gate_tail, up_tail], axis=2)
    attn_own = exchange_ctx(attn_pieces).reshape(8 * rows, 2 * head_width)
    attn_own, down_pieces, gate_up_pieces = tie(attn_own, down_pieces, gate_up_pieces)
    attn_cols = gather_seq(attn_own)
    core = lax.axis_index("ctx") % 2
    own_cols = attn_cols[:, head_width:]
    other_cols = swap_cores(own_cols)
    attn_cols = jnp.concatenate(
        [
            attn_cols[:, :head_width],
            jnp.where(core == 0, own_cols, other_cols),
            jnp.where(core == 0, other_cols, own_cols),
        ],
        axis=1,
    )
    out_rows = gather_seq(out_weight)
    down_own = exchange_ctx(down_pieces).reshape(8 * rows, -1)
    down_own, gate_up_pieces = tie(down_own, gate_up_pieces)
    gate_up_own = exchange_ctx(gate_up_pieces).reshape(8 * rows, -1)

    edge = jnp.sum((segments[0] == 0).astype(jnp.int32))
    token = jnp.arange(length, dtype=jnp.int32)
    position = jnp.where(token < edge, token + (length - edge), token - edge)
    cosine, sine_table = rope_tables(position, HEAD)
    cosine = jnp.tile(cosine, (1, KV_HEADS))
    sine_table = jnp.tile(sine_table, (1, KV_HEADS))
    edge = edge[None]

    wide = inputs_all.astype(f32)
    shaped_all = (wide * rms_scale(wide)).astype(bf16)
    raw = jnp.dot(shaped_all, attn_cols, preferred_element_type=f32)
    raw, down_own = tie(raw, down_own)
    down_near = gather_seq_near(down_own)
    queries = turn(raw[:, :head_width], cosine, sine_table).astype(bf16)
    keys = turn(raw[:, head_width : 2 * head_width], cosine, sine_table).astype(bf16)
    values = raw[:, 2 * head_width :].astype(bf16)
    queries = queries * jnp.asarray(score_scale, bf16)
    attn_low = attend(edge, queries, keys, values)
    attn_low, out_rows, back_late, gate_up_own, *down_near = tie(
        attn_low, out_rows, out_back, gate_up_own, *down_near
    )
    gate_up_near = gather_seq_near(gate_up_own)
    down_cols = gather_seq_far(down_own, *down_near)
    mixed = jnp.dot(attn_low, out_rows, preferred_element_type=f32).astype(bf16)
    mixed_own = reduce_ctx(mixed)
    mixed_own, down_cols, *gate_up_near = tie(mixed_own, down_cols, *gate_up_near)
    residual = inputs + mixed_own.astype(f32)
    scale_two = rms_scale(residual)
    shaped_two = residual * scale_two
    shaped_low = shaped_two.astype(bf16)
    normed_all = gather_ctx(shaped_low)
    shaped_two, back_late = tie(shaped_two, back_late)
    gate_up = gather_seq_far(gate_up_own, *gate_up_near)
    back_all = gather_ctx(back_late)
    proj = jnp.dot(normed_all, gate_up, preferred_element_type=f32)

    def halves(left_tail, right_tail, left, right):
        return jnp.concatenate([left, left_tail], axis=1), jnp.concatenate([right, right_tail], axis=1)

    gate_proj, up_proj = halves(
        proj[:, 2 * main : 2 * main + tail],
        proj[:, 2 * main + tail :],
        proj[:, :main],
        proj[:, main : 2 * main],
    )
    sigmoid_gate = jax.nn.sigmoid(gate_proj)
    silu_gate = gate_proj * sigmoid_gate
    hidden = (silu_gate * up_proj).astype(bf16)
    mixed_out = contract_cols(hidden, down_cols).astype(bf16)
    mixed_out, back_all = tie(mixed_out, back_all)
    out_own = reduce_ctx(mixed_out)
    hidden_back = jnp.dot(back_all, down_cols, preferred_element_type=f32)
    gate_back = (
        hidden_back * up_proj * sigmoid_gate * (1.0 + gate_proj * (1.0 - sigmoid_gate))
    ).astype(bf16)
    upper_back = (hidden_back * silu_gate).astype(bf16)
    gate_up_back = jnp.concatenate(
        [gate_back[:, :main], upper_back[:, :main], gate_back[:, main:], upper_back[:, main:]],
        axis=1,
    )
    weighted = reduce_ctx(contract_cols(gate_up_back, gate_up).astype(bf16))
    gate_up_grad = contract_rows(normed_all, gate_up_back).astype(bf16)
    down_grad = contract_rows(back_all, hidden).astype(bf16)
    mlp_grads = [gate_up_grad, down_grad]
    out_own, *mlp_parts = tie(out_own, *seq_parts(mlp_grads))
    mlp_near = send_parts(mlp_parts)
    weighted, *mlp_near = tie(weighted, *mlp_near)
    weighted = weighted.astype(f32)
    residual_back = out_back.astype(f32) + scale_two * (
        weighted - shaped_two * jnp.mean(weighted * shaped_two, axis=-1, keepdims=True)
    )
    residual_low = residual_back.astype(bf16)
    low_all = gather_ctx(residual_low)
    residual_back, *mlp_near = tie(residual_back, *mlp_near)
    mlp_sums = far_sums(mlp_grads, *mlp_near[:2])
    mlp_grads_own = reduce_seq_far(mlp_grads, mlp_sums, *mlp_near[2:])
    mlp_grad = exchange_ctx(mlp_grads_own.reshape(8, rows, -1))
    attn_back = contract_cols(low_all, out_rows).astype(bf16)
    query_back, key_back, value_back = attend_back(
        edge, queries, keys, values, attn_back, score_scale
    )
    heads_back = jnp.concatenate(
        [
            turn(query_back, cosine, -sine_table).astype(bf16),
            turn(key_back, cosine, -sine_table).astype(bf16),
            value_back.astype(bf16),
        ],
        axis=1,
    )
    heads_back, mlp_grad = tie(heads_back, mlp_grad)
    attn_full_grad = contract_rows(shaped_all, heads_back)
    key_part = attn_full_grad[:, head_width : 2 * head_width]
    value_part = attn_full_grad[:, 2 * head_width :]
    other_part = jnp.where(core == 0, value_part, key_part).astype(bf16)
    heads_back, other_part = tie(heads_back, other_part)
    other_part = swap_cores(other_part)
    weighted_part = contract_cols(heads_back, attn_cols).astype(bf16)
    weighted_part, low_all = tie(weighted_part, low_all)
    weighted_one = reduce_ctx(weighted_part).astype(f32)
    own_part = jnp.where(core == 0, key_part, value_part) + other_part.astype(f32)
    attn_grad_own = reduce_seq(
        [jnp.concatenate([attn_full_grad[:, :head_width].astype(bf16), own_part.astype(bf16)], axis=1)]
    )
    out_grad = reduce_seq([contract_rows(attn_low, low_all).astype(bf16)]).astype(f32)
    attn_grad_own, mlp_grad = tie(attn_grad_own, mlp_grad)
    mlp_grad = mlp_grad.astype(f32)
    attn_grad = exchange_ctx(attn_grad_own.reshape(8, rows, -1))

    scale_one = rms_scale(inputs)
    shaped_one = inputs * scale_one
    input_grad = residual_back + scale_one * (
        weighted_one - shaped_one * jnp.mean(weighted_one * shaped_one, axis=-1, keepdims=True)
    )
    block_output = (residual + out_own.astype(f32)).astype(bf16)
    gate_rows = ff_rows(mlp_grad[:, :, :main], mlp_grad[:, :, 2 * main : 2 * main + tail])
    up_rows = ff_rows(mlp_grad[:, :, main : 2 * main], mlp_grad[:, :, 2 * main + tail : both])
    down_grad = ff_rows(mlp_grad[:, :, both : both + main], mlp_grad[:, :, both + main :])
    attn_grad, out_grad, gate_rows, up_rows, down_grad = tie(
        attn_grad, out_grad, gate_rows, up_rows, down_grad
    )
    attn_grad = attn_grad.astype(f32)
    query_rows = from_head_slices(attn_grad[:, :, :head_width])
    pair_rows = jnp.sum(attn_grad[:, :, head_width:].reshape(4, 2, rows, head_width), axis=0)
    key_rows, value_rows = pair_rows[0], pair_rows[1]

    def row_sum(weight, grad):
        return jnp.sum(weight.astype(f32) * grad, axis=1)

    attn_gain_grad = (
        row_sum(query_weight, query_rows)
        + row_sum(key_weight, key_rows)
        + row_sum(value_weight, value_rows)
    )
    mlp_gain_grad = row_sum(gate_weight, gate_rows) + row_sum(up_weight, up_rows)
    return (
        block_output[None],
        input_grad[None],
        attn_gain_grad,
        query_rows * gain_one,
        key_rows * gain_one,
        value_rows * gain_one,
        out_grad,
        mlp_gain_grad,
        gate_rows * gain_two,
        up_rows * gain_two,
        down_grad,
    )


def solution(mesh):
    placed = (
        P("seq", "ctx", None),
        P("seq", "ctx"),
        P("seq", None),
        P("seq", "ctx", None),
        P(("seq", "ctx")),
        P(("seq", "ctx"), None),
        P(("seq", "ctx"), None),
        P(("seq", "ctx"), None),
        P(("seq", "ctx"), None),
        P(("seq", "ctx")),
        P(("seq", "ctx"), None),
        P(("seq", "ctx"), None),
        P(("seq", "ctx"), None),
    )
    seq_count, ctx_count = mesh.shape["seq"], mesh.shape["ctx"]

    def run(*args):
        width = args[0].shape[2]
        fits = (
            seq_count == KV_HEADS == 4
            and ctx_count == HEADS // KV_HEADS == 8
            and width == seq_count * ctx_count * HEAD
        )
        return jax.shard_map(
            local_columns if fits else local_rows,
            mesh=mesh,
            in_specs=placed,
            out_specs=(
                P("seq", "ctx", None),
                P("seq", "ctx", None),
                P(("seq", "ctx")),
                P(("seq", "ctx"), None),
                P(("seq", "ctx"), None),
                P(("seq", "ctx"), None),
                P(("seq", "ctx"), None),
                P(("seq", "ctx")),
                P(("seq", "ctx"), None),
                P(("seq", "ctx"), None),
                P(("seq", "ctx"), None),
            ),
            check_vma=False,
        )(*args)

    return run
```

```python
import jax
import jax.numpy as jnp
from jax import lax
from jax.experimental import pallas as pl
from jax.experimental.pallas import tpu as pltpu
from jax.sharding import PartitionSpec as P

HEADS = 32
KV_HEADS = 4
HEAD = 64


EPSILON = 1e-05
MASKED = -1e30


def rope_tables(position, head_size):
    half_size = head_size // 2
    inverse = 1.0 / 10000.0 ** (jnp.arange(half_size, dtype=jnp.float32) * 2.0 / head_size)
    angles = position.astype(jnp.float32)[:, None] * inverse[None, :]
    cosine = jnp.cos(angles)
    sine_table = jnp.sin(angles)
    return (jnp.concatenate([cosine, cosine], -1), jnp.concatenate([sine_table, sine_table], -1))


def rotate(values, cosine, sine_table):
    half_size = values.shape[-1] // 2
    turned = jnp.concatenate([-values[..., half_size:], values[..., :half_size]], -1)
    return values * cosine[:, None, :] + turned * sine_table[:, None, :]


def rms_scale(inputs):
    return lax.rsqrt(jnp.mean(inputs * inputs, axis=-1, keepdims=True) + EPSILON)


def norm_back(inputs, row_scale, gain, upstream):
    shaped = inputs * row_scale
    weighted = upstream * gain
    gain_term = jnp.sum(upstream * shaped, axis=0)
    return (
        row_scale * (weighted - shaped * jnp.mean(weighted * shaped, axis=-1, keepdims=True)),
        gain_term,
    )


def contract_rows(left, right):
    return lax.dot_general(
        left, right, (((0,), (0,)), ((), ())), preferred_element_type=jnp.float32
    )


def contract_cols(left, right):
    return lax.dot_general(
        left, right, (((1,), (1,)), ((), ())), preferred_element_type=jnp.float32
    )


def local_rows(
    block_input,
    positions,
    segments,
    cotangent,
    attn_gain,
    query_weight,
    key_weight,
    value_weight,
    out_weight,
    mlp_gain,
    gate_weight,
    up_weight,
    down_weight,
):
    row_count = block_input.shape[1]
    group_size = HEADS // KV_HEADS
    score_scale = HEAD ** (-0.5)
    inputs = block_input[0].astype(jnp.float32)
    seg_all = segments[0]
    length = seg_all.shape[0]
    block_size = min(512, length)
    block_count = length // block_size
    first_row = lax.axis_index("ctx") * row_count
    query_index = first_row + jnp.arange(row_count, dtype=jnp.int32)
    seg_rows = lax.dynamic_slice_in_dim(seg_all, first_row, row_count)
    cosine, sine_table = rope_tables(positions[0], HEAD)
    starts = jnp.arange(block_count, dtype=jnp.int32) * block_size
    seg_blocks = seg_all.reshape(block_count, block_size)

    def key_mask(seg_block, block_start):
        key_index = block_start + jnp.arange(block_size, dtype=jnp.int32)
        return (seg_rows[:, None] == seg_block[None, :]) & (
            key_index[None, :] <= query_index[:, None]
        )

    def guarded(compute, running):
        result = compute(running)
        return result

    attn_params = (
        lax.all_gather(attn_gain, ("seq", "ctx"), axis=0, tiled=True),
        lax.all_gather(query_weight, ("seq", "ctx"), axis=0, tiled=True),
        lax.all_gather(key_weight, ("seq", "ctx"), axis=0, tiled=True),
        lax.all_gather(value_weight, ("seq", "ctx"), axis=0, tiled=True),
        lax.all_gather(out_weight, ("seq", "ctx"), axis=0, tiled=True),
    )
    gain_one = attn_params[0].astype(jnp.float32)
    scale_one = rms_scale(inputs)
    normed1 = (inputs * scale_one * gain_one).astype(jnp.bfloat16)
    query_raw = jnp.dot(normed1, attn_params[1], preferred_element_type=jnp.float32)
    key_raw = jnp.dot(normed1, attn_params[2], preferred_element_type=jnp.float32)
    value_raw = jnp.dot(normed1, attn_params[3], preferred_element_type=jnp.float32)
    queries = rotate(query_raw.reshape(row_count, HEADS, HEAD), cosine, sine_table).astype(
        jnp.bfloat16
    )
    keys_local = (
        rotate(key_raw.reshape(row_count, KV_HEADS, HEAD), cosine, sine_table)
        .astype(jnp.bfloat16)
        .reshape(row_count, KV_HEADS * HEAD)
    )
    values_local = value_raw.astype(jnp.bfloat16)
    keys_all, values_all = (
        lax.all_gather(keys_local, "ctx", axis=0, tiled=True),
        lax.all_gather(values_local, "ctx", axis=0, tiled=True),
    )
    key_blocks = keys_all.reshape(block_count, block_size, KV_HEADS, HEAD)
    value_blocks = values_all.reshape(block_count, block_size, KV_HEADS, HEAD)
    query_group = queries.reshape(row_count, KV_HEADS, group_size, HEAD)

    def block_scores(key_block, allowed):
        scores = (
            jnp.einsum("tkgd,jkd->kgtj", query_group, key_block, preferred_element_type=jnp.float32)
            * score_scale
        )
        return jnp.where(allowed[None, None], scores, MASKED)

    def max_step(carry, pieces):
        key_block, seg_block, block_start = pieces
        allowed = key_mask(seg_block, block_start)

        def compute(running):
            run_max, run_sum = running
            scores = block_scores(key_block, allowed)
            new_max = jnp.maximum(run_max, jnp.max(scores, axis=-1))
            exponents = jnp.where(allowed[None, None], jnp.exp(scores - new_max[..., None]), 0.0)
            return (new_max, run_sum * jnp.exp(run_max - new_max) + jnp.sum(exponents, axis=-1))

        return (guarded(compute, carry), None)

    start_max = jnp.full((KV_HEADS, group_size, row_count), MASKED, jnp.float32)
    start_sum = jnp.zeros((KV_HEADS, group_size, row_count), jnp.float32)
    (run_max, run_sum), unused = lax.scan(
        max_step, (start_max, start_sum), (key_blocks, seg_blocks, starts)
    )
    log_sum = run_max + jnp.log(run_sum)

    def block_soft(key_block, allowed):
        scores = block_scores(key_block, allowed)
        return jnp.where(allowed[None, None], jnp.exp(scores - log_sum[..., None]), 0.0)

    def value_step(carry, pieces):
        key_block, value_block, seg_block, block_start = pieces
        allowed = key_mask(seg_block, block_start)

        def compute(running):
            acc_out, acc_fix = running
            soft_weights = block_soft(key_block, allowed)
            rounded = soft_weights.astype(jnp.bfloat16)
            leftover = (soft_weights - rounded.astype(jnp.float32)).astype(jnp.bfloat16)
            acc_out = acc_out + jnp.einsum(
                "kgtj,jkd->tkgd", rounded, value_block, preferred_element_type=jnp.float32
            )
            acc_fix = acc_fix + jnp.einsum(
                "kgtj,jkd->tkgd", leftover, value_block, preferred_element_type=jnp.float32
            )
            return (acc_out, acc_fix)

        return (guarded(compute, carry), None)

    zero_mix = jnp.zeros((row_count, KV_HEADS, group_size, HEAD), jnp.float32)
    (acc_out, acc_fix), unused = lax.scan(
        value_step, (zero_mix, zero_mix), (key_blocks, value_blocks, seg_blocks, starts)
    )
    attn_low = acc_out.reshape(row_count, HEADS * HEAD).astype(jnp.bfloat16)
    full_mix = acc_out + acc_fix
    residual = inputs + jnp.dot(attn_low, attn_params[4], preferred_element_type=jnp.float32)
    mlp_params = (
        lax.all_gather(mlp_gain, ("seq", "ctx"), axis=0, tiled=True),
        lax.all_gather(gate_weight, ("seq", "ctx"), axis=0, tiled=True),
        lax.all_gather(up_weight, ("seq", "ctx"), axis=0, tiled=True),
        lax.all_gather(down_weight, ("seq", "ctx"), axis=0, tiled=True),
    )
    gain_two = mlp_params[0].astype(jnp.float32)
    scale_two = rms_scale(residual)
    normed2 = (residual * scale_two * gain_two).astype(jnp.bfloat16)
    gate_proj = jnp.dot(normed2, mlp_params[1], preferred_element_type=jnp.float32)
    up_proj = jnp.dot(normed2, mlp_params[2], preferred_element_type=jnp.float32)
    sigmoid_gate = jax.nn.sigmoid(gate_proj)
    silu_gate = gate_proj * sigmoid_gate
    hidden = (silu_gate * up_proj).astype(jnp.bfloat16)
    block_output = (residual + contract_cols(hidden, mlp_params[3])).astype(jnp.bfloat16)
    out_back = cotangent[0]
    out_float = out_back.astype(jnp.float32)
    mlp_again = (
        lax.all_gather(mlp_gain, ("seq", "ctx"), axis=0, tiled=True),
        lax.all_gather(gate_weight, ("seq", "ctx"), axis=0, tiled=True),
        lax.all_gather(up_weight, ("seq", "ctx"), axis=0, tiled=True),
        lax.all_gather(down_weight, ("seq", "ctx"), axis=0, tiled=True),
    )
    down_grad = lax.psum_scatter(
        contract_rows(out_back, hidden), ("seq", "ctx"), scatter_dimension=0, tiled=True
    )
    hidden_back = jnp.dot(out_back, mlp_again[3], preferred_element_type=jnp.float32)
    gate_back = (
        hidden_back * up_proj * sigmoid_gate * (1.0 + gate_proj * (1.0 - sigmoid_gate))
    ).astype(jnp.bfloat16)
    upper_back = (hidden_back * silu_gate).astype(jnp.bfloat16)
    gate_full_grad = contract_rows(normed2, gate_back)
    up_full_grad = contract_rows(normed2, upper_back)
    normed2_back = contract_cols(gate_back, mlp_again[1]) + contract_cols(upper_back, mlp_again[2])
    residual_norm, mlp_gain_term = norm_back(
        residual, scale_two, mlp_again[0].astype(jnp.float32), normed2_back
    )
    mlp_sums = (
        lax.psum_scatter(mlp_gain_term, ("seq", "ctx"), scatter_dimension=0, tiled=True),
        lax.psum_scatter(gate_full_grad, ("seq", "ctx"), scatter_dimension=0, tiled=True),
        lax.psum_scatter(up_full_grad, ("seq", "ctx"), scatter_dimension=0, tiled=True),
    )
    residual_back = out_float + residual_norm
    attn_again = (
        lax.all_gather(attn_gain, ("seq", "ctx"), axis=0, tiled=True),
        lax.all_gather(query_weight, ("seq", "ctx"), axis=0, tiled=True),
        lax.all_gather(key_weight, ("seq", "ctx"), axis=0, tiled=True),
        lax.all_gather(value_weight, ("seq", "ctx"), axis=0, tiled=True),
        lax.all_gather(out_weight, ("seq", "ctx"), axis=0, tiled=True),
    )
    residual_low = residual_back.astype(jnp.bfloat16)
    out_full_grad = contract_rows(attn_low, residual_low)
    attn_back = contract_cols(residual_low, attn_again[4]).astype(jnp.bfloat16)
    grad_mix = attn_back.reshape(row_count, KV_HEADS, group_size, HEAD)
    delta_rows = jnp.transpose(jnp.sum(grad_mix.astype(jnp.float32) * full_mix, axis=-1), (1, 2, 0))

    def grad_step(carry, pieces):
        key_block, value_block, seg_block, block_start = pieces
        allowed = key_mask(seg_block, block_start)

        def compute(acc_query):
            soft_weights = block_soft(key_block, allowed)
            rounded = soft_weights.astype(jnp.bfloat16)
            value_part = jnp.einsum(
                "kgtj,tkgd->jkd", rounded, grad_mix, preferred_element_type=jnp.float32
            )
            soft_back = jnp.einsum(
                "tkgd,jkd->kgtj", grad_mix, value_block, preferred_element_type=jnp.float32
            )
            score_back = (soft_weights * (soft_back - delta_rows[..., None])).astype(jnp.bfloat16)
            acc_query = acc_query + jnp.einsum(
                "kgtj,jkd->tkgd", score_back, key_block, preferred_element_type=jnp.float32
            )
            key_part = jnp.einsum(
                "kgtj,tkgd->jkd", score_back, query_group, preferred_element_type=jnp.float32
            )
            return (acc_query, (key_part, value_part))

        return guarded(compute, carry)

    acc_query, (key_parts, value_parts) = lax.scan(
        grad_step, zero_mix, (key_blocks, value_blocks, seg_blocks, starts)
    )
    key_sums, value_sums = (
        lax.psum_scatter(
            key_parts.reshape(length, KV_HEADS * HEAD).astype(jnp.bfloat16),
            "ctx",
            scatter_dimension=0,
            tiled=True,
        ).astype(jnp.float32),
        lax.psum_scatter(
            value_parts.reshape(length, KV_HEADS * HEAD).astype(jnp.bfloat16),
            "ctx",
            scatter_dimension=0,
            tiled=True,
        ).astype(jnp.float32),
    )
    query_low = (
        rotate((acc_query * score_scale).reshape(row_count, HEADS, HEAD), cosine, -sine_table)
        .astype(jnp.bfloat16)
        .reshape(row_count, HEADS * HEAD)
    )
    key_low = (
        rotate((key_sums * score_scale).reshape(row_count, KV_HEADS, HEAD), cosine, -sine_table)
        .astype(jnp.bfloat16)
        .reshape(row_count, KV_HEADS * HEAD)
    )
    value_low = value_sums.astype(jnp.bfloat16)
    query_full_grad = contract_rows(normed1, query_low)
    key_full_grad = contract_rows(normed1, key_low)
    value_full_grad = contract_rows(normed1, value_low)
    normed1_back = (
        contract_cols(query_low, attn_again[1])
        + contract_cols(key_low, attn_again[2])
        + contract_cols(value_low, attn_again[3])
    )
    input_norm, attn_gain_term = norm_back(
        inputs, scale_one, attn_again[0].astype(jnp.float32), normed1_back
    )
    attn_sums = (
        lax.psum_scatter(attn_gain_term, ("seq", "ctx"), scatter_dimension=0, tiled=True),
        lax.psum_scatter(query_full_grad, ("seq", "ctx"), scatter_dimension=0, tiled=True),
        lax.psum_scatter(key_full_grad, ("seq", "ctx"), scatter_dimension=0, tiled=True),
        lax.psum_scatter(value_full_grad, ("seq", "ctx"), scatter_dimension=0, tiled=True),
        lax.psum_scatter(out_full_grad, ("seq", "ctx"), scatter_dimension=0, tiled=True),
    )
    input_grad = residual_back + input_norm
    return (
        block_output[None],
        input_grad[None],
        attn_sums[0],
        attn_sums[1],
        attn_sums[2],
        attn_sums[3],
        attn_sums[4],
        mlp_sums[0],
        mlp_sums[1],
        mlp_sums[2],
        down_grad,
    )


SEQ_X = [(0, 1), (1, 0), (2, 3), (3, 2)]
SEQ_Y = [(0, 2), (2, 0), (1, 3), (3, 1)]


def gather_ctx(block):
    return lax.all_gather(block, "ctx", axis=0, tiled=True)


def reduce_ctx(partial):
    return lax.psum_scatter(partial, "ctx", scatter_dimension=0, tiled=True)


def exchange_ctx(pieces):
    return lax.all_to_all(pieces, "ctx", 0, 0, tiled=True)


def gather_seq_near(block):
    return lax.ppermute(block, "seq", SEQ_X), lax.ppermute(block, "seq", SEQ_Y)


def gather_seq_far(block, from_x, from_y):
    rows, width = block.shape
    half = rows // 2
    mine = lax.axis_index("seq")
    far_top = lax.ppermute(from_x[:half], "seq", SEQ_Y)
    far_low = lax.ppermute(from_y[half:], "seq", SEQ_X)
    whole = jnp.zeros((4 * rows, width), block.dtype)
    for piece, start in (
        (block, mine * rows),
        (from_x, (mine ^ 1) * rows),
        (from_y, (mine ^ 2) * rows),
        (far_top, (mine ^ 3) * rows),
        (far_low, (mine ^ 3) * rows + half),
    ):
        whole = lax.dynamic_update_slice_in_dim(whole, piece, start, 0)
    return whole


def gather_seq(block):
    return gather_seq_far(block, *gather_seq_near(block))


def seq_part(partials, other, low):
    rows = partials[0].shape[0] // 4
    half = rows // 2
    start = (lax.axis_index("seq") ^ other) * rows + (half if low else 0)
    return jnp.concatenate(
        [lax.dynamic_slice_in_dim(partial, start, half, 0) for partial in partials], axis=1
    )


def seq_parts(partials):
    return (
        seq_part(partials, 3, False),
        seq_part(partials, 3, True),
        seq_part(partials, 1, False),
        seq_part(partials, 2, True),
    )


def send_parts(parts):
    return tuple(
        lax.ppermute(part, "seq", axis) for part, axis in zip(parts, (SEQ_X, SEQ_Y) * 2)
    )


def reduce_seq_near(partials):
    return send_parts(seq_parts(partials))


def add_wide(*terms):
    total = terms[0].astype(jnp.float32)
    for term in terms[1:]:
        total = total + term.astype(jnp.float32)
    return total


def far_sums(partials, top_far, low_far):
    return (
        add_wide(seq_part(partials, 2, False), top_far).astype(jnp.bfloat16),
        add_wide(seq_part(partials, 1, True), low_far).astype(jnp.bfloat16),
    )


def reduce_seq_far(partials, sums, top_near, low_near):
    top_send, low_send = sums
    top_last = lax.ppermute(top_send, "seq", SEQ_Y)
    low_last = lax.ppermute(low_send, "seq", SEQ_X)
    return jnp.concatenate(
        [
            add_wide(seq_part(partials, 0, False), top_near, top_last),
            add_wide(seq_part(partials, 0, True), low_near, low_last),
        ],
        axis=0,
    ).astype(jnp.bfloat16)


def reduce_seq(partials):
    top_far, low_far, *nears = reduce_seq_near(partials)
    return reduce_seq_far(partials, far_sums(partials, top_far, low_far), *nears)


def tie(*values):
    return lax.optimization_barrier(values)


def swap_cores(block):
    return lax.ppermute(block, "ctx", [(device, device ^ 1) for device in range(8)])


def ff_split(width):
    main = width // 8 // 128 * 128
    return main, width // 8 - main


def ff_slices(weight):
    rows, width = weight.shape
    main, tail = ff_split(width)
    return (
        jnp.transpose(weight[:, : 8 * main].reshape(rows, 8, main), (1, 0, 2)),
        jnp.transpose(weight[:, 8 * main :].reshape(rows, 8, tail), (1, 0, 2)),
    )


def ff_rows(main, tail):
    count, rows, width = main.shape
    return jnp.concatenate(
        [
            jnp.transpose(main, (1, 0, 2)).reshape(rows, count * width),
            jnp.transpose(tail, (1, 0, 2)).reshape(rows, count * tail.shape[2]),
        ],
        axis=1,
    )


def head_slices(weight):
    rows = weight.shape[0]
    split = weight.reshape(rows, KV_HEADS, 8, HEAD)
    return jnp.transpose(split, (2, 0, 1, 3)).reshape(8, rows, KV_HEADS * HEAD)


def from_head_slices(pieces):
    rows = pieces.shape[1]
    split = pieces.reshape(8, rows, KV_HEADS, HEAD)
    return jnp.transpose(split, (1, 2, 0, 3)).reshape(rows, HEADS * HEAD)


def attend_mask(edge, first_row, block, span):
    row = first_row + lax.broadcasted_iota(jnp.int32, (block, span), 0)
    column = lax.broadcasted_iota(jnp.int32, (block, span), 1)
    return (column <= row) & (column >= jnp.where(row >= edge, edge, 0))


def soft_rows(query, key, allowed):
    scores = lax.dot_general(
        query, key, (((1,), (1,)), ((), ())), preferred_element_type=jnp.float32
    )
    scores = jnp.where(allowed, scores, MASKED)
    exponents = jnp.exp(scores - jnp.max(scores, axis=-1, keepdims=True))
    return exponents * (1.0 / jnp.sum(exponents, axis=-1, keepdims=True))


def attend_kernel(edge_ref, query_ref, key_ref, value_ref, mix_ref, *, block, blocks):
    step = pl.program_id(1)
    for index in range(blocks):

        @pl.when(step == index)
        def _(index=index):
            span = (index + 1) * block
            allowed = attend_mask(edge_ref[0], index * block, block, span)
            mixed = []
            for head in range(2):
                cut = slice(head * HEAD, (head + 1) * HEAD)
                soft = soft_rows(query_ref[:, cut], key_ref[:span, cut], allowed)
                mixed.append(
                    jnp.dot(
                        soft.astype(jnp.bfloat16),
                        value_ref[:span, cut],
                        preferred_element_type=jnp.float32,
                    )
                )
            mix_ref[...] = jnp.concatenate(mixed, axis=-1).astype(mix_ref.dtype)


def attend_back_kernel(
    edge_ref,
    query_ref,
    key_ref,
    value_ref,
    back_ref,
    query_back_ref,
    key_back_ref,
    value_back_ref,
    *,
    block,
    blocks,
    score_scale,
):
    step = pl.program_id(1)

    @pl.when(step == 0)
    def _():
        key_back_ref[...] = jnp.zeros_like(key_back_ref)
        value_back_ref[...] = jnp.zeros_like(value_back_ref)

    for index in range(blocks):

        @pl.when(step == index)
        def _(index=index):
            span = (index + 1) * block
            allowed = attend_mask(edge_ref[0], index * block, block, span)
            query_parts, key_parts, value_parts = [], [], []
            for head in range(2):
                cut = slice(head * HEAD, (head + 1) * HEAD)
                query, key = query_ref[:, cut], key_ref[:span, cut]
                back = back_ref[:, cut]
                soft = soft_rows(query, key, allowed)
                soft_back = contract_cols(back, value_ref[:span, cut])
                delta = jnp.sum(soft * soft_back, axis=-1, keepdims=True)
                score_back = (soft * (soft_back - delta)).astype(jnp.bfloat16)
                query_parts.append(
                    jnp.dot(score_back, key, preferred_element_type=jnp.float32) * score_scale
                )
                key_parts.append(contract_rows(score_back, query))
                value_parts.append(contract_rows(soft.astype(jnp.bfloat16), back))
            query_back_ref[...] = jnp.concatenate(query_parts, axis=-1)
            key_back_ref[:span, :] += jnp.concatenate(key_parts, axis=-1)
            value_back_ref[:span, :] += jnp.concatenate(value_parts, axis=-1)


def attend_specs(length, block):
    rows = pl.BlockSpec((block, 2 * HEAD), lambda pair, step: (step, pair))
    whole = pl.BlockSpec((length, 2 * HEAD), lambda pair, step: (0, pair))
    edge = pl.BlockSpec(memory_space=pltpu.SMEM)
    return edge, rows, whole


def attend_cost(length, width, products):
    return pl.CostEstimate(
        flops=8 * products * length * length * width,
        transcendentals=length * length * width // HEAD,
        bytes_accessed=(2 * products + 4) * length * width,
    )


def attend(edge, queries, keys, values):
    length, width = queries.shape
    block = 256
    blocks = length // block
    scalar, rows, whole = attend_specs(length, block)

    def body(*refs):
        attend_kernel(*refs, block=block, blocks=blocks)

    return pl.pallas_call(
        body,
        name="attend",
        grid=(width // (2 * HEAD), blocks),
        in_specs=[scalar, rows, whole, whole],
        out_specs=rows,
        out_shape=jax.ShapeDtypeStruct((length, width), jnp.bfloat16),
        cost_estimate=attend_cost(length, width, 2),
    )(edge, queries, keys, values)


def attend_back(edge, queries, keys, values, back, score_scale):
    length, width = queries.shape
    block = 256
    blocks = length // block
    scalar, rows, whole = attend_specs(length, block)

    def body(*refs):
        attend_back_kernel(*refs, block=block, blocks=blocks, score_scale=score_scale)

    shape = jax.ShapeDtypeStruct((length, width), jnp.float32)
    return pl.pallas_call(
        body,
        name="attend_back",
        grid=(width // (2 * HEAD), blocks),
        in_specs=[scalar, rows, whole, whole, rows],
        out_specs=(rows, whole, whole),
        out_shape=(shape, shape, shape),
        cost_estimate=attend_cost(length, width, 5),
    )(edge, queries, keys, values, back)


def turn(values, cosine, sine_table):
    half = HEAD // 2
    lane = lax.broadcasted_iota(jnp.int32, values.shape, 1) % HEAD
    turned = jnp.where(
        lane < half, -jnp.roll(values, -half, axis=1), jnp.roll(values, half, axis=1)
    )
    return values * cosine + turned * sine_table


def local_columns(
    block_input,
    positions,
    segments,
    cotangent,
    attn_gain,
    query_weight,
    key_weight,
    value_weight,
    out_weight,
    mlp_gain,
    gate_weight,
    up_weight,
    down_weight,
):
    f32, bf16 = jnp.float32, jnp.bfloat16
    score_scale = HEAD ** (-0.5)
    length = segments.shape[1]
    rows = query_weight.shape[0]
    head_width = KV_HEADS * HEAD
    inputs = block_input[0].astype(f32)
    out_back = cotangent[0]
    gain_one = attn_gain.astype(f32)[:, None]
    gain_two = mlp_gain.astype(f32)[:, None]

    def fold(weight, gain):
        return (weight.astype(f32) * gain).astype(bf16)

    inputs_all = gather_ctx(block_input[0])
    key_value = jnp.stack([fold(key_weight, gain_one), fold(value_weight, gain_one)])
    attn_pieces = jnp.concatenate(
        [
            head_slices(fold(query_weight, gain_one)),
            jnp.tile(key_value, (4, 1, 1)),
        ],
        axis=2,
    )
    main, tail = ff_split(gate_weight.shape[1])
    both = 2 * (main + tail)
    gate_main, gate_tail = ff_slices(fold(gate_weight, gain_two))
    up_main, up_tail = ff_slices(fold(up_weight, gain_two))
    down_pieces = jnp.concatenate(ff_slices(down_weight), axis=2)
    gate_up_pieces = jnp.concatenate([gate_main, up_main, gate_tail, up_tail], axis=2)
    attn_own = exchange_ctx(attn_pieces).reshape(8 * rows, 2 * head_width)
    edge = jnp.sum((segments[0] == 0).astype(jnp.int32))
    token = jnp.arange(length, dtype=jnp.int32)
    position = jnp.where(token < edge, token + (length - edge), token - edge)
    cosine, sine_table = rope_tables(position, HEAD)
    cosine = jnp.tile(cosine, (1, KV_HEADS))
    sine_table = jnp.tile(sine_table, (1, KV_HEADS))
    edge = edge[None]
    attn_own, down_pieces, gate_up_pieces, cosine, sine_table = tie(
        attn_own, down_pieces, gate_up_pieces, cosine, sine_table
    )
    attn_cols = gather_seq(attn_own)
    core = lax.axis_index("ctx") % 2
    other_cols = swap_cores(attn_cols[:, head_width:])
    out_rows = gather_seq(out_weight)
    down_own = exchange_ctx(down_pieces).reshape(8 * rows, -1)
    down_own, gate_up_pieces = tie(down_own, gate_up_pieces)
    gate_up_own = exchange_ctx(gate_up_pieces).reshape(8 * rows, -1)

    wide = inputs_all.astype(f32)
    shaped_all = (wide * rms_scale(wide)).astype(bf16)
    raw = jnp.dot(shaped_all, attn_cols, preferred_element_type=f32)
    raw_other = jnp.dot(shaped_all, other_cols, preferred_element_type=f32)
    raw, raw_other, down_own = tie(raw, raw_other, down_own)
    raw_own = raw[:, head_width:]
    down_near = gather_seq_near(down_own)
    queries = turn(raw[:, :head_width], cosine, sine_table).astype(bf16)
    keys = turn(jnp.where(core == 0, raw_own, raw_other), cosine, sine_table).astype(bf16)
    values = jnp.where(core == 0, raw_other, raw_own).astype(bf16)
    queries = queries * jnp.asarray(score_scale, bf16)
    attn_low = attend(edge, queries, keys, values)
    attn_low, out_rows, back_late, gate_up_own, *down_near = tie(
        attn_low, out_rows, out_back, gate_up_own, *down_near
    )
    gate_up_near = gather_seq_near(gate_up_own)
    down_cols = gather_seq_far(down_own, *down_near)
    mixed = jnp.dot(attn_low, out_rows, preferred_element_type=f32).astype(bf16)
    mixed_own = reduce_ctx(mixed)
    mixed_own, down_cols, *gate_up_near = tie(mixed_own, down_cols, *gate_up_near)
    residual = inputs + mixed_own.astype(f32)
    scale_two = rms_scale(residual)
    shaped_two = residual * scale_two
    shaped_low = shaped_two.astype(bf16)
    normed_all = gather_ctx(shaped_low)
    shaped_two, back_late = tie(shaped_two, back_late)
    gate_up = gather_seq_far(gate_up_own, *gate_up_near)
    back_all = gather_ctx(back_late)
    proj = jnp.dot(normed_all, gate_up, preferred_element_type=f32)

    def halves(left_tail, right_tail, left, right):
        return jnp.concatenate([left, left_tail], axis=1), jnp.concatenate([right, right_tail], axis=1)

    gate_proj, up_proj = halves(
        proj[:, 2 * main : 2 * main + tail],
        proj[:, 2 * main + tail :],
        proj[:, :main],
        proj[:, main : 2 * main],
    )
    sigmoid_gate = jax.nn.sigmoid(gate_proj)
    silu_gate = gate_proj * sigmoid_gate
    hidden = (silu_gate * up_proj).astype(bf16)
    mixed_out = contract_cols(hidden, down_cols).astype(bf16)
    mixed_out, back_all = tie(mixed_out, back_all)
    out_own = reduce_ctx(mixed_out)
    hidden_back = jnp.dot(back_all, down_cols, preferred_element_type=f32)
    gate_back = (
        hidden_back * up_proj * sigmoid_gate * (1.0 + gate_proj * (1.0 - sigmoid_gate))
    ).astype(bf16)
    upper_back = (hidden_back * silu_gate).astype(bf16)
    gate_up_back = jnp.concatenate(
        [gate_back[:, :main], upper_back[:, :main], gate_back[:, main:], upper_back[:, main:]],
        axis=1,
    )
    weighted = reduce_ctx(contract_cols(gate_up_back, gate_up).astype(bf16))
    gate_up_grad = contract_rows(normed_all, gate_up_back).astype(bf16)
    down_grad = contract_rows(back_all, hidden).astype(bf16)
    mlp_grads = [gate_up_grad, down_grad]
    out_own, *mlp_parts = tie(out_own, *seq_parts(mlp_grads))
    mlp_near = send_parts(mlp_parts)
    weighted, *mlp_near = tie(weighted, *mlp_near)
    weighted = weighted.astype(f32)
    residual_back = out_back.astype(f32) + scale_two * (
        weighted - shaped_two * jnp.mean(weighted * shaped_two, axis=-1, keepdims=True)
    )
    residual_low = residual_back.astype(bf16)
    low_all = gather_ctx(residual_low)
    residual_back, *mlp_near = tie(residual_back, *mlp_near)
    mlp_sums = far_sums(mlp_grads, *mlp_near[:2])
    mlp_grads_own = reduce_seq_far(mlp_grads, mlp_sums, *mlp_near[2:])
    mlp_grad = exchange_ctx(mlp_grads_own.reshape(8, rows, -1))
    attn_back = contract_cols(low_all, out_rows).astype(bf16)
    query_back, key_back, value_back = attend_back(
        edge, queries, keys, values, attn_back, score_scale
    )
    key_low = turn(key_back, cosine, -sine_table).astype(bf16)
    value_low = value_back.astype(bf16)
    other_back = jnp.where(core == 0, value_low, key_low)
    other_back, mlp_grad = tie(other_back, mlp_grad)
    other_part = contract_rows(shaped_all, other_back).astype(bf16)
    heads_back = jnp.concatenate(
        [
            turn(query_back, cosine, -sine_table).astype(bf16),
            jnp.where(core == 0, key_low, value_low),
        ],
        axis=1,
    )
    heads_back, other_part = tie(heads_back, other_part)
    other_part = swap_cores(other_part)
    weighted_part = contract_cols(
        jnp.concatenate([heads_back, other_back], axis=1),
        jnp.concatenate([attn_cols, other_cols], axis=1),
    ).astype(bf16)
    weighted_part, low_all = tie(weighted_part, low_all)
    weighted_one = reduce_ctx(weighted_part).astype(f32)
    attn_part = contract_rows(shaped_all, heads_back)
    own_part = attn_part[:, head_width:] + other_part.astype(f32)
    attn_grad_own = reduce_seq(
        [jnp.concatenate([attn_part[:, :head_width].astype(bf16), own_part.astype(bf16)], axis=1)]
    )
    out_grad = reduce_seq([contract_rows(attn_low, low_all).astype(bf16)]).astype(f32)
    attn_grad_own, mlp_grad = tie(attn_grad_own, mlp_grad)
    mlp_grad = mlp_grad.astype(f32)
    attn_grad = exchange_ctx(attn_grad_own.reshape(8, rows, -1))

    scale_one = rms_scale(inputs)
    shaped_one = inputs * scale_one
    input_grad = residual_back + scale_one * (
        weighted_one - shaped_one * jnp.mean(weighted_one * shaped_one, axis=-1, keepdims=True)
    )
    block_output = (residual + out_own.astype(f32)).astype(bf16)
    gate_rows = ff_rows(mlp_grad[:, :, :main], mlp_grad[:, :, 2 * main : 2 * main + tail])
    up_rows = ff_rows(mlp_grad[:, :, main : 2 * main], mlp_grad[:, :, 2 * main + tail : both])
    down_grad = ff_rows(mlp_grad[:, :, both : both + main], mlp_grad[:, :, both + main :])
    attn_grad, out_grad, gate_rows, up_rows, down_grad = tie(
        attn_grad, out_grad, gate_rows, up_rows, down_grad
    )
    attn_grad = attn_grad.astype(f32)
    query_rows = from_head_slices(attn_grad[:, :, :head_width])
    pair_rows = jnp.sum(attn_grad[:, :, head_width:].reshape(4, 2, rows, head_width), axis=0)
    key_rows, value_rows = pair_rows[0], pair_rows[1]

    def row_sum(weight, grad):
        return jnp.sum(weight.astype(f32) * grad, axis=1)

    attn_gain_grad = (
        row_sum(query_weight, query_rows)
        + row_sum(key_weight, key_rows)
        + row_sum(value_weight, value_rows)
    )
    mlp_gain_grad = row_sum(gate_weight, gate_rows) + row_sum(up_weight, up_rows)
    return (
        block_output[None],
        input_grad[None],
        attn_gain_grad,
        query_rows * gain_one,
        key_rows * gain_one,
        value_rows * gain_one,
        out_grad,
        mlp_gain_grad,
        gate_rows * gain_two,
        up_rows * gain_two,
        down_grad,
    )


def solution(mesh):
    placed = (
        P("seq", "ctx", None),
        P("seq", "ctx"),
        P("seq", None),
        P("seq", "ctx", None),
        P(("seq", "ctx")),
        P(("seq", "ctx"), None),
        P(("seq", "ctx"), None),
        P(("seq", "ctx"), None),
        P(("seq", "ctx"), None),
        P(("seq", "ctx")),
        P(("seq", "ctx"), None),
        P(("seq", "ctx"), None),
        P(("seq", "ctx"), None),
    )
    seq_count, ctx_count = mesh.shape["seq"], mesh.shape["ctx"]

    def run(*args):
        width = args[0].shape[2]
        fits = (
            seq_count == KV_HEADS == 4
            and ctx_count == HEADS // KV_HEADS == 8
            and width == seq_count * ctx_count * HEAD
        )
        return jax.shard_map(
            local_columns if fits else local_rows,
            mesh=mesh,
            in_specs=placed,
            out_specs=(
                P("seq", "ctx", None),
                P("seq", "ctx", None),
                P(("seq", "ctx")),
                P(("seq", "ctx"), None),
                P(("seq", "ctx"), None),
                P(("seq", "ctx"), None),
                P(("seq", "ctx"), None),
                P(("seq", "ctx")),
                P(("seq", "ctx"), None),
                P(("seq", "ctx"), None),
                P(("seq", "ctx"), None),
            ),
            check_vma=False,
        )(*args)

    return run
```

```python
import jax
import jax.numpy as jnp
from jax import lax
from jax.experimental import pallas as pl
from jax.experimental.pallas import tpu as pltpu
from jax.sharding import PartitionSpec as P

HEADS = 32
KV_HEADS = 4
HEAD = 64


EPSILON = 1e-05
MASKED = -1e30


def rope_tables(position, head_size):
    half_size = head_size // 2
    inverse = 1.0 / 10000.0 ** (jnp.arange(half_size, dtype=jnp.float32) * 2.0 / head_size)
    angles = position.astype(jnp.float32)[:, None] * inverse[None, :]
    cosine = jnp.cos(angles)
    sine_table = jnp.sin(angles)
    return (jnp.concatenate([cosine, cosine], -1), jnp.concatenate([sine_table, sine_table], -1))


def rotate(values, cosine, sine_table):
    half_size = values.shape[-1] // 2
    turned = jnp.concatenate([-values[..., half_size:], values[..., :half_size]], -1)
    return values * cosine[:, None, :] + turned * sine_table[:, None, :]


def rms_scale(inputs):
    return lax.rsqrt(jnp.mean(inputs * inputs, axis=-1, keepdims=True) + EPSILON)


def norm_back(inputs, row_scale, gain, upstream):
    shaped = inputs * row_scale
    weighted = upstream * gain
    gain_term = jnp.sum(upstream * shaped, axis=0)
    return (
        row_scale * (weighted - shaped * jnp.mean(weighted * shaped, axis=-1, keepdims=True)),
        gain_term,
    )


def contract_rows(left, right):
    return lax.dot_general(
        left, right, (((0,), (0,)), ((), ())), preferred_element_type=jnp.float32
    )


def contract_cols(left, right):
    return lax.dot_general(
        left, right, (((1,), (1,)), ((), ())), preferred_element_type=jnp.float32
    )


def local_rows(
    block_input,
    positions,
    segments,
    cotangent,
    attn_gain,
    query_weight,
    key_weight,
    value_weight,
    out_weight,
    mlp_gain,
    gate_weight,
    up_weight,
    down_weight,
):
    row_count = block_input.shape[1]
    group_size = HEADS // KV_HEADS
    score_scale = HEAD ** (-0.5)
    inputs = block_input[0].astype(jnp.float32)
    seg_all = segments[0]
    length = seg_all.shape[0]
    block_size = min(512, length)
    block_count = length // block_size
    first_row = lax.axis_index("ctx") * row_count
    query_index = first_row + jnp.arange(row_count, dtype=jnp.int32)
    seg_rows = lax.dynamic_slice_in_dim(seg_all, first_row, row_count)
    cosine, sine_table = rope_tables(positions[0], HEAD)
    starts = jnp.arange(block_count, dtype=jnp.int32) * block_size
    seg_blocks = seg_all.reshape(block_count, block_size)

    def key_mask(seg_block, block_start):
        key_index = block_start + jnp.arange(block_size, dtype=jnp.int32)
        return (seg_rows[:, None] == seg_block[None, :]) & (
            key_index[None, :] <= query_index[:, None]
        )

    def guarded(compute, running):
        result = compute(running)
        return result

    attn_params = (
        lax.all_gather(attn_gain, ("seq", "ctx"), axis=0, tiled=True),
        lax.all_gather(query_weight, ("seq", "ctx"), axis=0, tiled=True),
        lax.all_gather(key_weight, ("seq", "ctx"), axis=0, tiled=True),
        lax.all_gather(value_weight, ("seq", "ctx"), axis=0, tiled=True),
        lax.all_gather(out_weight, ("seq", "ctx"), axis=0, tiled=True),
    )
    gain_one = attn_params[0].astype(jnp.float32)
    scale_one = rms_scale(inputs)
    normed1 = (inputs * scale_one * gain_one).astype(jnp.bfloat16)
    query_raw = jnp.dot(normed1, attn_params[1], preferred_element_type=jnp.float32)
    key_raw = jnp.dot(normed1, attn_params[2], preferred_element_type=jnp.float32)
    value_raw = jnp.dot(normed1, attn_params[3], preferred_element_type=jnp.float32)
    queries = rotate(query_raw.reshape(row_count, HEADS, HEAD), cosine, sine_table).astype(
        jnp.bfloat16
    )
    keys_local = (
        rotate(key_raw.reshape(row_count, KV_HEADS, HEAD), cosine, sine_table)
        .astype(jnp.bfloat16)
        .reshape(row_count, KV_HEADS * HEAD)
    )
    values_local = value_raw.astype(jnp.bfloat16)
    keys_all, values_all = (
        lax.all_gather(keys_local, "ctx", axis=0, tiled=True),
        lax.all_gather(values_local, "ctx", axis=0, tiled=True),
    )
    key_blocks = keys_all.reshape(block_count, block_size, KV_HEADS, HEAD)
    value_blocks = values_all.reshape(block_count, block_size, KV_HEADS, HEAD)
    query_group = queries.reshape(row_count, KV_HEADS, group_size, HEAD)

    def block_scores(key_block, allowed):
        scores = (
            jnp.einsum("tkgd,jkd->kgtj", query_group, key_block, preferred_element_type=jnp.float32)
            * score_scale
        )
        return jnp.where(allowed[None, None], scores, MASKED)

    def max_step(carry, pieces):
        key_block, seg_block, block_start = pieces
        allowed = key_mask(seg_block, block_start)

        def compute(running):
            run_max, run_sum = running
            scores = block_scores(key_block, allowed)
            new_max = jnp.maximum(run_max, jnp.max(scores, axis=-1))
            exponents = jnp.where(allowed[None, None], jnp.exp(scores - new_max[..., None]), 0.0)
            return (new_max, run_sum * jnp.exp(run_max - new_max) + jnp.sum(exponents, axis=-1))

        return (guarded(compute, carry), None)

    start_max = jnp.full((KV_HEADS, group_size, row_count), MASKED, jnp.float32)
    start_sum = jnp.zeros((KV_HEADS, group_size, row_count), jnp.float32)
    (run_max, run_sum), unused = lax.scan(
        max_step, (start_max, start_sum), (key_blocks, seg_blocks, starts)
    )
    log_sum = run_max + jnp.log(run_sum)

    def block_soft(key_block, allowed):
        scores = block_scores(key_block, allowed)
        return jnp.where(allowed[None, None], jnp.exp(scores - log_sum[..., None]), 0.0)

    def value_step(carry, pieces):
        key_block, value_block, seg_block, block_start = pieces
        allowed = key_mask(seg_block, block_start)

        def compute(running):
            acc_out, acc_fix = running
            soft_weights = block_soft(key_block, allowed)
            rounded = soft_weights.astype(jnp.bfloat16)
            leftover = (soft_weights - rounded.astype(jnp.float32)).astype(jnp.bfloat16)
            acc_out = acc_out + jnp.einsum(
                "kgtj,jkd->tkgd", rounded, value_block, preferred_element_type=jnp.float32
            )
            acc_fix = acc_fix + jnp.einsum(
                "kgtj,jkd->tkgd", leftover, value_block, preferred_element_type=jnp.float32
            )
            return (acc_out, acc_fix)

        return (guarded(compute, carry), None)

    zero_mix = jnp.zeros((row_count, KV_HEADS, group_size, HEAD), jnp.float32)
    (acc_out, acc_fix), unused = lax.scan(
        value_step, (zero_mix, zero_mix), (key_blocks, value_blocks, seg_blocks, starts)
    )
    attn_low = acc_out.reshape(row_count, HEADS * HEAD).astype(jnp.bfloat16)
    full_mix = acc_out + acc_fix
    residual = inputs + jnp.dot(attn_low, attn_params[4], preferred_element_type=jnp.float32)
    mlp_params = (
        lax.all_gather(mlp_gain, ("seq", "ctx"), axis=0, tiled=True),
        lax.all_gather(gate_weight, ("seq", "ctx"), axis=0, tiled=True),
        lax.all_gather(up_weight, ("seq", "ctx"), axis=0, tiled=True),
        lax.all_gather(down_weight, ("seq", "ctx"), axis=0, tiled=True),
    )
    gain_two = mlp_params[0].astype(jnp.float32)
    scale_two = rms_scale(residual)
    normed2 = (residual * scale_two * gain_two).astype(jnp.bfloat16)
    gate_proj = jnp.dot(normed2, mlp_params[1], preferred_element_type=jnp.float32)
    up_proj = jnp.dot(normed2, mlp_params[2], preferred_element_type=jnp.float32)
    sigmoid_gate = jax.nn.sigmoid(gate_proj)
    silu_gate = gate_proj * sigmoid_gate
    hidden = (silu_gate * up_proj).astype(jnp.bfloat16)
    block_output = (residual + contract_cols(hidden, mlp_params[3])).astype(jnp.bfloat16)
    out_back = cotangent[0]
    out_float = out_back.astype(jnp.float32)
    mlp_again = (
        lax.all_gather(mlp_gain, ("seq", "ctx"), axis=0, tiled=True),
        lax.all_gather(gate_weight, ("seq", "ctx"), axis=0, tiled=True),
        lax.all_gather(up_weight, ("seq", "ctx"), axis=0, tiled=True),
        lax.all_gather(down_weight, ("seq", "ctx"), axis=0, tiled=True),
    )
    down_grad = lax.psum_scatter(
        contract_rows(out_back, hidden), ("seq", "ctx"), scatter_dimension=0, tiled=True
    )
    hidden_back = jnp.dot(out_back, mlp_again[3], preferred_element_type=jnp.float32)
    gate_back = (
        hidden_back * up_proj * sigmoid_gate * (1.0 + gate_proj * (1.0 - sigmoid_gate))
    ).astype(jnp.bfloat16)
    upper_back = (hidden_back * silu_gate).astype(jnp.bfloat16)
    gate_full_grad = contract_rows(normed2, gate_back)
    up_full_grad = contract_rows(normed2, upper_back)
    normed2_back = contract_cols(gate_back, mlp_again[1]) + contract_cols(upper_back, mlp_again[2])
    residual_norm, mlp_gain_term = norm_back(
        residual, scale_two, mlp_again[0].astype(jnp.float32), normed2_back
    )
    mlp_sums = (
        lax.psum_scatter(mlp_gain_term, ("seq", "ctx"), scatter_dimension=0, tiled=True),
        lax.psum_scatter(gate_full_grad, ("seq", "ctx"), scatter_dimension=0, tiled=True),
        lax.psum_scatter(up_full_grad, ("seq", "ctx"), scatter_dimension=0, tiled=True),
    )
    residual_back = out_float + residual_norm
    attn_again = (
        lax.all_gather(attn_gain, ("seq", "ctx"), axis=0, tiled=True),
        lax.all_gather(query_weight, ("seq", "ctx"), axis=0, tiled=True),
        lax.all_gather(key_weight, ("seq", "ctx"), axis=0, tiled=True),
        lax.all_gather(value_weight, ("seq", "ctx"), axis=0, tiled=True),
        lax.all_gather(out_weight, ("seq", "ctx"), axis=0, tiled=True),
    )
    residual_low = residual_back.astype(jnp.bfloat16)
    out_full_grad = contract_rows(attn_low, residual_low)
    attn_back = contract_cols(residual_low, attn_again[4]).astype(jnp.bfloat16)
    grad_mix = attn_back.reshape(row_count, KV_HEADS, group_size, HEAD)
    delta_rows = jnp.transpose(jnp.sum(grad_mix.astype(jnp.float32) * full_mix, axis=-1), (1, 2, 0))

    def grad_step(carry, pieces):
        key_block, value_block, seg_block, block_start = pieces
        allowed = key_mask(seg_block, block_start)

        def compute(acc_query):
            soft_weights = block_soft(key_block, allowed)
            rounded = soft_weights.astype(jnp.bfloat16)
            value_part = jnp.einsum(
                "kgtj,tkgd->jkd", rounded, grad_mix, preferred_element_type=jnp.float32
            )
            soft_back = jnp.einsum(
                "tkgd,jkd->kgtj", grad_mix, value_block, preferred_element_type=jnp.float32
            )
            score_back = (soft_weights * (soft_back - delta_rows[..., None])).astype(jnp.bfloat16)
            acc_query = acc_query + jnp.einsum(
                "kgtj,jkd->tkgd", score_back, key_block, preferred_element_type=jnp.float32
            )
            key_part = jnp.einsum(
                "kgtj,tkgd->jkd", score_back, query_group, preferred_element_type=jnp.float32
            )
            return (acc_query, (key_part, value_part))

        return guarded(compute, carry)

    acc_query, (key_parts, value_parts) = lax.scan(
        grad_step, zero_mix, (key_blocks, value_blocks, seg_blocks, starts)
    )
    key_sums, value_sums = (
        lax.psum_scatter(
            key_parts.reshape(length, KV_HEADS * HEAD).astype(jnp.bfloat16),
            "ctx",
            scatter_dimension=0,
            tiled=True,
        ).astype(jnp.float32),
        lax.psum_scatter(
            value_parts.reshape(length, KV_HEADS * HEAD).astype(jnp.bfloat16),
            "ctx",
            scatter_dimension=0,
            tiled=True,
        ).astype(jnp.float32),
    )
    query_low = (
        rotate((acc_query * score_scale).reshape(row_count, HEADS, HEAD), cosine, -sine_table)
        .astype(jnp.bfloat16)
        .reshape(row_count, HEADS * HEAD)
    )
    key_low = (
        rotate((key_sums * score_scale).reshape(row_count, KV_HEADS, HEAD), cosine, -sine_table)
        .astype(jnp.bfloat16)
        .reshape(row_count, KV_HEADS * HEAD)
    )
    value_low = value_sums.astype(jnp.bfloat16)
    query_full_grad = contract_rows(normed1, query_low)
    key_full_grad = contract_rows(normed1, key_low)
    value_full_grad = contract_rows(normed1, value_low)
    normed1_back = (
        contract_cols(query_low, attn_again[1])
        + contract_cols(key_low, attn_again[2])
        + contract_cols(value_low, attn_again[3])
    )
    input_norm, attn_gain_term = norm_back(
        inputs, scale_one, attn_again[0].astype(jnp.float32), normed1_back
    )
    attn_sums = (
        lax.psum_scatter(attn_gain_term, ("seq", "ctx"), scatter_dimension=0, tiled=True),
        lax.psum_scatter(query_full_grad, ("seq", "ctx"), scatter_dimension=0, tiled=True),
        lax.psum_scatter(key_full_grad, ("seq", "ctx"), scatter_dimension=0, tiled=True),
        lax.psum_scatter(value_full_grad, ("seq", "ctx"), scatter_dimension=0, tiled=True),
        lax.psum_scatter(out_full_grad, ("seq", "ctx"), scatter_dimension=0, tiled=True),
    )
    input_grad = residual_back + input_norm
    return (
        block_output[None],
        input_grad[None],
        attn_sums[0],
        attn_sums[1],
        attn_sums[2],
        attn_sums[3],
        attn_sums[4],
        mlp_sums[0],
        mlp_sums[1],
        mlp_sums[2],
        down_grad,
    )


SEQ_X = [(0, 1), (1, 0), (2, 3), (3, 2)]
SEQ_Y = [(0, 2), (2, 0), (1, 3), (3, 1)]


def gather_ctx(block):
    return lax.all_gather(block, "ctx", axis=0, tiled=True)


def reduce_ctx(partial):
    return lax.psum_scatter(partial, "ctx", scatter_dimension=0, tiled=True)


def exchange_ctx(pieces):
    return lax.all_to_all(pieces, "ctx", 0, 0, tiled=True)


def gather_seq_near(block):
    return lax.ppermute(block, "seq", SEQ_X), lax.ppermute(block, "seq", SEQ_Y)


def gather_seq_far(block, from_x, from_y):
    rows, width = block.shape
    half = rows // 2
    mine = lax.axis_index("seq")
    far_top = lax.ppermute(from_x[:half], "seq", SEQ_Y)
    far_low = lax.ppermute(from_y[half:], "seq", SEQ_X)
    whole = jnp.zeros((4 * rows, width), block.dtype)
    for piece, start in (
        (block, mine * rows),
        (from_x, (mine ^ 1) * rows),
        (from_y, (mine ^ 2) * rows),
        (far_top, (mine ^ 3) * rows),
        (far_low, (mine ^ 3) * rows + half),
    ):
        whole = lax.dynamic_update_slice_in_dim(whole, piece, start, 0)
    return whole


def gather_seq(block):
    return gather_seq_far(block, *gather_seq_near(block))


def seq_part(partials, other, low):
    rows = partials[0].shape[0] // 4
    half = rows // 2
    start = (lax.axis_index("seq") ^ other) * rows + (half if low else 0)
    return jnp.concatenate(
        [lax.dynamic_slice_in_dim(partial, start, half, 0) for partial in partials], axis=1
    )


def seq_parts(partials):
    return (
        seq_part(partials, 3, False),
        seq_part(partials, 3, True),
        seq_part(partials, 1, False),
        seq_part(partials, 2, True),
    )


def send_parts(parts):
    return tuple(
        lax.ppermute(part, "seq", axis) for part, axis in zip(parts, (SEQ_X, SEQ_Y) * 2)
    )


def reduce_seq_near(partials):
    return send_parts(seq_parts(partials))


def add_wide(*terms):
    total = terms[0].astype(jnp.float32)
    for term in terms[1:]:
        total = total + term.astype(jnp.float32)
    return total


def far_sums(partials, top_far, low_far):
    return (
        add_wide(seq_part(partials, 2, False), top_far).astype(jnp.bfloat16),
        add_wide(seq_part(partials, 1, True), low_far).astype(jnp.bfloat16),
    )


def reduce_seq_far(partials, sums, top_near, low_near):
    top_send, low_send = sums
    top_last = lax.ppermute(top_send, "seq", SEQ_Y)
    low_last = lax.ppermute(low_send, "seq", SEQ_X)
    return jnp.concatenate(
        [
            add_wide(seq_part(partials, 0, False), top_near, top_last),
            add_wide(seq_part(partials, 0, True), low_near, low_last),
        ],
        axis=0,
    ).astype(jnp.bfloat16)


def reduce_seq(partials):
    top_far, low_far, *nears = reduce_seq_near(partials)
    return reduce_seq_far(partials, far_sums(partials, top_far, low_far), *nears)


def tie(*values):
    return lax.optimization_barrier(values)


def swap_cores(block):
    return lax.ppermute(block, "ctx", [(device, device ^ 1) for device in range(8)])


def ff_split(width):
    main = width // 8 // 128 * 128
    return main, width // 8 - main


def ff_slices(weight):
    rows, width = weight.shape
    main, tail = ff_split(width)
    return (
        jnp.transpose(weight[:, : 8 * main].reshape(rows, 8, main), (1, 0, 2)),
        jnp.transpose(weight[:, 8 * main :].reshape(rows, 8, tail), (1, 0, 2)),
    )


def ff_rows(main, tail):
    count, rows, width = main.shape
    return jnp.concatenate(
        [
            jnp.transpose(main, (1, 0, 2)).reshape(rows, count * width),
            jnp.transpose(tail, (1, 0, 2)).reshape(rows, count * tail.shape[2]),
        ],
        axis=1,
    )


def head_slices(weight):
    rows = weight.shape[0]
    split = weight.reshape(rows, KV_HEADS, 8, HEAD)
    return jnp.transpose(split, (2, 0, 1, 3)).reshape(8, rows, KV_HEADS * HEAD)


def from_head_slices(pieces):
    rows = pieces.shape[1]
    split = pieces.reshape(8, rows, KV_HEADS, HEAD)
    return jnp.transpose(split, (1, 2, 0, 3)).reshape(rows, HEADS * HEAD)


def attend_mask(edge, first_row, block, span):
    row = first_row + lax.broadcasted_iota(jnp.int32, (block, span), 0)
    column = lax.broadcasted_iota(jnp.int32, (block, span), 1)
    return (column <= row) & (column >= jnp.where(row >= edge, edge, 0))


def soft_rows(query, key, allowed):
    scores = lax.dot_general(
        query, key, (((1,), (1,)), ((), ())), preferred_element_type=jnp.float32
    )
    scores = jnp.where(allowed, scores, MASKED)
    exponents = jnp.exp(scores - jnp.max(scores, axis=-1, keepdims=True))
    return exponents * (1.0 / jnp.sum(exponents, axis=-1, keepdims=True))


def attend_kernel(edge_ref, query_ref, key_ref, value_ref, mix_ref, *, block, blocks):
    step = pl.program_id(1)
    for index in range(blocks):

        @pl.when(step == index)
        def _(index=index):
            span = (index + 1) * block
            allowed = attend_mask(edge_ref[0], index * block, block, span)
            mixed = []
            for head in range(2):
                cut = slice(head * HEAD, (head + 1) * HEAD)
                soft = soft_rows(query_ref[:, cut], key_ref[:span, cut], allowed)
                mixed.append(
                    jnp.dot(
                        soft.astype(jnp.bfloat16),
                        value_ref[:span, cut],
                        preferred_element_type=jnp.float32,
                    )
                )
            mix_ref[...] = jnp.concatenate(mixed, axis=-1).astype(mix_ref.dtype)


def attend_back_kernel(
    edge_ref,
    query_ref,
    key_ref,
    value_ref,
    back_ref,
    query_back_ref,
    key_back_ref,
    value_back_ref,
    *,
    block,
    blocks,
    score_scale,
):
    step = pl.program_id(1)

    @pl.when(step == 0)
    def _():
        key_back_ref[...] = jnp.zeros_like(key_back_ref)
        value_back_ref[...] = jnp.zeros_like(value_back_ref)

    for index in range(blocks):

        @pl.when(step == index)
        def _(index=index):
            span = (index + 1) * block
            allowed = attend_mask(edge_ref[0], index * block, block, span)
            query_parts, key_parts, value_parts = [], [], []
            for head in range(2):
                cut = slice(head * HEAD, (head + 1) * HEAD)
                query, key = query_ref[:, cut], key_ref[:span, cut]
                back = back_ref[:, cut]
                soft = soft_rows(query, key, allowed)
                soft_back = contract_cols(back, value_ref[:span, cut])
                delta = jnp.sum(soft * soft_back, axis=-1, keepdims=True)
                score_back = (soft * (soft_back - delta)).astype(jnp.bfloat16)
                query_parts.append(
                    jnp.dot(score_back, key, preferred_element_type=jnp.float32) * score_scale
                )
                key_parts.append(contract_rows(score_back, query))
                value_parts.append(contract_rows(soft.astype(jnp.bfloat16), back))
            query_back_ref[...] = jnp.concatenate(query_parts, axis=-1)
            key_back_ref[:span, :] += jnp.concatenate(key_parts, axis=-1)
            value_back_ref[:span, :] += jnp.concatenate(value_parts, axis=-1)


def attend_specs(length, block):
    rows = pl.BlockSpec((block, 2 * HEAD), lambda pair, step: (step, pair))
    whole = pl.BlockSpec((length, 2 * HEAD), lambda pair, step: (0, pair))
    edge = pl.BlockSpec(memory_space=pltpu.SMEM)
    return edge, rows, whole


def attend_cost(length, width, products):
    return pl.CostEstimate(
        flops=8 * products * length * length * width,
        transcendentals=length * length * width // HEAD,
        bytes_accessed=(2 * products + 4) * length * width,
    )


def attend(edge, queries, keys, values):
    length, width = queries.shape
    block = 256
    blocks = length // block
    scalar, rows, whole = attend_specs(length, block)

    def body(*refs):
        attend_kernel(*refs, block=block, blocks=blocks)

    return pl.pallas_call(
        body,
        name="attend",
        grid=(width // (2 * HEAD), blocks),
        in_specs=[scalar, rows, whole, whole],
        out_specs=rows,
        out_shape=jax.ShapeDtypeStruct((length, width), jnp.bfloat16),
        cost_estimate=attend_cost(length, width, 2),
    )(edge, queries, keys, values)


def attend_back(edge, queries, keys, values, back, score_scale):
    length, width = queries.shape
    block = 256
    blocks = length // block
    scalar, rows, whole = attend_specs(length, block)

    def body(*refs):
        attend_back_kernel(*refs, block=block, blocks=blocks, score_scale=score_scale)

    shape = jax.ShapeDtypeStruct((length, width), jnp.float32)
    return pl.pallas_call(
        body,
        name="attend_back",
        grid=(width // (2 * HEAD), blocks),
        in_specs=[scalar, rows, whole, whole, rows],
        out_specs=(rows, whole, whole),
        out_shape=(shape, shape, shape),
        cost_estimate=attend_cost(length, width, 5),
    )(edge, queries, keys, values, back)


def turn(values, cosine, sine_table):
    half = HEAD // 2
    lane = lax.broadcasted_iota(jnp.int32, values.shape, 1) % HEAD
    turned = jnp.where(
        lane < half, -jnp.roll(values, -half, axis=1), jnp.roll(values, half, axis=1)
    )
    return values * cosine + turned * sine_table


def local_columns(
    block_input,
    positions,
    segments,
    cotangent,
    attn_gain,
    query_weight,
    key_weight,
    value_weight,
    out_weight,
    mlp_gain,
    gate_weight,
    up_weight,
    down_weight,
):
    f32, bf16 = jnp.float32, jnp.bfloat16
    score_scale = HEAD ** (-0.5)
    length = segments.shape[1]
    rows = query_weight.shape[0]
    head_width = KV_HEADS * HEAD
    inputs = block_input[0].astype(f32)
    out_back = cotangent[0]
    gain_one = attn_gain.astype(f32)[:, None]
    gain_two = mlp_gain.astype(f32)[:, None]

    def fold(weight, gain):
        return (weight.astype(f32) * gain).astype(bf16)

    inputs_all = gather_ctx(block_input[0])
    key_value = jnp.stack([fold(key_weight, gain_one), fold(value_weight, gain_one)])
    attn_pieces = jnp.concatenate(
        [
            head_slices(fold(query_weight, gain_one)),
            jnp.tile(key_value, (4, 1, 1)),
        ],
        axis=2,
    )
    main, tail = ff_split(gate_weight.shape[1])
    both = 2 * (main + tail)
    gate_main, gate_tail = ff_slices(fold(gate_weight, gain_two))
    up_main, up_tail = ff_slices(fold(up_weight, gain_two))
    down_pieces = jnp.concatenate(ff_slices(down_weight), axis=2)
    gate_up_pieces = jnp.concatenate([gate_main, up_main, gate_tail, up_tail], axis=2)
    attn_own = exchange_ctx(attn_pieces).reshape(8 * rows, 2 * head_width)
    edge = jnp.sum((segments[0] == 0).astype(jnp.int32))
    token = jnp.arange(length, dtype=jnp.int32)
    position = jnp.where(token < edge, token + (length - edge), token - edge)
    cosine, sine_table = rope_tables(position, HEAD)
    cosine = jnp.tile(cosine, (1, KV_HEADS))
    sine_table = jnp.tile(sine_table, (1, KV_HEADS))
    edge = edge[None]
    attn_own, down_pieces, gate_up_pieces, cosine, sine_table = tie(
        attn_own, down_pieces, gate_up_pieces, cosine, sine_table
    )
    attn_cols = gather_seq(attn_own)
    core = lax.axis_index("ctx") % 2
    other_cols = swap_cores(attn_cols[:, head_width:])
    out_rows = gather_seq(out_weight)
    down_own = exchange_ctx(down_pieces).reshape(8 * rows, -1)
    down_own, gate_up_pieces = tie(down_own, gate_up_pieces)
    gate_up_own = exchange_ctx(gate_up_pieces).reshape(8 * rows, -1)

    wide = inputs_all.astype(f32)
    shaped_all = (wide * rms_scale(wide)).astype(bf16)
    raw = jnp.dot(shaped_all, attn_cols, preferred_element_type=f32)
    raw_other = jnp.dot(shaped_all, other_cols, preferred_element_type=f32)
    raw, raw_other, down_own = tie(raw, raw_other, down_own)
    raw_own = raw[:, head_width:]
    down_near = gather_seq_near(down_own)
    queries = turn(raw[:, :head_width], cosine, sine_table).astype(bf16)
    keys = turn(jnp.where(core == 0, raw_own, raw_other), cosine, sine_table).astype(bf16)
    values = jnp.where(core == 0, raw_other, raw_own).astype(bf16)
    queries = queries * jnp.asarray(score_scale, bf16)
    attn_low = attend(edge, queries, keys, values)
    attn_low, out_rows, back_late, gate_up_own, *down_near = tie(
        attn_low, out_rows, out_back, gate_up_own, *down_near
    )
    gate_up_near = gather_seq_near(gate_up_own)
    down_cols = gather_seq_far(down_own, *down_near)
    mixed = jnp.dot(attn_low, out_rows, preferred_element_type=f32).astype(bf16)
    mixed_own = reduce_ctx(mixed)
    mixed_own, down_cols, *gate_up_near = tie(mixed_own, down_cols, *gate_up_near)
    residual = inputs + mixed_own.astype(f32)
    scale_two = rms_scale(residual)
    shaped_two = residual * scale_two
    shaped_low = shaped_two.astype(bf16)
    normed_all = gather_ctx(shaped_low)
    shaped_two, back_late = tie(shaped_two, back_late)
    gate_up = gather_seq_far(gate_up_own, *gate_up_near)
    back_all = gather_ctx(back_late)
    proj = jnp.dot(normed_all, gate_up, preferred_element_type=f32)

    def halves(left_tail, right_tail, left, right):
        return jnp.concatenate([left, left_tail], axis=1), jnp.concatenate([right, right_tail], axis=1)

    gate_proj, up_proj = halves(
        proj[:, 2 * main : 2 * main + tail],
        proj[:, 2 * main + tail :],
        proj[:, :main],
        proj[:, main : 2 * main],
    )
    sigmoid_gate = jax.nn.sigmoid(gate_proj)
    silu_gate = gate_proj * sigmoid_gate
    hidden = (silu_gate * up_proj).astype(bf16)
    mixed_out = contract_cols(hidden, down_cols).astype(bf16)
    mixed_out, back_all = tie(mixed_out, back_all)
    out_own = reduce_ctx(mixed_out)
    hidden_back = jnp.dot(back_all, down_cols, preferred_element_type=f32)
    gate_back = (
        hidden_back * up_proj * sigmoid_gate * (1.0 + gate_proj * (1.0 - sigmoid_gate))
    ).astype(bf16)
    upper_back = (hidden_back * silu_gate).astype(bf16)
    gate_up_back = jnp.concatenate(
        [gate_back[:, :main], upper_back[:, :main], gate_back[:, main:], upper_back[:, main:]],
        axis=1,
    )
    weighted = reduce_ctx(contract_cols(gate_up_back, gate_up).astype(bf16))
    gate_up_grad = contract_rows(normed_all, gate_up_back).astype(bf16)
    down_grad = contract_rows(back_all, hidden).astype(bf16)
    mlp_grads = [gate_up_grad, down_grad]
    out_own, *mlp_parts = tie(out_own, *seq_parts(mlp_grads))
    mlp_near = send_parts(mlp_parts)
    weighted, *mlp_near = tie(weighted, *mlp_near)
    weighted = weighted.astype(f32)
    residual_back = out_back.astype(f32) + scale_two * (
        weighted - shaped_two * jnp.mean(weighted * shaped_two, axis=-1, keepdims=True)
    )
    residual_low = residual_back.astype(bf16)
    low_all = gather_ctx(residual_low)
    residual_back, *mlp_near = tie(residual_back, *mlp_near)
    mlp_sums = far_sums(mlp_grads, *mlp_near[:2])
    mlp_grads_own = reduce_seq_far(mlp_grads, mlp_sums, *mlp_near[2:])
    mlp_grad = exchange_ctx(mlp_grads_own.reshape(8, rows, -1))
    attn_back = contract_cols(low_all, out_rows).astype(bf16)
    query_back, key_back, value_back = attend_back(
        edge, queries, keys, values, attn_back, score_scale
    )
    key_low = turn(key_back, cosine, -sine_table).astype(bf16)
    value_low = value_back.astype(bf16)
    other_back = jnp.where(core == 0, value_low, key_low)
    other_part = contract_rows(shaped_all, other_back).astype(bf16)
    heads_back = jnp.concatenate(
        [
            turn(query_back, cosine, -sine_table).astype(bf16),
            jnp.where(core == 0, key_low, value_low),
        ],
        axis=1,
    )
    heads_back, other_part = tie(heads_back, other_part)
    other_part = swap_cores(other_part)
    weighted_part = contract_cols(
        jnp.concatenate([heads_back, other_back], axis=1),
        jnp.concatenate([attn_cols, other_cols], axis=1),
    ).astype(bf16)
    weighted_part, low_all, mlp_grad = tie(weighted_part, low_all, mlp_grad)
    weighted_one = reduce_ctx(weighted_part).astype(f32)
    attn_part = contract_rows(shaped_all, heads_back)
    own_part = attn_part[:, head_width:] + other_part.astype(f32)
    attn_grad_own = reduce_seq(
        [jnp.concatenate([attn_part[:, :head_width].astype(bf16), own_part.astype(bf16)], axis=1)]
    )
    out_grad = reduce_seq([contract_rows(attn_low, low_all).astype(bf16)]).astype(f32)
    attn_grad_own, mlp_grad = tie(attn_grad_own, mlp_grad)
    mlp_grad = mlp_grad.astype(f32)
    attn_grad = exchange_ctx(attn_grad_own.reshape(8, rows, -1))

    gate_rows = ff_rows(mlp_grad[:, :, :main], mlp_grad[:, :, 2 * main : 2 * main + tail])
    up_rows = ff_rows(mlp_grad[:, :, main : 2 * main], mlp_grad[:, :, 2 * main + tail : both])
    down_grad = ff_rows(mlp_grad[:, :, both : both + main], mlp_grad[:, :, both + main :])
    scale_one = rms_scale(inputs)
    shaped_one = inputs * scale_one
    input_grad = residual_back + scale_one * (
        weighted_one - shaped_one * jnp.mean(weighted_one * shaped_one, axis=-1, keepdims=True)
    )
    block_output = (residual + out_own.astype(f32)).astype(bf16)
    attn_grad, out_grad, gate_rows, up_rows, down_grad, input_grad, block_output = tie(
        attn_grad, out_grad, gate_rows, up_rows, down_grad, input_grad, block_output
    )
    attn_grad = attn_grad.astype(f32)
    query_rows = from_head_slices(attn_grad[:, :, :head_width])
    pair_rows = jnp.sum(attn_grad[:, :, head_width:].reshape(4, 2, rows, head_width), axis=0)
    key_rows, value_rows = pair_rows[0], pair_rows[1]

    def row_sum(weight, grad):
        return jnp.sum(weight.astype(f32) * grad, axis=1)

    attn_gain_grad = (
        row_sum(query_weight, query_rows)
        + row_sum(key_weight, key_rows)
        + row_sum(value_weight, value_rows)
    )
    mlp_gain_grad = row_sum(gate_weight, gate_rows) + row_sum(up_weight, up_rows)
    return (
        block_output[None],
        input_grad[None],
        attn_gain_grad,
        query_rows * gain_one,
        key_rows * gain_one,
        value_rows * gain_one,
        out_grad,
        mlp_gain_grad,
        gate_rows * gain_two,
        up_rows * gain_two,
        down_grad,
    )


def solution(mesh):
    placed = (
        P("seq", "ctx", None),
        P("seq", "ctx"),
        P("seq", None),
        P("seq", "ctx", None),
        P(("seq", "ctx")),
        P(("seq", "ctx"), None),
        P(("seq", "ctx"), None),
        P(("seq", "ctx"), None),
        P(("seq", "ctx"), None),
        P(("seq", "ctx")),
        P(("seq", "ctx"), None),
        P(("seq", "ctx"), None),
        P(("seq", "ctx"), None),
    )
    seq_count, ctx_count = mesh.shape["seq"], mesh.shape["ctx"]

    def run(*args):
        width = args[0].shape[2]
        fits = (
            seq_count == KV_HEADS == 4
            and ctx_count == HEADS // KV_HEADS == 8
            and width == seq_count * ctx_count * HEAD
        )
        return jax.shard_map(
            local_columns if fits else local_rows,
            mesh=mesh,
            in_specs=placed,
            out_specs=(
                P("seq", "ctx", None),
                P("seq", "ctx", None),
                P(("seq", "ctx")),
                P(("seq", "ctx"), None),
                P(("seq", "ctx"), None),
                P(("seq", "ctx"), None),
                P(("seq", "ctx"), None),
                P(("seq", "ctx")),
                P(("seq", "ctx"), None),
                P(("seq", "ctx"), None),
                P(("seq", "ctx"), None),
            ),
            check_vma=False,
        )(*args)

    return run
```

```python
import jax
import jax.numpy as jnp
from jax import lax
from jax.experimental import pallas as pl
from jax.experimental.pallas import tpu as pltpu
from jax.sharding import PartitionSpec as P

HEADS = 32
KV_HEADS = 4
HEAD = 64


EPSILON = 1e-05
MASKED = -1e30


def rope_tables(position, head_size):
    half_size = head_size // 2
    inverse = 1.0 / 10000.0 ** (jnp.arange(half_size, dtype=jnp.float32) * 2.0 / head_size)
    angles = position.astype(jnp.float32)[:, None] * inverse[None, :]
    cosine = jnp.cos(angles)
    sine_table = jnp.sin(angles)
    return (jnp.concatenate([cosine, cosine], -1), jnp.concatenate([sine_table, sine_table], -1))


def rotate(values, cosine, sine_table):
    half_size = values.shape[-1] // 2
    turned = jnp.concatenate([-values[..., half_size:], values[..., :half_size]], -1)
    return values * cosine[:, None, :] + turned * sine_table[:, None, :]


def rms_scale(inputs):
    return lax.rsqrt(jnp.mean(inputs * inputs, axis=-1, keepdims=True) + EPSILON)


def norm_back(inputs, row_scale, gain, upstream):
    shaped = inputs * row_scale
    weighted = upstream * gain
    gain_term = jnp.sum(upstream * shaped, axis=0)
    return (
        row_scale * (weighted - shaped * jnp.mean(weighted * shaped, axis=-1, keepdims=True)),
        gain_term,
    )


def contract_rows(left, right):
    return lax.dot_general(
        left, right, (((0,), (0,)), ((), ())), preferred_element_type=jnp.float32
    )


def contract_cols(left, right):
    return lax.dot_general(
        left, right, (((1,), (1,)), ((), ())), preferred_element_type=jnp.float32
    )


def local_rows(
    block_input,
    positions,
    segments,
    cotangent,
    attn_gain,
    query_weight,
    key_weight,
    value_weight,
    out_weight,
    mlp_gain,
    gate_weight,
    up_weight,
    down_weight,
):
    row_count = block_input.shape[1]
    group_size = HEADS // KV_HEADS
    score_scale = HEAD ** (-0.5)
    inputs = block_input[0].astype(jnp.float32)
    seg_all = segments[0]
    length = seg_all.shape[0]
    block_size = min(512, length)
    block_count = length // block_size
    first_row = lax.axis_index("ctx") * row_count
    query_index = first_row + jnp.arange(row_count, dtype=jnp.int32)
    seg_rows = lax.dynamic_slice_in_dim(seg_all, first_row, row_count)
    cosine, sine_table = rope_tables(positions[0], HEAD)
    starts = jnp.arange(block_count, dtype=jnp.int32) * block_size
    seg_blocks = seg_all.reshape(block_count, block_size)

    def key_mask(seg_block, block_start):
        key_index = block_start + jnp.arange(block_size, dtype=jnp.int32)
        return (seg_rows[:, None] == seg_block[None, :]) & (
            key_index[None, :] <= query_index[:, None]
        )

    def guarded(compute, running):
        result = compute(running)
        return result

    attn_params = (
        lax.all_gather(attn_gain, ("seq", "ctx"), axis=0, tiled=True),
        lax.all_gather(query_weight, ("seq", "ctx"), axis=0, tiled=True),
        lax.all_gather(key_weight, ("seq", "ctx"), axis=0, tiled=True),
        lax.all_gather(value_weight, ("seq", "ctx"), axis=0, tiled=True),
        lax.all_gather(out_weight, ("seq", "ctx"), axis=0, tiled=True),
    )
    gain_one = attn_params[0].astype(jnp.float32)
    scale_one = rms_scale(inputs)
    normed1 = (inputs * scale_one * gain_one).astype(jnp.bfloat16)
    query_raw = jnp.dot(normed1, attn_params[1], preferred_element_type=jnp.float32)
    key_raw = jnp.dot(normed1, attn_params[2], preferred_element_type=jnp.float32)
    value_raw = jnp.dot(normed1, attn_params[3], preferred_element_type=jnp.float32)
    queries = rotate(query_raw.reshape(row_count, HEADS, HEAD), cosine, sine_table).astype(
        jnp.bfloat16
    )
    keys_local = (
        rotate(key_raw.reshape(row_count, KV_HEADS, HEAD), cosine, sine_table)
        .astype(jnp.bfloat16)
        .reshape(row_count, KV_HEADS * HEAD)
    )
    values_local = value_raw.astype(jnp.bfloat16)
    keys_all, values_all = (
        lax.all_gather(keys_local, "ctx", axis=0, tiled=True),
        lax.all_gather(values_local, "ctx", axis=0, tiled=True),
    )
    key_blocks = keys_all.reshape(block_count, block_size, KV_HEADS, HEAD)
    value_blocks = values_all.reshape(block_count, block_size, KV_HEADS, HEAD)
    query_group = queries.reshape(row_count, KV_HEADS, group_size, HEAD)

    def block_scores(key_block, allowed):
        scores = (
            jnp.einsum("tkgd,jkd->kgtj", query_group, key_block, preferred_element_type=jnp.float32)
            * score_scale
        )
        return jnp.where(allowed[None, None], scores, MASKED)

    def max_step(carry, pieces):
        key_block, seg_block, block_start = pieces
        allowed = key_mask(seg_block, block_start)

        def compute(running):
            run_max, run_sum = running
            scores = block_scores(key_block, allowed)
            new_max = jnp.maximum(run_max, jnp.max(scores, axis=-1))
            exponents = jnp.where(allowed[None, None], jnp.exp(scores - new_max[..., None]), 0.0)
            return (new_max, run_sum * jnp.exp(run_max - new_max) + jnp.sum(exponents, axis=-1))

        return (guarded(compute, carry), None)

    start_max = jnp.full((KV_HEADS, group_size, row_count), MASKED, jnp.float32)
    start_sum = jnp.zeros((KV_HEADS, group_size, row_count), jnp.float32)
    (run_max, run_sum), unused = lax.scan(
        max_step, (start_max, start_sum), (key_blocks, seg_blocks, starts)
    )
    log_sum = run_max + jnp.log(run_sum)

    def block_soft(key_block, allowed):
        scores = block_scores(key_block, allowed)
        return jnp.where(allowed[None, None], jnp.exp(scores - log_sum[..., None]), 0.0)

    def value_step(carry, pieces):
        key_block, value_block, seg_block, block_start = pieces
        allowed = key_mask(seg_block, block_start)

        def compute(running):
            acc_out, acc_fix = running
            soft_weights = block_soft(key_block, allowed)
            rounded = soft_weights.astype(jnp.bfloat16)
            leftover = (soft_weights - rounded.astype(jnp.float32)).astype(jnp.bfloat16)
            acc_out = acc_out + jnp.einsum(
                "kgtj,jkd->tkgd", rounded, value_block, preferred_element_type=jnp.float32
            )
            acc_fix = acc_fix + jnp.einsum(
                "kgtj,jkd->tkgd", leftover, value_block, preferred_element_type=jnp.float32
            )
            return (acc_out, acc_fix)

        return (guarded(compute, carry), None)

    zero_mix = jnp.zeros((row_count, KV_HEADS, group_size, HEAD), jnp.float32)
    (acc_out, acc_fix), unused = lax.scan(
        value_step, (zero_mix, zero_mix), (key_blocks, value_blocks, seg_blocks, starts)
    )
    attn_low = acc_out.reshape(row_count, HEADS * HEAD).astype(jnp.bfloat16)
    full_mix = acc_out + acc_fix
    residual = inputs + jnp.dot(attn_low, attn_params[4], preferred_element_type=jnp.float32)
    mlp_params = (
        lax.all_gather(mlp_gain, ("seq", "ctx"), axis=0, tiled=True),
        lax.all_gather(gate_weight, ("seq", "ctx"), axis=0, tiled=True),
        lax.all_gather(up_weight, ("seq", "ctx"), axis=0, tiled=True),
        lax.all_gather(down_weight, ("seq", "ctx"), axis=0, tiled=True),
    )
    gain_two = mlp_params[0].astype(jnp.float32)
    scale_two = rms_scale(residual)
    normed2 = (residual * scale_two * gain_two).astype(jnp.bfloat16)
    gate_proj = jnp.dot(normed2, mlp_params[1], preferred_element_type=jnp.float32)
    up_proj = jnp.dot(normed2, mlp_params[2], preferred_element_type=jnp.float32)
    sigmoid_gate = jax.nn.sigmoid(gate_proj)
    silu_gate = gate_proj * sigmoid_gate
    hidden = (silu_gate * up_proj).astype(jnp.bfloat16)
    block_output = (residual + contract_cols(hidden, mlp_params[3])).astype(jnp.bfloat16)
    out_back = cotangent[0]
    out_float = out_back.astype(jnp.float32)
    mlp_again = (
        lax.all_gather(mlp_gain, ("seq", "ctx"), axis=0, tiled=True),
        lax.all_gather(gate_weight, ("seq", "ctx"), axis=0, tiled=True),
        lax.all_gather(up_weight, ("seq", "ctx"), axis=0, tiled=True),
        lax.all_gather(down_weight, ("seq", "ctx"), axis=0, tiled=True),
    )
    down_grad = lax.psum_scatter(
        contract_rows(out_back, hidden), ("seq", "ctx"), scatter_dimension=0, tiled=True
    )
    hidden_back = jnp.dot(out_back, mlp_again[3], preferred_element_type=jnp.float32)
    gate_back = (
        hidden_back * up_proj * sigmoid_gate * (1.0 + gate_proj * (1.0 - sigmoid_gate))
    ).astype(jnp.bfloat16)
    upper_back = (hidden_back * silu_gate).astype(jnp.bfloat16)
    gate_full_grad = contract_rows(normed2, gate_back)
    up_full_grad = contract_rows(normed2, upper_back)
    normed2_back = contract_cols(gate_back, mlp_again[1]) + contract_cols(upper_back, mlp_again[2])
    residual_norm, mlp_gain_term = norm_back(
        residual, scale_two, mlp_again[0].astype(jnp.float32), normed2_back
    )
    mlp_sums = (
        lax.psum_scatter(mlp_gain_term, ("seq", "ctx"), scatter_dimension=0, tiled=True),
        lax.psum_scatter(gate_full_grad, ("seq", "ctx"), scatter_dimension=0, tiled=True),
        lax.psum_scatter(up_full_grad, ("seq", "ctx"), scatter_dimension=0, tiled=True),
    )
    residual_back = out_float + residual_norm
    attn_again = (
        lax.all_gather(attn_gain, ("seq", "ctx"), axis=0, tiled=True),
        lax.all_gather(query_weight, ("seq", "ctx"), axis=0, tiled=True),
        lax.all_gather(key_weight, ("seq", "ctx"), axis=0, tiled=True),
        lax.all_gather(value_weight, ("seq", "ctx"), axis=0, tiled=True),
        lax.all_gather(out_weight, ("seq", "ctx"), axis=0, tiled=True),
    )
    residual_low = residual_back.astype(jnp.bfloat16)
    out_full_grad = contract_rows(attn_low, residual_low)
    attn_back = contract_cols(residual_low, attn_again[4]).astype(jnp.bfloat16)
    grad_mix = attn_back.reshape(row_count, KV_HEADS, group_size, HEAD)
    delta_rows = jnp.transpose(jnp.sum(grad_mix.astype(jnp.float32) * full_mix, axis=-1), (1, 2, 0))

    def grad_step(carry, pieces):
        key_block, value_block, seg_block, block_start = pieces
        allowed = key_mask(seg_block, block_start)

        def compute(acc_query):
            soft_weights = block_soft(key_block, allowed)
            rounded = soft_weights.astype(jnp.bfloat16)
            value_part = jnp.einsum(
                "kgtj,tkgd->jkd", rounded, grad_mix, preferred_element_type=jnp.float32
            )
            soft_back = jnp.einsum(
                "tkgd,jkd->kgtj", grad_mix, value_block, preferred_element_type=jnp.float32
            )
            score_back = (soft_weights * (soft_back - delta_rows[..., None])).astype(jnp.bfloat16)
            acc_query = acc_query + jnp.einsum(
                "kgtj,jkd->tkgd", score_back, key_block, preferred_element_type=jnp.float32
            )
            key_part = jnp.einsum(
                "kgtj,tkgd->jkd", score_back, query_group, preferred_element_type=jnp.float32
            )
            return (acc_query, (key_part, value_part))

        return guarded(compute, carry)

    acc_query, (key_parts, value_parts) = lax.scan(
        grad_step, zero_mix, (key_blocks, value_blocks, seg_blocks, starts)
    )
    key_sums, value_sums = (
        lax.psum_scatter(
            key_parts.reshape(length, KV_HEADS * HEAD).astype(jnp.bfloat16),
            "ctx",
            scatter_dimension=0,
            tiled=True,
        ).astype(jnp.float32),
        lax.psum_scatter(
            value_parts.reshape(length, KV_HEADS * HEAD).astype(jnp.bfloat16),
            "ctx",
            scatter_dimension=0,
            tiled=True,
        ).astype(jnp.float32),
    )
    query_low = (
        rotate((acc_query * score_scale).reshape(row_count, HEADS, HEAD), cosine, -sine_table)
        .astype(jnp.bfloat16)
        .reshape(row_count, HEADS * HEAD)
    )
    key_low = (
        rotate((key_sums * score_scale).reshape(row_count, KV_HEADS, HEAD), cosine, -sine_table)
        .astype(jnp.bfloat16)
        .reshape(row_count, KV_HEADS * HEAD)
    )
    value_low = value_sums.astype(jnp.bfloat16)
    query_full_grad = contract_rows(normed1, query_low)
    key_full_grad = contract_rows(normed1, key_low)
    value_full_grad = contract_rows(normed1, value_low)
    normed1_back = (
        contract_cols(query_low, attn_again[1])
        + contract_cols(key_low, attn_again[2])
        + contract_cols(value_low, attn_again[3])
    )
    input_norm, attn_gain_term = norm_back(
        inputs, scale_one, attn_again[0].astype(jnp.float32), normed1_back
    )
    attn_sums = (
        lax.psum_scatter(attn_gain_term, ("seq", "ctx"), scatter_dimension=0, tiled=True),
        lax.psum_scatter(query_full_grad, ("seq", "ctx"), scatter_dimension=0, tiled=True),
        lax.psum_scatter(key_full_grad, ("seq", "ctx"), scatter_dimension=0, tiled=True),
        lax.psum_scatter(value_full_grad, ("seq", "ctx"), scatter_dimension=0, tiled=True),
        lax.psum_scatter(out_full_grad, ("seq", "ctx"), scatter_dimension=0, tiled=True),
    )
    input_grad = residual_back + input_norm
    return (
        block_output[None],
        input_grad[None],
        attn_sums[0],
        attn_sums[1],
        attn_sums[2],
        attn_sums[3],
        attn_sums[4],
        mlp_sums[0],
        mlp_sums[1],
        mlp_sums[2],
        down_grad,
    )


SEQ_X = [(0, 1), (1, 0), (2, 3), (3, 2)]
SEQ_Y = [(0, 2), (2, 0), (1, 3), (3, 1)]


def gather_ctx(block):
    return lax.all_gather(block, "ctx", axis=0, tiled=True)


def reduce_ctx(partial):
    return lax.psum_scatter(partial, "ctx", scatter_dimension=0, tiled=True)


def exchange_ctx(pieces):
    return lax.all_to_all(pieces, "ctx", 0, 0, tiled=True)


def gather_seq_near(block):
    return lax.ppermute(block, "seq", SEQ_X), lax.ppermute(block, "seq", SEQ_Y)


def gather_seq_far(block, from_x, from_y):
    rows, width = block.shape
    half = rows // 2
    mine = lax.axis_index("seq")
    far_top = lax.ppermute(from_x[:half], "seq", SEQ_Y)
    far_low = lax.ppermute(from_y[half:], "seq", SEQ_X)
    whole = jnp.zeros((4 * rows, width), block.dtype)
    for piece, start in (
        (block, mine * rows),
        (from_x, (mine ^ 1) * rows),
        (from_y, (mine ^ 2) * rows),
        (far_top, (mine ^ 3) * rows),
        (far_low, (mine ^ 3) * rows + half),
    ):
        whole = lax.dynamic_update_slice_in_dim(whole, piece, start, 0)
    return whole


def gather_seq(block):
    return gather_seq_far(block, *gather_seq_near(block))


def seq_part(partials, other, low):
    rows = partials[0].shape[0] // 4
    half = rows // 2
    start = (lax.axis_index("seq") ^ other) * rows + (half if low else 0)
    return jnp.concatenate(
        [lax.dynamic_slice_in_dim(partial, start, half, 0) for partial in partials], axis=1
    )


def seq_parts(partials):
    return (
        seq_part(partials, 3, False),
        seq_part(partials, 3, True),
        seq_part(partials, 1, False),
        seq_part(partials, 2, True),
    )


def send_parts(parts):
    return tuple(
        lax.ppermute(part, "seq", axis) for part, axis in zip(parts, (SEQ_X, SEQ_Y) * 2)
    )


def reduce_seq_near(partials):
    return send_parts(seq_parts(partials))


def add_wide(*terms):
    total = terms[0].astype(jnp.float32)
    for term in terms[1:]:
        total = total + term.astype(jnp.float32)
    return total


def far_sums(partials, top_far, low_far):
    return (
        add_wide(seq_part(partials, 2, False), top_far).astype(jnp.bfloat16),
        add_wide(seq_part(partials, 1, True), low_far).astype(jnp.bfloat16),
    )


def reduce_seq_far(partials, sums, top_near, low_near):
    top_send, low_send = sums
    top_last = lax.ppermute(top_send, "seq", SEQ_Y)
    low_last = lax.ppermute(low_send, "seq", SEQ_X)
    return jnp.concatenate(
        [
            add_wide(seq_part(partials, 0, False), top_near, top_last),
            add_wide(seq_part(partials, 0, True), low_near, low_last),
        ],
        axis=0,
    ).astype(jnp.bfloat16)


def reduce_seq(partials):
    top_far, low_far, *nears = reduce_seq_near(partials)
    return reduce_seq_far(partials, far_sums(partials, top_far, low_far), *nears)


def tie(*values):
    return lax.optimization_barrier(values)


def swap_cores(block):
    return lax.ppermute(block, "ctx", [(device, device ^ 1) for device in range(8)])


def ff_split(width):
    main = width // 8 // 128 * 128
    return main, width // 8 - main


def ff_slices(weight):
    rows, width = weight.shape
    main, tail = ff_split(width)
    return (
        jnp.transpose(weight[:, : 8 * main].reshape(rows, 8, main), (1, 0, 2)),
        jnp.transpose(weight[:, 8 * main :].reshape(rows, 8, tail), (1, 0, 2)),
    )


def ff_rows(main, tail):
    count, rows, width = main.shape
    return jnp.concatenate(
        [
            jnp.transpose(main, (1, 0, 2)).reshape(rows, count * width),
            jnp.transpose(tail, (1, 0, 2)).reshape(rows, count * tail.shape[2]),
        ],
        axis=1,
    )


def head_slices(weight):
    rows = weight.shape[0]
    split = weight.reshape(rows, KV_HEADS, 8, HEAD)
    return jnp.transpose(split, (2, 0, 1, 3)).reshape(8, rows, KV_HEADS * HEAD)


def from_head_slices(pieces):
    rows = pieces.shape[1]
    split = pieces.reshape(8, rows, KV_HEADS, HEAD)
    return jnp.transpose(split, (1, 2, 0, 3)).reshape(rows, HEADS * HEAD)


def attend_mask(edge, first_row, block, span):
    row = first_row + lax.broadcasted_iota(jnp.int32, (block, span), 0)
    column = lax.broadcasted_iota(jnp.int32, (block, span), 1)
    return (column <= row) & (column >= jnp.where(row >= edge, edge, 0))


def soft_rows(query, key, allowed):
    scores = lax.dot_general(
        query, key, (((1,), (1,)), ((), ())), preferred_element_type=jnp.float32
    )
    scores = jnp.where(allowed, scores, MASKED)
    exponents = jnp.exp(scores - jnp.max(scores, axis=-1, keepdims=True))
    return exponents * (1.0 / jnp.sum(exponents, axis=-1, keepdims=True))


def attend_kernel(edge_ref, query_ref, key_ref, value_ref, mix_ref, *, block, blocks):
    step = pl.program_id(1)
    for index in range(blocks):

        @pl.when(step == index)
        def _(index=index):
            span = (index + 1) * block
            allowed = attend_mask(edge_ref[0], index * block, block, span)
            mixed = []
            for head in range(2):
                cut = slice(head * HEAD, (head + 1) * HEAD)
                soft = soft_rows(query_ref[:, cut], key_ref[:span, cut], allowed)
                mixed.append(
                    jnp.dot(
                        soft.astype(jnp.bfloat16),
                        value_ref[:span, cut],
                        preferred_element_type=jnp.float32,
                    )
                )
            mix_ref[...] = jnp.concatenate(mixed, axis=-1).astype(mix_ref.dtype)


def attend_back_kernel(
    edge_ref,
    query_ref,
    key_ref,
    value_ref,
    back_ref,
    query_back_ref,
    key_back_ref,
    value_back_ref,
    *,
    block,
    blocks,
    score_scale,
):
    step = pl.program_id(1)

    @pl.when(step == 0)
    def _():
        key_back_ref[...] = jnp.zeros_like(key_back_ref)
        value_back_ref[...] = jnp.zeros_like(value_back_ref)

    for index in range(blocks):

        @pl.when(step == index)
        def _(index=index):
            span = (index + 1) * block
            allowed = attend_mask(edge_ref[0], index * block, block, span)
            query_parts, key_parts, value_parts = [], [], []
            for head in range(2):
                cut = slice(head * HEAD, (head + 1) * HEAD)
                query, key = query_ref[:, cut], key_ref[:span, cut]
                back = back_ref[:, cut]
                soft = soft_rows(query, key, allowed)
                soft_back = contract_cols(back, value_ref[:span, cut])
                delta = jnp.sum(soft * soft_back, axis=-1, keepdims=True)
                score_back = (soft * (soft_back - delta)).astype(jnp.bfloat16)
                query_parts.append(
                    jnp.dot(score_back, key, preferred_element_type=jnp.float32) * score_scale
                )
                key_parts.append(contract_rows(score_back, query))
                value_parts.append(contract_rows(soft.astype(jnp.bfloat16), back))
            query_back_ref[...] = jnp.concatenate(query_parts, axis=-1)
            key_back_ref[:span, :] += jnp.concatenate(key_parts, axis=-1)
            value_back_ref[:span, :] += jnp.concatenate(value_parts, axis=-1)


def attend_specs(length, block):
    rows = pl.BlockSpec((block, 2 * HEAD), lambda pair, step: (step, pair))
    whole = pl.BlockSpec((length, 2 * HEAD), lambda pair, step: (0, pair))
    edge = pl.BlockSpec(memory_space=pltpu.SMEM)
    return edge, rows, whole


def attend_cost(length, width, products):
    return pl.CostEstimate(
        flops=8 * products * length * length * width,
        transcendentals=length * length * width // HEAD,
        bytes_accessed=(2 * products + 4) * length * width,
    )


def attend(edge, queries, keys, values):
    length, width = queries.shape
    block = 256
    blocks = length // block
    scalar, rows, whole = attend_specs(length, block)

    def body(*refs):
        attend_kernel(*refs, block=block, blocks=blocks)

    return pl.pallas_call(
        body,
        name="attend",
        grid=(width // (2 * HEAD), blocks),
        in_specs=[scalar, rows, whole, whole],
        out_specs=rows,
        out_shape=jax.ShapeDtypeStruct((length, width), jnp.bfloat16),
        cost_estimate=attend_cost(length, width, 2),
    )(edge, queries, keys, values)


def attend_back(edge, queries, keys, values, back, score_scale):
    length, width = queries.shape
    block = 256
    blocks = length // block
    scalar, rows, whole = attend_specs(length, block)

    def body(*refs):
        attend_back_kernel(*refs, block=block, blocks=blocks, score_scale=score_scale)

    shape = jax.ShapeDtypeStruct((length, width), jnp.float32)
    return pl.pallas_call(
        body,
        name="attend_back",
        grid=(width // (2 * HEAD), blocks),
        in_specs=[scalar, rows, whole, whole, rows],
        out_specs=(rows, whole, whole),
        out_shape=(shape, shape, shape),
        cost_estimate=attend_cost(length, width, 5),
    )(edge, queries, keys, values, back)


def turn(values, cosine, sine_table):
    half = HEAD // 2
    lane = lax.broadcasted_iota(jnp.int32, values.shape, 1) % HEAD
    turned = jnp.where(
        lane < half, -jnp.roll(values, -half, axis=1), jnp.roll(values, half, axis=1)
    )
    return values * cosine + turned * sine_table


def local_columns(
    block_input,
    positions,
    segments,
    cotangent,
    attn_gain,
    query_weight,
    key_weight,
    value_weight,
    out_weight,
    mlp_gain,
    gate_weight,
    up_weight,
    down_weight,
):
    f32, bf16 = jnp.float32, jnp.bfloat16
    score_scale = HEAD ** (-0.5)
    length = segments.shape[1]
    rows = query_weight.shape[0]
    head_width = KV_HEADS * HEAD
    inputs = block_input[0].astype(f32)
    out_back = cotangent[0]
    gain_one = attn_gain.astype(f32)[:, None]
    gain_two = mlp_gain.astype(f32)[:, None]

    def fold(weight, gain):
        return (weight.astype(f32) * gain).astype(bf16)

    inputs_all = gather_ctx(block_input[0])
    key_value = jnp.stack([fold(key_weight, gain_one), fold(value_weight, gain_one)])
    attn_pieces = jnp.concatenate(
        [
            head_slices(fold(query_weight, gain_one)),
            jnp.tile(key_value, (4, 1, 1)),
        ],
        axis=2,
    )
    main, tail = ff_split(gate_weight.shape[1])
    both = 2 * (main + tail)
    gate_main, gate_tail = ff_slices(fold(gate_weight, gain_two))
    up_main, up_tail = ff_slices(fold(up_weight, gain_two))
    down_pieces = jnp.concatenate(ff_slices(down_weight), axis=2)
    gate_up_pieces = jnp.concatenate([gate_main, up_main, gate_tail, up_tail], axis=2)
    attn_own = exchange_ctx(attn_pieces).reshape(8 * rows, 2 * head_width)
    edge = jnp.sum((segments[0] == 0).astype(jnp.int32))
    token = jnp.arange(length, dtype=jnp.int32)
    position = jnp.where(token < edge, token + (length - edge), token - edge)
    cosine, sine_table = rope_tables(position, HEAD)
    cosine = jnp.tile(cosine, (1, KV_HEADS))
    sine_table = jnp.tile(sine_table, (1, KV_HEADS))
    edge = edge[None]
    attn_own, down_pieces, gate_up_pieces, cosine, sine_table = tie(
        attn_own, down_pieces, gate_up_pieces, cosine, sine_table
    )
    attn_cols = gather_seq(attn_own)
    core = lax.axis_index("ctx") % 2
    other_cols = swap_cores(attn_cols[:, head_width:])
    out_rows = gather_seq(out_weight)
    down_own = exchange_ctx(down_pieces).reshape(8 * rows, -1)
    down_own, gate_up_pieces = tie(down_own, gate_up_pieces)
    gate_up_own = exchange_ctx(gate_up_pieces).reshape(8 * rows, -1)

    wide = inputs_all.astype(f32)
    shaped_all = (wide * rms_scale(wide)).astype(bf16)
    raw = jnp.dot(shaped_all, attn_cols, preferred_element_type=f32)
    raw_other = jnp.dot(shaped_all, other_cols, preferred_element_type=f32)
    raw, raw_other, down_own = tie(raw, raw_other, down_own)
    raw_own = raw[:, head_width:]
    down_near = gather_seq_near(down_own)
    queries = turn(raw[:, :head_width], cosine, sine_table).astype(bf16)
    keys = turn(jnp.where(core == 0, raw_own, raw_other), cosine, sine_table).astype(bf16)
    values = jnp.where(core == 0, raw_other, raw_own).astype(bf16)
    queries = queries * jnp.asarray(score_scale, bf16)
    attn_low = attend(edge, queries, keys, values)
    attn_low, out_rows, back_late, gate_up_own, *down_near = tie(
        attn_low, out_rows, out_back, gate_up_own, *down_near
    )
    gate_up_near = gather_seq_near(gate_up_own)
    down_cols = gather_seq_far(down_own, *down_near)
    mixed = jnp.dot(attn_low, out_rows, preferred_element_type=f32).astype(bf16)
    mixed_own = reduce_ctx(mixed)
    mixed_own, down_cols, *gate_up_near = tie(mixed_own, down_cols, *gate_up_near)
    residual = inputs + mixed_own.astype(f32)
    scale_two = rms_scale(residual)
    shaped_two = residual * scale_two
    shaped_low = shaped_two.astype(bf16)
    normed_all = gather_ctx(shaped_low)
    shaped_two, back_late = tie(shaped_two, back_late)
    gate_up = gather_seq_far(gate_up_own, *gate_up_near)
    back_all = gather_ctx(back_late)
    proj = jnp.dot(normed_all, gate_up, preferred_element_type=f32)

    def halves(left_tail, right_tail, left, right):
        return jnp.concatenate([left, left_tail], axis=1), jnp.concatenate([right, right_tail], axis=1)

    gate_proj, up_proj = halves(
        proj[:, 2 * main : 2 * main + tail],
        proj[:, 2 * main + tail :],
        proj[:, :main],
        proj[:, main : 2 * main],
    )
    sigmoid_gate = jax.nn.sigmoid(gate_proj)
    silu_gate = gate_proj * sigmoid_gate
    hidden = (silu_gate * up_proj).astype(bf16)
    mixed_out = contract_cols(hidden, down_cols).astype(bf16)
    mixed_out, back_all = tie(mixed_out, back_all)
    out_own = reduce_ctx(mixed_out)
    hidden_back = jnp.dot(back_all, down_cols, preferred_element_type=f32)
    gate_back = (
        hidden_back * up_proj * sigmoid_gate * (1.0 + gate_proj * (1.0 - sigmoid_gate))
    ).astype(bf16)
    upper_back = (hidden_back * silu_gate).astype(bf16)
    gate_up_back = jnp.concatenate(
        [gate_back[:, :main], upper_back[:, :main], gate_back[:, main:], upper_back[:, main:]],
        axis=1,
    )
    weighted = reduce_ctx(contract_cols(gate_up_back, gate_up).astype(bf16))
    gate_up_grad = contract_rows(normed_all, gate_up_back).astype(bf16)
    down_grad = contract_rows(back_all, hidden).astype(bf16)
    mlp_grads = [gate_up_grad, down_grad]
    out_own, *mlp_parts = tie(out_own, *seq_parts(mlp_grads))
    mlp_near = send_parts(mlp_parts)
    weighted, *mlp_near = tie(weighted, *mlp_near)
    weighted = weighted.astype(f32)
    residual_back = out_back.astype(f32) + scale_two * (
        weighted - shaped_two * jnp.mean(weighted * shaped_two, axis=-1, keepdims=True)
    )
    residual_low = residual_back.astype(bf16)
    low_all = gather_ctx(residual_low)
    residual_back, *mlp_near = tie(residual_back, *mlp_near)
    mlp_sums = far_sums(mlp_grads, *mlp_near[:2])
    mlp_grads_own = reduce_seq_far(mlp_grads, mlp_sums, *mlp_near[2:])
    mlp_grad = exchange_ctx(mlp_grads_own.reshape(8, rows, -1))
    attn_back = contract_cols(low_all, out_rows).astype(bf16)
    query_back, key_back, value_back = attend_back(
        edge, queries, keys, values, attn_back, score_scale
    )
    key_low = turn(key_back, cosine, -sine_table).astype(bf16)
    value_low = value_back.astype(bf16)
    other_back = jnp.where(core == 0, value_low, key_low)
    other_part = contract_rows(shaped_all, other_back).astype(bf16)
    heads_back = jnp.concatenate(
        [
            turn(query_back, cosine, -sine_table).astype(bf16),
            jnp.where(core == 0, key_low, value_low),
        ],
        axis=1,
    )
    heads_back, other_part = tie(heads_back, other_part)
    other_part = swap_cores(other_part)
    weighted_part = contract_cols(
        jnp.concatenate([heads_back, other_back], axis=1),
        jnp.concatenate([attn_cols, other_cols], axis=1),
    ).astype(bf16)
    weighted_part, mlp_grad, other_part = tie(weighted_part, mlp_grad, other_part)
    weighted_one = reduce_ctx(weighted_part)
    attn_part = contract_rows(shaped_all, heads_back)
    own_part = attn_part[:, head_width:] + other_part.astype(f32)
    attn_parts = [
        jnp.concatenate([attn_part[:, :head_width].astype(bf16), own_part.astype(bf16)], axis=1)
    ]
    attn_near = reduce_seq_near(attn_parts)
    low_all, *attn_near = tie(low_all, *attn_near)
    attn_sums = far_sums(attn_parts, *attn_near[:2])
    attn_grad_own = reduce_seq_far(attn_parts, attn_sums, *attn_near[2:])
    out_grad = reduce_seq([contract_rows(attn_low, low_all).astype(bf16)]).astype(f32)
    attn_grad_own, mlp_grad = tie(attn_grad_own, mlp_grad)
    mlp_grad = mlp_grad.astype(f32)
    attn_grad = exchange_ctx(attn_grad_own.reshape(8, rows, -1))

    gate_rows = ff_rows(mlp_grad[:, :, :main], mlp_grad[:, :, 2 * main : 2 * main + tail])
    up_rows = ff_rows(mlp_grad[:, :, main : 2 * main], mlp_grad[:, :, 2 * main + tail : both])
    down_grad = ff_rows(mlp_grad[:, :, both : both + main], mlp_grad[:, :, both + main :])
    block_output = (residual + out_own.astype(f32)).astype(bf16)
    attn_grad, out_grad, gate_rows, up_rows, down_grad, block_output = tie(
        attn_grad, out_grad, gate_rows, up_rows, down_grad, block_output
    )
    attn_grad = attn_grad.astype(f32)
    query_rows = from_head_slices(attn_grad[:, :, :head_width])
    pair_rows = jnp.sum(attn_grad[:, :, head_width:].reshape(4, 2, rows, head_width), axis=0)
    key_rows, value_rows = pair_rows[0], pair_rows[1]

    def row_sum(weight, grad):
        return jnp.sum(weight.astype(f32) * grad, axis=1)

    attn_gain_grad = (
        row_sum(query_weight, query_rows)
        + row_sum(key_weight, key_rows)
        + row_sum(value_weight, value_rows)
    )
    mlp_gain_grad = row_sum(gate_weight, gate_rows) + row_sum(up_weight, up_rows)
    weighted_one, attn_gain_grad = tie(weighted_one, attn_gain_grad)
    weighted_one = weighted_one.astype(f32)
    scale_one = rms_scale(inputs)
    shaped_one = inputs * scale_one
    input_grad = residual_back + scale_one * (
        weighted_one - shaped_one * jnp.mean(weighted_one * shaped_one, axis=-1, keepdims=True)
    )
    return (
        block_output[None],
        input_grad[None],
        attn_gain_grad,
        query_rows * gain_one,
        key_rows * gain_one,
        value_rows * gain_one,
        out_grad,
        mlp_gain_grad,
        gate_rows * gain_two,
        up_rows * gain_two,
        down_grad,
    )


def solution(mesh):
    placed = (
        P("seq", "ctx", None),
        P("seq", "ctx"),
        P("seq", None),
        P("seq", "ctx", None),
        P(("seq", "ctx")),
        P(("seq", "ctx"), None),
        P(("seq", "ctx"), None),
        P(("seq", "ctx"), None),
        P(("seq", "ctx"), None),
        P(("seq", "ctx")),
        P(("seq", "ctx"), None),
        P(("seq", "ctx"), None),
        P(("seq", "ctx"), None),
    )
    seq_count, ctx_count = mesh.shape["seq"], mesh.shape["ctx"]

    def run(*args):
        width = args[0].shape[2]
        fits = (
            seq_count == KV_HEADS == 4
            and ctx_count == HEADS // KV_HEADS == 8
            and width == seq_count * ctx_count * HEAD
        )
        return jax.shard_map(
            local_columns if fits else local_rows,
            mesh=mesh,
            in_specs=placed,
            out_specs=(
                P("seq", "ctx", None),
                P("seq", "ctx", None),
                P(("seq", "ctx")),
                P(("seq", "ctx"), None),
                P(("seq", "ctx"), None),
                P(("seq", "ctx"), None),
                P(("seq", "ctx"), None),
                P(("seq", "ctx")),
                P(("seq", "ctx"), None),
                P(("seq", "ctx"), None),
                P(("seq", "ctx"), None),
            ),
            check_vma=False,
        )(*args)

    return run
```

```python
import jax
import jax.numpy as jnp
from jax import lax
from jax.experimental import pallas as pl
from jax.experimental.pallas import tpu as pltpu
from jax.sharding import PartitionSpec as P

HEADS = 32
KV_HEADS = 4
HEAD = 64


EPSILON = 1e-05
MASKED = -1e30


def rope_tables(position, head_size):
    half_size = head_size // 2
    inverse = 1.0 / 10000.0 ** (jnp.arange(half_size, dtype=jnp.float32) * 2.0 / head_size)
    angles = position.astype(jnp.float32)[:, None] * inverse[None, :]
    cosine = jnp.cos(angles)
    sine_table = jnp.sin(angles)
    return (jnp.concatenate([cosine, cosine], -1), jnp.concatenate([sine_table, sine_table], -1))


def rotate(values, cosine, sine_table):
    half_size = values.shape[-1] // 2
    turned = jnp.concatenate([-values[..., half_size:], values[..., :half_size]], -1)
    return values * cosine[:, None, :] + turned * sine_table[:, None, :]


def rms_scale(inputs):
    return lax.rsqrt(jnp.mean(inputs * inputs, axis=-1, keepdims=True) + EPSILON)


def norm_back(inputs, row_scale, gain, upstream):
    shaped = inputs * row_scale
    weighted = upstream * gain
    gain_term = jnp.sum(upstream * shaped, axis=0)
    return (
        row_scale * (weighted - shaped * jnp.mean(weighted * shaped, axis=-1, keepdims=True)),
        gain_term,
    )


def contract_rows(left, right):
    return lax.dot_general(
        left, right, (((0,), (0,)), ((), ())), preferred_element_type=jnp.float32
    )


def contract_cols(left, right):
    return lax.dot_general(
        left, right, (((1,), (1,)), ((), ())), preferred_element_type=jnp.float32
    )


def local_rows(
    block_input,
    positions,
    segments,
    cotangent,
    attn_gain,
    query_weight,
    key_weight,
    value_weight,
    out_weight,
    mlp_gain,
    gate_weight,
    up_weight,
    down_weight,
):
    row_count = block_input.shape[1]
    group_size = HEADS // KV_HEADS
    score_scale = HEAD ** (-0.5)
    inputs = block_input[0].astype(jnp.float32)
    seg_all = segments[0]
    length = seg_all.shape[0]
    block_size = min(512, length)
    block_count = length // block_size
    first_row = lax.axis_index("ctx") * row_count
    query_index = first_row + jnp.arange(row_count, dtype=jnp.int32)
    seg_rows = lax.dynamic_slice_in_dim(seg_all, first_row, row_count)
    cosine, sine_table = rope_tables(positions[0], HEAD)
    starts = jnp.arange(block_count, dtype=jnp.int32) * block_size
    seg_blocks = seg_all.reshape(block_count, block_size)

    def key_mask(seg_block, block_start):
        key_index = block_start + jnp.arange(block_size, dtype=jnp.int32)
        return (seg_rows[:, None] == seg_block[None, :]) & (
            key_index[None, :] <= query_index[:, None]
        )

    def guarded(compute, running):
        result = compute(running)
        return result

    attn_params = (
        lax.all_gather(attn_gain, ("seq", "ctx"), axis=0, tiled=True),
        lax.all_gather(query_weight, ("seq", "ctx"), axis=0, tiled=True),
        lax.all_gather(key_weight, ("seq", "ctx"), axis=0, tiled=True),
        lax.all_gather(value_weight, ("seq", "ctx"), axis=0, tiled=True),
        lax.all_gather(out_weight, ("seq", "ctx"), axis=0, tiled=True),
    )
    gain_one = attn_params[0].astype(jnp.float32)
    scale_one = rms_scale(inputs)
    normed1 = (inputs * scale_one * gain_one).astype(jnp.bfloat16)
    query_raw = jnp.dot(normed1, attn_params[1], preferred_element_type=jnp.float32)
    key_raw = jnp.dot(normed1, attn_params[2], preferred_element_type=jnp.float32)
    value_raw = jnp.dot(normed1, attn_params[3], preferred_element_type=jnp.float32)
    queries = rotate(query_raw.reshape(row_count, HEADS, HEAD), cosine, sine_table).astype(
        jnp.bfloat16
    )
    keys_local = (
        rotate(key_raw.reshape(row_count, KV_HEADS, HEAD), cosine, sine_table)
        .astype(jnp.bfloat16)
        .reshape(row_count, KV_HEADS * HEAD)
    )
    values_local = value_raw.astype(jnp.bfloat16)
    keys_all, values_all = (
        lax.all_gather(keys_local, "ctx", axis=0, tiled=True),
        lax.all_gather(values_local, "ctx", axis=0, tiled=True),
    )
    key_blocks = keys_all.reshape(block_count, block_size, KV_HEADS, HEAD)
    value_blocks = values_all.reshape(block_count, block_size, KV_HEADS, HEAD)
    query_group = queries.reshape(row_count, KV_HEADS, group_size, HEAD)

    def block_scores(key_block, allowed):
        scores = (
            jnp.einsum("tkgd,jkd->kgtj", query_group, key_block, preferred_element_type=jnp.float32)
            * score_scale
        )
        return jnp.where(allowed[None, None], scores, MASKED)

    def max_step(carry, pieces):
        key_block, seg_block, block_start = pieces
        allowed = key_mask(seg_block, block_start)

        def compute(running):
            run_max, run_sum = running
            scores = block_scores(key_block, allowed)
            new_max = jnp.maximum(run_max, jnp.max(scores, axis=-1))
            exponents = jnp.where(allowed[None, None], jnp.exp(scores - new_max[..., None]), 0.0)
            return (new_max, run_sum * jnp.exp(run_max - new_max) + jnp.sum(exponents, axis=-1))

        return (guarded(compute, carry), None)

    start_max = jnp.full((KV_HEADS, group_size, row_count), MASKED, jnp.float32)
    start_sum = jnp.zeros((KV_HEADS, group_size, row_count), jnp.float32)
    (run_max, run_sum), unused = lax.scan(
        max_step, (start_max, start_sum), (key_blocks, seg_blocks, starts)
    )
    log_sum = run_max + jnp.log(run_sum)

    def block_soft(key_block, allowed):
        scores = block_scores(key_block, allowed)
        return jnp.where(allowed[None, None], jnp.exp(scores - log_sum[..., None]), 0.0)

    def value_step(carry, pieces):
        key_block, value_block, seg_block, block_start = pieces
        allowed = key_mask(seg_block, block_start)

        def compute(running):
            acc_out, acc_fix = running
            soft_weights = block_soft(key_block, allowed)
            rounded = soft_weights.astype(jnp.bfloat16)
            leftover = (soft_weights - rounded.astype(jnp.float32)).astype(jnp.bfloat16)
            acc_out = acc_out + jnp.einsum(
                "kgtj,jkd->tkgd", rounded, value_block, preferred_element_type=jnp.float32
            )
            acc_fix = acc_fix + jnp.einsum(
                "kgtj,jkd->tkgd", leftover, value_block, preferred_element_type=jnp.float32
            )
            return (acc_out, acc_fix)

        return (guarded(compute, carry), None)

    zero_mix = jnp.zeros((row_count, KV_HEADS, group_size, HEAD), jnp.float32)
    (acc_out, acc_fix), unused = lax.scan(
        value_step, (zero_mix, zero_mix), (key_blocks, value_blocks, seg_blocks, starts)
    )
    attn_low = acc_out.reshape(row_count, HEADS * HEAD).astype(jnp.bfloat16)
    full_mix = acc_out + acc_fix
    residual = inputs + jnp.dot(attn_low, attn_params[4], preferred_element_type=jnp.float32)
    mlp_params = (
        lax.all_gather(mlp_gain, ("seq", "ctx"), axis=0, tiled=True),
        lax.all_gather(gate_weight, ("seq", "ctx"), axis=0, tiled=True),
        lax.all_gather(up_weight, ("seq", "ctx"), axis=0, tiled=True),
        lax.all_gather(down_weight, ("seq", "ctx"), axis=0, tiled=True),
    )
    gain_two = mlp_params[0].astype(jnp.float32)
    scale_two = rms_scale(residual)
    normed2 = (residual * scale_two * gain_two).astype(jnp.bfloat16)
    gate_proj = jnp.dot(normed2, mlp_params[1], preferred_element_type=jnp.float32)
    up_proj = jnp.dot(normed2, mlp_params[2], preferred_element_type=jnp.float32)
    sigmoid_gate = jax.nn.sigmoid(gate_proj)
    silu_gate = gate_proj * sigmoid_gate
    hidden = (silu_gate * up_proj).astype(jnp.bfloat16)
    block_output = (residual + contract_cols(hidden, mlp_params[3])).astype(jnp.bfloat16)
    out_back = cotangent[0]
    out_float = out_back.astype(jnp.float32)
    mlp_again = (
        lax.all_gather(mlp_gain, ("seq", "ctx"), axis=0, tiled=True),
        lax.all_gather(gate_weight, ("seq", "ctx"), axis=0, tiled=True),
        lax.all_gather(up_weight, ("seq", "ctx"), axis=0, tiled=True),
        lax.all_gather(down_weight, ("seq", "ctx"), axis=0, tiled=True),
    )
    down_grad = lax.psum_scatter(
        contract_rows(out_back, hidden), ("seq", "ctx"), scatter_dimension=0, tiled=True
    )
    hidden_back = jnp.dot(out_back, mlp_again[3], preferred_element_type=jnp.float32)
    gate_back = (
        hidden_back * up_proj * sigmoid_gate * (1.0 + gate_proj * (1.0 - sigmoid_gate))
    ).astype(jnp.bfloat16)
    upper_back = (hidden_back * silu_gate).astype(jnp.bfloat16)
    gate_full_grad = contract_rows(normed2, gate_back)
    up_full_grad = contract_rows(normed2, upper_back)
    normed2_back = contract_cols(gate_back, mlp_again[1]) + contract_cols(upper_back, mlp_again[2])
    residual_norm, mlp_gain_term = norm_back(
        residual, scale_two, mlp_again[0].astype(jnp.float32), normed2_back
    )
    mlp_sums = (
        lax.psum_scatter(mlp_gain_term, ("seq", "ctx"), scatter_dimension=0, tiled=True),
        lax.psum_scatter(gate_full_grad, ("seq", "ctx"), scatter_dimension=0, tiled=True),
        lax.psum_scatter(up_full_grad, ("seq", "ctx"), scatter_dimension=0, tiled=True),
    )
    residual_back = out_float + residual_norm
    attn_again = (
        lax.all_gather(attn_gain, ("seq", "ctx"), axis=0, tiled=True),
        lax.all_gather(query_weight, ("seq", "ctx"), axis=0, tiled=True),
        lax.all_gather(key_weight, ("seq", "ctx"), axis=0, tiled=True),
        lax.all_gather(value_weight, ("seq", "ctx"), axis=0, tiled=True),
        lax.all_gather(out_weight, ("seq", "ctx"), axis=0, tiled=True),
    )
    residual_low = residual_back.astype(jnp.bfloat16)
    out_full_grad = contract_rows(attn_low, residual_low)
    attn_back = contract_cols(residual_low, attn_again[4]).astype(jnp.bfloat16)
    grad_mix = attn_back.reshape(row_count, KV_HEADS, group_size, HEAD)
    delta_rows = jnp.transpose(jnp.sum(grad_mix.astype(jnp.float32) * full_mix, axis=-1), (1, 2, 0))

    def grad_step(carry, pieces):
        key_block, value_block, seg_block, block_start = pieces
        allowed = key_mask(seg_block, block_start)

        def compute(acc_query):
            soft_weights = block_soft(key_block, allowed)
            rounded = soft_weights.astype(jnp.bfloat16)
            value_part = jnp.einsum(
                "kgtj,tkgd->jkd", rounded, grad_mix, preferred_element_type=jnp.float32
            )
            soft_back = jnp.einsum(
                "tkgd,jkd->kgtj", grad_mix, value_block, preferred_element_type=jnp.float32
            )
            score_back = (soft_weights * (soft_back - delta_rows[..., None])).astype(jnp.bfloat16)
            acc_query = acc_query + jnp.einsum(
                "kgtj,jkd->tkgd", score_back, key_block, preferred_element_type=jnp.float32
            )
            key_part = jnp.einsum(
                "kgtj,tkgd->jkd", score_back, query_group, preferred_element_type=jnp.float32
            )
            return (acc_query, (key_part, value_part))

        return guarded(compute, carry)

    acc_query, (key_parts, value_parts) = lax.scan(
        grad_step, zero_mix, (key_blocks, value_blocks, seg_blocks, starts)
    )
    key_sums, value_sums = (
        lax.psum_scatter(
            key_parts.reshape(length, KV_HEADS * HEAD).astype(jnp.bfloat16),
            "ctx",
            scatter_dimension=0,
            tiled=True,
        ).astype(jnp.float32),
        lax.psum_scatter(
            value_parts.reshape(length, KV_HEADS * HEAD).astype(jnp.bfloat16),
            "ctx",
            scatter_dimension=0,
            tiled=True,
        ).astype(jnp.float32),
    )
    query_low = (
        rotate((acc_query * score_scale).reshape(row_count, HEADS, HEAD), cosine, -sine_table)
        .astype(jnp.bfloat16)
        .reshape(row_count, HEADS * HEAD)
    )
    key_low = (
        rotate((key_sums * score_scale).reshape(row_count, KV_HEADS, HEAD), cosine, -sine_table)
        .astype(jnp.bfloat16)
        .reshape(row_count, KV_HEADS * HEAD)
    )
    value_low = value_sums.astype(jnp.bfloat16)
    query_full_grad = contract_rows(normed1, query_low)
    key_full_grad = contract_rows(normed1, key_low)
    value_full_grad = contract_rows(normed1, value_low)
    normed1_back = (
        contract_cols(query_low, attn_again[1])
        + contract_cols(key_low, attn_again[2])
        + contract_cols(value_low, attn_again[3])
    )
    input_norm, attn_gain_term = norm_back(
        inputs, scale_one, attn_again[0].astype(jnp.float32), normed1_back
    )
    attn_sums = (
        lax.psum_scatter(attn_gain_term, ("seq", "ctx"), scatter_dimension=0, tiled=True),
        lax.psum_scatter(query_full_grad, ("seq", "ctx"), scatter_dimension=0, tiled=True),
        lax.psum_scatter(key_full_grad, ("seq", "ctx"), scatter_dimension=0, tiled=True),
        lax.psum_scatter(value_full_grad, ("seq", "ctx"), scatter_dimension=0, tiled=True),
        lax.psum_scatter(out_full_grad, ("seq", "ctx"), scatter_dimension=0, tiled=True),
    )
    input_grad = residual_back + input_norm
    return (
        block_output[None],
        input_grad[None],
        attn_sums[0],
        attn_sums[1],
        attn_sums[2],
        attn_sums[3],
        attn_sums[4],
        mlp_sums[0],
        mlp_sums[1],
        mlp_sums[2],
        down_grad,
    )


SEQ_X = [(0, 1), (1, 0), (2, 3), (3, 2)]
SEQ_Y = [(0, 2), (2, 0), (1, 3), (3, 1)]


def gather_ctx(block):
    return lax.all_gather(block, "ctx", axis=0, tiled=True)


def reduce_ctx(partial):
    return lax.psum_scatter(partial, "ctx", scatter_dimension=0, tiled=True)


def exchange_ctx(pieces):
    return lax.all_to_all(pieces, "ctx", 0, 0, tiled=True)


def gather_seq_near(block):
    return lax.ppermute(block, "seq", SEQ_X), lax.ppermute(block, "seq", SEQ_Y)


def gather_seq_far(block, from_x, from_y):
    rows, width = block.shape
    half = rows // 2
    mine = lax.axis_index("seq")
    far_top = lax.ppermute(from_x[:half], "seq", SEQ_Y)
    far_low = lax.ppermute(from_y[half:], "seq", SEQ_X)
    whole = jnp.zeros((4 * rows, width), block.dtype)
    for piece, start in (
        (block, mine * rows),
        (from_x, (mine ^ 1) * rows),
        (from_y, (mine ^ 2) * rows),
        (far_top, (mine ^ 3) * rows),
        (far_low, (mine ^ 3) * rows + half),
    ):
        whole = lax.dynamic_update_slice_in_dim(whole, piece, start, 0)
    return whole


def gather_seq(block):
    return gather_seq_far(block, *gather_seq_near(block))


def seq_part(partials, other, low):
    rows = partials[0].shape[0] // 4
    half = rows // 2
    start = (lax.axis_index("seq") ^ other) * rows + (half if low else 0)
    return jnp.concatenate(
        [lax.dynamic_slice_in_dim(partial, start, half, 0) for partial in partials], axis=1
    )


def seq_parts(partials):
    return (
        seq_part(partials, 3, False),
        seq_part(partials, 3, True),
        seq_part(partials, 1, False),
        seq_part(partials, 2, True),
    )


def send_parts(parts):
    return tuple(
        lax.ppermute(part, "seq", axis) for part, axis in zip(parts, (SEQ_X, SEQ_Y) * 2)
    )


def reduce_seq_near(partials):
    return send_parts(seq_parts(partials))


def add_wide(*terms):
    total = terms[0].astype(jnp.float32)
    for term in terms[1:]:
        total = total + term.astype(jnp.float32)
    return total


def far_sums(partials, top_far, low_far):
    return (
        add_wide(seq_part(partials, 2, False), top_far).astype(jnp.bfloat16),
        add_wide(seq_part(partials, 1, True), low_far).astype(jnp.bfloat16),
    )


def reduce_seq_far(partials, sums, top_near, low_near):
    top_send, low_send = sums
    top_last = lax.ppermute(top_send, "seq", SEQ_Y)
    low_last = lax.ppermute(low_send, "seq", SEQ_X)
    return jnp.concatenate(
        [
            add_wide(seq_part(partials, 0, False), top_near, top_last),
            add_wide(seq_part(partials, 0, True), low_near, low_last),
        ],
        axis=0,
    ).astype(jnp.bfloat16)


def reduce_seq(partials):
    top_far, low_far, *nears = reduce_seq_near(partials)
    return reduce_seq_far(partials, far_sums(partials, top_far, low_far), *nears)


def tie(*values):
    return lax.optimization_barrier(values)


def swap_cores(block):
    return lax.ppermute(block, "ctx", [(device, device ^ 1) for device in range(8)])


def ff_split(width):
    main = width // 8 // 128 * 128
    return main, width // 8 - main


def ff_slices(weight):
    rows, width = weight.shape
    main, tail = ff_split(width)
    return (
        jnp.transpose(weight[:, : 8 * main].reshape(rows, 8, main), (1, 0, 2)),
        jnp.transpose(weight[:, 8 * main :].reshape(rows, 8, tail), (1, 0, 2)),
    )


def ff_rows(main, tail):
    count, rows, width = main.shape
    return jnp.concatenate(
        [
            jnp.transpose(main, (1, 0, 2)).reshape(rows, count * width),
            jnp.transpose(tail, (1, 0, 2)).reshape(rows, count * tail.shape[2]),
        ],
        axis=1,
    )


def head_slices(weight):
    rows = weight.shape[0]
    split = weight.reshape(rows, KV_HEADS, 8, HEAD)
    return jnp.transpose(split, (2, 0, 1, 3)).reshape(8, rows, KV_HEADS * HEAD)


def from_head_slices(pieces):
    rows = pieces.shape[1]
    split = pieces.reshape(8, rows, KV_HEADS, HEAD)
    return jnp.transpose(split, (1, 2, 0, 3)).reshape(rows, HEADS * HEAD)


def attend_mask(edge, first_row, block, span):
    row = first_row + lax.broadcasted_iota(jnp.int32, (block, span), 0)
    column = lax.broadcasted_iota(jnp.int32, (block, span), 1)
    return (column <= row) & (column >= jnp.where(row >= edge, edge, 0))


def soft_rows(query, key, allowed):
    scores = lax.dot_general(
        query, key, (((1,), (1,)), ((), ())), preferred_element_type=jnp.float32
    )
    scores = jnp.where(allowed, scores, MASKED)
    exponents = jnp.exp(scores - jnp.max(scores, axis=-1, keepdims=True))
    return exponents * (1.0 / jnp.sum(exponents, axis=-1, keepdims=True))


def attend_kernel(edge_ref, query_ref, key_ref, value_ref, mix_ref, *, block, blocks):
    step = pl.program_id(1)
    for index in range(blocks):

        @pl.when(step == index)
        def _(index=index):
            span = (index + 1) * block
            allowed = attend_mask(edge_ref[0], index * block, block, span)
            mixed = []
            for head in range(2):
                cut = slice(head * HEAD, (head + 1) * HEAD)
                soft = soft_rows(query_ref[:, cut], key_ref[:span, cut], allowed)
                mixed.append(
                    jnp.dot(
                        soft.astype(jnp.bfloat16),
                        value_ref[:span, cut],
                        preferred_element_type=jnp.float32,
                    )
                )
            mix_ref[...] = jnp.concatenate(mixed, axis=-1).astype(mix_ref.dtype)


def attend_back_kernel(
    edge_ref,
    query_ref,
    key_ref,
    value_ref,
    back_ref,
    query_back_ref,
    key_back_ref,
    value_back_ref,
    *,
    block,
    blocks,
    score_scale,
):
    step = pl.program_id(1)

    @pl.when(step == 0)
    def _():
        key_back_ref[...] = jnp.zeros_like(key_back_ref)
        value_back_ref[...] = jnp.zeros_like(value_back_ref)

    for index in range(blocks):

        @pl.when(step == index)
        def _(index=index):
            span = (index + 1) * block
            allowed = attend_mask(edge_ref[0], index * block, block, span)
            query_parts, key_parts, value_parts = [], [], []
            for head in range(2):
                cut = slice(head * HEAD, (head + 1) * HEAD)
                query, key = query_ref[:, cut], key_ref[:span, cut]
                back = back_ref[:, cut]
                soft = soft_rows(query, key, allowed)
                soft_back = contract_cols(back, value_ref[:span, cut])
                delta = jnp.sum(soft * soft_back, axis=-1, keepdims=True)
                score_back = (soft * (soft_back - delta)).astype(jnp.bfloat16)
                query_parts.append(
                    jnp.dot(score_back, key, preferred_element_type=jnp.float32) * score_scale
                )
                key_parts.append(contract_rows(score_back, query))
                value_parts.append(contract_rows(soft.astype(jnp.bfloat16), back))
            query_back_ref[...] = jnp.concatenate(query_parts, axis=-1)
            key_back_ref[:span, :] += jnp.concatenate(key_parts, axis=-1)
            value_back_ref[:span, :] += jnp.concatenate(value_parts, axis=-1)


def attend_specs(length, block):
    rows = pl.BlockSpec((block, 2 * HEAD), lambda pair, step: (step, pair))
    whole = pl.BlockSpec((length, 2 * HEAD), lambda pair, step: (0, pair))
    edge = pl.BlockSpec(memory_space=pltpu.SMEM)
    return edge, rows, whole


def attend_cost(length, width, products):
    return pl.CostEstimate(
        flops=8 * products * length * length * width,
        transcendentals=length * length * width // HEAD,
        bytes_accessed=(2 * products + 4) * length * width,
    )


def attend(edge, queries, keys, values):
    length, width = queries.shape
    block = 256
    blocks = length // block
    scalar, rows, whole = attend_specs(length, block)

    def body(*refs):
        attend_kernel(*refs, block=block, blocks=blocks)

    return pl.pallas_call(
        body,
        name="attend",
        grid=(width // (2 * HEAD), blocks),
        in_specs=[scalar, rows, whole, whole],
        out_specs=rows,
        out_shape=jax.ShapeDtypeStruct((length, width), jnp.bfloat16),
        cost_estimate=attend_cost(length, width, 2),
    )(edge, queries, keys, values)


def attend_back(edge, queries, keys, values, back, score_scale):
    length, width = queries.shape
    block = 256
    blocks = length // block
    scalar, rows, whole = attend_specs(length, block)

    def body(*refs):
        attend_back_kernel(*refs, block=block, blocks=blocks, score_scale=score_scale)

    shape = jax.ShapeDtypeStruct((length, width), jnp.float32)
    return pl.pallas_call(
        body,
        name="attend_back",
        grid=(width // (2 * HEAD), blocks),
        in_specs=[scalar, rows, whole, whole, rows],
        out_specs=(rows, whole, whole),
        out_shape=(shape, shape, shape),
        cost_estimate=attend_cost(length, width, 5),
    )(edge, queries, keys, values, back)


def turn(values, cosine, sine_table):
    half = HEAD // 2
    lane = lax.broadcasted_iota(jnp.int32, values.shape, 1) % HEAD
    turned = jnp.where(
        lane < half, -jnp.roll(values, -half, axis=1), jnp.roll(values, half, axis=1)
    )
    return values * cosine + turned * sine_table


def local_columns(
    block_input,
    positions,
    segments,
    cotangent,
    attn_gain,
    query_weight,
    key_weight,
    value_weight,
    out_weight,
    mlp_gain,
    gate_weight,
    up_weight,
    down_weight,
):
    f32, bf16 = jnp.float32, jnp.bfloat16
    score_scale = HEAD ** (-0.5)
    length = segments.shape[1]
    rows = query_weight.shape[0]
    head_width = KV_HEADS * HEAD
    inputs = block_input[0].astype(f32)
    out_back = cotangent[0]
    gain_one = attn_gain.astype(f32)[:, None]
    gain_two = mlp_gain.astype(f32)[:, None]

    def fold(weight, gain):
        return (weight.astype(f32) * gain).astype(bf16)

    inputs_all = gather_ctx(block_input[0])
    key_value = jnp.stack([fold(key_weight, gain_one), fold(value_weight, gain_one)])
    attn_pieces = jnp.concatenate(
        [
            head_slices(fold(query_weight, gain_one)),
            jnp.tile(key_value, (4, 1, 1)),
        ],
        axis=2,
    )
    main, tail = ff_split(gate_weight.shape[1])
    both = 2 * (main + tail)
    gate_main, gate_tail = ff_slices(fold(gate_weight, gain_two))
    up_main, up_tail = ff_slices(fold(up_weight, gain_two))
    down_pieces = jnp.concatenate(ff_slices(down_weight), axis=2)
    gate_up_pieces = jnp.concatenate([gate_main, up_main, gate_tail, up_tail], axis=2)
    attn_own = exchange_ctx(attn_pieces).reshape(8 * rows, 2 * head_width)
    edge = jnp.sum((segments[0] == 0).astype(jnp.int32))
    token = jnp.arange(length, dtype=jnp.int32)
    position = jnp.where(token < edge, token + (length - edge), token - edge)
    cosine, sine_table = rope_tables(position, HEAD)
    cosine = jnp.tile(cosine, (1, KV_HEADS))
    sine_table = jnp.tile(sine_table, (1, KV_HEADS))
    edge = edge[None]
    attn_own, down_pieces, gate_up_pieces, cosine, sine_table = tie(
        attn_own, down_pieces, gate_up_pieces, cosine, sine_table
    )
    attn_cols = gather_seq(attn_own)
    core = lax.axis_index("ctx") % 2
    other_cols = swap_cores(attn_cols[:, head_width:])
    out_rows = gather_seq(out_weight)
    down_own = exchange_ctx(down_pieces).reshape(8 * rows, -1)
    down_own, gate_up_pieces = tie(down_own, gate_up_pieces)
    gate_up_own = exchange_ctx(gate_up_pieces).reshape(8 * rows, -1)

    wide = inputs_all.astype(f32)
    shaped_all = (wide * rms_scale(wide)).astype(bf16)
    raw = jnp.dot(shaped_all, attn_cols, preferred_element_type=f32)
    raw_other = jnp.dot(shaped_all, other_cols, preferred_element_type=f32)
    raw, raw_other, down_own = tie(raw, raw_other, down_own)
    raw_own = raw[:, head_width:]
    down_near = gather_seq_near(down_own)
    queries = turn(raw[:, :head_width], cosine, sine_table).astype(bf16)
    keys = turn(jnp.where(core == 0, raw_own, raw_other), cosine, sine_table).astype(bf16)
    values = jnp.where(core == 0, raw_other, raw_own).astype(bf16)
    queries = queries * jnp.asarray(score_scale, bf16)
    attn_low = attend(edge, queries, keys, values)
    attn_low, out_rows, back_late, gate_up_own, *down_near = tie(
        attn_low, out_rows, out_back, gate_up_own, *down_near
    )
    gate_up_near = gather_seq_near(gate_up_own)
    down_cols = gather_seq_far(down_own, *down_near)
    mixed = jnp.dot(attn_low, out_rows, preferred_element_type=f32).astype(bf16)
    mixed_own = reduce_ctx(mixed)
    mixed_own, down_cols, *gate_up_near = tie(mixed_own, down_cols, *gate_up_near)
    residual = inputs + mixed_own.astype(f32)
    scale_two = rms_scale(residual)
    shaped_two = residual * scale_two
    shaped_low = shaped_two.astype(bf16)
    normed_all = gather_ctx(shaped_low)
    shaped_two, back_late = tie(shaped_two, back_late)
    gate_up = gather_seq_far(gate_up_own, *gate_up_near)
    back_all = gather_ctx(back_late)
    proj = jnp.dot(normed_all, gate_up, preferred_element_type=f32)

    def halves(left_tail, right_tail, left, right):
        return jnp.concatenate([left, left_tail], axis=1), jnp.concatenate([right, right_tail], axis=1)

    gate_proj, up_proj = halves(
        proj[:, 2 * main : 2 * main + tail],
        proj[:, 2 * main + tail :],
        proj[:, :main],
        proj[:, main : 2 * main],
    )
    sigmoid_gate = jax.nn.sigmoid(gate_proj)
    silu_gate = gate_proj * sigmoid_gate
    hidden = (silu_gate * up_proj).astype(bf16)
    mixed_out = contract_cols(hidden, down_cols).astype(bf16)
    mixed_out, back_all = tie(mixed_out, back_all)
    out_own = reduce_ctx(mixed_out)
    hidden_back = jnp.dot(back_all, down_cols, preferred_element_type=f32)
    gate_back = (
        hidden_back * up_proj * sigmoid_gate * (1.0 + gate_proj * (1.0 - sigmoid_gate))
    ).astype(bf16)
    upper_back = (hidden_back * silu_gate).astype(bf16)
    gate_up_back = jnp.concatenate(
        [gate_back[:, :main], upper_back[:, :main], gate_back[:, main:], upper_back[:, main:]],
        axis=1,
    )
    weighted = reduce_ctx(contract_cols(gate_up_back, gate_up).astype(bf16))
    gate_up_grad = contract_rows(normed_all, gate_up_back).astype(bf16)
    down_grad = contract_rows(back_all, hidden).astype(bf16)
    mlp_grads = [gate_up_grad, down_grad]
    out_own, *mlp_parts = tie(out_own, *seq_parts(mlp_grads))
    mlp_near = send_parts(mlp_parts)
    weighted, *mlp_near = tie(weighted, *mlp_near)
    weighted = weighted.astype(f32)
    residual_back = out_back.astype(f32) + scale_two * (
        weighted - shaped_two * jnp.mean(weighted * shaped_two, axis=-1, keepdims=True)
    )
    residual_low = residual_back.astype(bf16)
    low_all = gather_ctx(residual_low)
    residual_back, *mlp_near = tie(residual_back, *mlp_near)
    mlp_sums = far_sums(mlp_grads, *mlp_near[:2])
    mlp_grads_own = reduce_seq_far(mlp_grads, mlp_sums, *mlp_near[2:])
    mlp_grad = exchange_ctx(mlp_grads_own.reshape(8, rows, -1))
    attn_back = contract_cols(low_all, out_rows).astype(bf16)
    query_back, key_back, value_back = attend_back(
        edge, queries, keys, values, attn_back, score_scale
    )
    key_low = turn(key_back, cosine, -sine_table).astype(bf16)
    value_low = value_back.astype(bf16)
    other_back = jnp.where(core == 0, value_low, key_low)
    other_part = contract_rows(shaped_all, other_back).astype(bf16)
    heads_back = jnp.concatenate(
        [
            turn(query_back, cosine, -sine_table).astype(bf16),
            jnp.where(core == 0, key_low, value_low),
        ],
        axis=1,
    )
    heads_back, other_part = tie(heads_back, other_part)
    other_part = swap_cores(other_part)
    weighted_part = contract_cols(
        jnp.concatenate([heads_back, other_back], axis=1),
        jnp.concatenate([attn_cols, other_cols], axis=1),
    ).astype(bf16)
    weighted_part, mlp_grad, other_part, low_all = tie(
        weighted_part, mlp_grad, other_part, low_all
    )
    weighted_one = reduce_ctx(weighted_part)
    attn_part = contract_rows(shaped_all, heads_back)
    own_part = attn_part[:, head_width:] + other_part.astype(f32)
    attn_grad_own = reduce_seq(
        [jnp.concatenate([attn_part[:, :head_width].astype(bf16), own_part.astype(bf16)], axis=1)]
    )
    out_grad = reduce_seq([contract_rows(attn_low, low_all).astype(bf16)]).astype(f32)
    attn_grad_own, mlp_grad = tie(attn_grad_own, mlp_grad)
    mlp_grad = mlp_grad.astype(f32)
    attn_grad = exchange_ctx(attn_grad_own.reshape(8, rows, -1))

    gate_rows = ff_rows(mlp_grad[:, :, :main], mlp_grad[:, :, 2 * main : 2 * main + tail])
    up_rows = ff_rows(mlp_grad[:, :, main : 2 * main], mlp_grad[:, :, 2 * main + tail : both])
    down_grad = ff_rows(mlp_grad[:, :, both : both + main], mlp_grad[:, :, both + main :])
    block_output = (residual + out_own.astype(f32)).astype(bf16)
    attn_grad, out_grad, gate_rows, up_rows, down_grad, block_output = tie(
        attn_grad, out_grad, gate_rows, up_rows, down_grad, block_output
    )
    attn_grad = attn_grad.astype(f32)
    query_rows = from_head_slices(attn_grad[:, :, :head_width])
    pair_rows = jnp.sum(attn_grad[:, :, head_width:].reshape(4, 2, rows, head_width), axis=0)
    key_rows, value_rows = pair_rows[0], pair_rows[1]

    def row_sum(weight, grad):
        return jnp.sum(weight.astype(f32) * grad, axis=1)

    attn_gain_grad = (
        row_sum(query_weight, query_rows)
        + row_sum(key_weight, key_rows)
        + row_sum(value_weight, value_rows)
    )
    mlp_gain_grad = row_sum(gate_weight, gate_rows) + row_sum(up_weight, up_rows)
    weighted_one, attn_gain_grad = tie(weighted_one, attn_gain_grad)
    weighted_one = weighted_one.astype(f32)
    scale_one = rms_scale(inputs)
    shaped_one = inputs * scale_one
    input_grad = residual_back + scale_one * (
        weighted_one - shaped_one * jnp.mean(weighted_one * shaped_one, axis=-1, keepdims=True)
    )
    return (
        block_output[None],
        input_grad[None],
        attn_gain_grad,
        query_rows * gain_one,
        key_rows * gain_one,
        value_rows * gain_one,
        out_grad,
        mlp_gain_grad,
        gate_rows * gain_two,
        up_rows * gain_two,
        down_grad,
    )


def solution(mesh):
    placed = (
        P("seq", "ctx", None),
        P("seq", "ctx"),
        P("seq", None),
        P("seq", "ctx", None),
        P(("seq", "ctx")),
        P(("seq", "ctx"), None),
        P(("seq", "ctx"), None),
        P(("seq", "ctx"), None),
        P(("seq", "ctx"), None),
        P(("seq", "ctx")),
        P(("seq", "ctx"), None),
        P(("seq", "ctx"), None),
        P(("seq", "ctx"), None),
    )
    seq_count, ctx_count = mesh.shape["seq"], mesh.shape["ctx"]

    def run(*args):
        width = args[0].shape[2]
        fits = (
            seq_count == KV_HEADS == 4
            and ctx_count == HEADS // KV_HEADS == 8
            and width == seq_count * ctx_count * HEAD
        )
        return jax.shard_map(
            local_columns if fits else local_rows,
            mesh=mesh,
            in_specs=placed,
            out_specs=(
                P("seq", "ctx", None),
                P("seq", "ctx", None),
                P(("seq", "ctx")),
                P(("seq", "ctx"), None),
                P(("seq", "ctx"), None),
                P(("seq", "ctx"), None),
                P(("seq", "ctx"), None),
                P(("seq", "ctx")),
                P(("seq", "ctx"), None),
                P(("seq", "ctx"), None),
                P(("seq", "ctx"), None),
            ),
            check_vma=False,
        )(*args)

    return run
```

```python
import jax
import jax.numpy as jnp
from jax import lax
from jax.experimental import pallas as pl
from jax.experimental.pallas import tpu as pltpu
from jax.sharding import PartitionSpec as P

HEADS = 32
KV_HEADS = 4
HEAD = 64


EPSILON = 1e-05
MASKED = -1e30


def rope_tables(position, head_size):
    half_size = head_size // 2
    inverse = 1.0 / 10000.0 ** (jnp.arange(half_size, dtype=jnp.float32) * 2.0 / head_size)
    angles = position.astype(jnp.float32)[:, None] * inverse[None, :]
    cosine = jnp.cos(angles)
    sine_table = jnp.sin(angles)
    return (jnp.concatenate([cosine, cosine], -1), jnp.concatenate([sine_table, sine_table], -1))


def rotate(values, cosine, sine_table):
    half_size = values.shape[-1] // 2
    turned = jnp.concatenate([-values[..., half_size:], values[..., :half_size]], -1)
    return values * cosine[:, None, :] + turned * sine_table[:, None, :]


def rms_scale(inputs):
    return lax.rsqrt(jnp.mean(inputs * inputs, axis=-1, keepdims=True) + EPSILON)


def norm_back(inputs, row_scale, gain, upstream):
    shaped = inputs * row_scale
    weighted = upstream * gain
    gain_term = jnp.sum(upstream * shaped, axis=0)
    return (
        row_scale * (weighted - shaped * jnp.mean(weighted * shaped, axis=-1, keepdims=True)),
        gain_term,
    )


def contract_rows(left, right):
    return lax.dot_general(
        left, right, (((0,), (0,)), ((), ())), preferred_element_type=jnp.float32
    )


def contract_cols(left, right):
    return lax.dot_general(
        left, right, (((1,), (1,)), ((), ())), preferred_element_type=jnp.float32
    )


def local_rows(
    block_input,
    positions,
    segments,
    cotangent,
    attn_gain,
    query_weight,
    key_weight,
    value_weight,
    out_weight,
    mlp_gain,
    gate_weight,
    up_weight,
    down_weight,
):
    row_count = block_input.shape[1]
    group_size = HEADS // KV_HEADS
    score_scale = HEAD ** (-0.5)
    inputs = block_input[0].astype(jnp.float32)
    seg_all = segments[0]
    length = seg_all.shape[0]
    block_size = min(512, length)
    block_count = length // block_size
    first_row = lax.axis_index("ctx") * row_count
    query_index = first_row + jnp.arange(row_count, dtype=jnp.int32)
    seg_rows = lax.dynamic_slice_in_dim(seg_all, first_row, row_count)
    cosine, sine_table = rope_tables(positions[0], HEAD)
    starts = jnp.arange(block_count, dtype=jnp.int32) * block_size
    seg_blocks = seg_all.reshape(block_count, block_size)

    def key_mask(seg_block, block_start):
        key_index = block_start + jnp.arange(block_size, dtype=jnp.int32)
        return (seg_rows[:, None] == seg_block[None, :]) & (
            key_index[None, :] <= query_index[:, None]
        )

    def guarded(compute, running):
        result = compute(running)
        return result

    attn_params = (
        lax.all_gather(attn_gain, ("seq", "ctx"), axis=0, tiled=True),
        lax.all_gather(query_weight, ("seq", "ctx"), axis=0, tiled=True),
        lax.all_gather(key_weight, ("seq", "ctx"), axis=0, tiled=True),
        lax.all_gather(value_weight, ("seq", "ctx"), axis=0, tiled=True),
        lax.all_gather(out_weight, ("seq", "ctx"), axis=0, tiled=True),
    )
    gain_one = attn_params[0].astype(jnp.float32)
    scale_one = rms_scale(inputs)
    normed1 = (inputs * scale_one * gain_one).astype(jnp.bfloat16)
    query_raw = jnp.dot(normed1, attn_params[1], preferred_element_type=jnp.float32)
    key_raw = jnp.dot(normed1, attn_params[2], preferred_element_type=jnp.float32)
    value_raw = jnp.dot(normed1, attn_params[3], preferred_element_type=jnp.float32)
    queries = rotate(query_raw.reshape(row_count, HEADS, HEAD), cosine, sine_table).astype(
        jnp.bfloat16
    )
    keys_local = (
        rotate(key_raw.reshape(row_count, KV_HEADS, HEAD), cosine, sine_table)
        .astype(jnp.bfloat16)
        .reshape(row_count, KV_HEADS * HEAD)
    )
    values_local = value_raw.astype(jnp.bfloat16)
    keys_all, values_all = (
        lax.all_gather(keys_local, "ctx", axis=0, tiled=True),
        lax.all_gather(values_local, "ctx", axis=0, tiled=True),
    )
    key_blocks = keys_all.reshape(block_count, block_size, KV_HEADS, HEAD)
    value_blocks = values_all.reshape(block_count, block_size, KV_HEADS, HEAD)
    query_group = queries.reshape(row_count, KV_HEADS, group_size, HEAD)

    def block_scores(key_block, allowed):
        scores = (
            jnp.einsum("tkgd,jkd->kgtj", query_group, key_block, preferred_element_type=jnp.float32)
            * score_scale
        )
        return jnp.where(allowed[None, None], scores, MASKED)

    def max_step(carry, pieces):
        key_block, seg_block, block_start = pieces
        allowed = key_mask(seg_block, block_start)

        def compute(running):
            run_max, run_sum = running
            scores = block_scores(key_block, allowed)
            new_max = jnp.maximum(run_max, jnp.max(scores, axis=-1))
            exponents = jnp.where(allowed[None, None], jnp.exp(scores - new_max[..., None]), 0.0)
            return (new_max, run_sum * jnp.exp(run_max - new_max) + jnp.sum(exponents, axis=-1))

        return (guarded(compute, carry), None)

    start_max = jnp.full((KV_HEADS, group_size, row_count), MASKED, jnp.float32)
    start_sum = jnp.zeros((KV_HEADS, group_size, row_count), jnp.float32)
    (run_max, run_sum), unused = lax.scan(
        max_step, (start_max, start_sum), (key_blocks, seg_blocks, starts)
    )
    log_sum = run_max + jnp.log(run_sum)

    def block_soft(key_block, allowed):
        scores = block_scores(key_block, allowed)
        return jnp.where(allowed[None, None], jnp.exp(scores - log_sum[..., None]), 0.0)

    def value_step(carry, pieces):
        key_block, value_block, seg_block, block_start = pieces
        allowed = key_mask(seg_block, block_start)

        def compute(running):
            acc_out, acc_fix = running
            soft_weights = block_soft(key_block, allowed)
            rounded = soft_weights.astype(jnp.bfloat16)
            leftover = (soft_weights - rounded.astype(jnp.float32)).astype(jnp.bfloat16)
            acc_out = acc_out + jnp.einsum(
                "kgtj,jkd->tkgd", rounded, value_block, preferred_element_type=jnp.float32
            )
            acc_fix = acc_fix + jnp.einsum(
                "kgtj,jkd->tkgd", leftover, value_block, preferred_element_type=jnp.float32
            )
            return (acc_out, acc_fix)

        return (guarded(compute, carry), None)

    zero_mix = jnp.zeros((row_count, KV_HEADS, group_size, HEAD), jnp.float32)
    (acc_out, acc_fix), unused = lax.scan(
        value_step, (zero_mix, zero_mix), (key_blocks, value_blocks, seg_blocks, starts)
    )
    attn_low = acc_out.reshape(row_count, HEADS * HEAD).astype(jnp.bfloat16)
    full_mix = acc_out + acc_fix
    residual = inputs + jnp.dot(attn_low, attn_params[4], preferred_element_type=jnp.float32)
    mlp_params = (
        lax.all_gather(mlp_gain, ("seq", "ctx"), axis=0, tiled=True),
        lax.all_gather(gate_weight, ("seq", "ctx"), axis=0, tiled=True),
        lax.all_gather(up_weight, ("seq", "ctx"), axis=0, tiled=True),
        lax.all_gather(down_weight, ("seq", "ctx"), axis=0, tiled=True),
    )
    gain_two = mlp_params[0].astype(jnp.float32)
    scale_two = rms_scale(residual)
    normed2 = (residual * scale_two * gain_two).astype(jnp.bfloat16)
    gate_proj = jnp.dot(normed2, mlp_params[1], preferred_element_type=jnp.float32)
    up_proj = jnp.dot(normed2, mlp_params[2], preferred_element_type=jnp.float32)
    sigmoid_gate = jax.nn.sigmoid(gate_proj)
    silu_gate = gate_proj * sigmoid_gate
    hidden = (silu_gate * up_proj).astype(jnp.bfloat16)
    block_output = (residual + contract_cols(hidden, mlp_params[3])).astype(jnp.bfloat16)
    out_back = cotangent[0]
    out_float = out_back.astype(jnp.float32)
    mlp_again = (
        lax.all_gather(mlp_gain, ("seq", "ctx"), axis=0, tiled=True),
        lax.all_gather(gate_weight, ("seq", "ctx"), axis=0, tiled=True),
        lax.all_gather(up_weight, ("seq", "ctx"), axis=0, tiled=True),
        lax.all_gather(down_weight, ("seq", "ctx"), axis=0, tiled=True),
    )
    down_grad = lax.psum_scatter(
        contract_rows(out_back, hidden), ("seq", "ctx"), scatter_dimension=0, tiled=True
    )
    hidden_back = jnp.dot(out_back, mlp_again[3], preferred_element_type=jnp.float32)
    gate_back = (
        hidden_back * up_proj * sigmoid_gate * (1.0 + gate_proj * (1.0 - sigmoid_gate))
    ).astype(jnp.bfloat16)
    upper_back = (hidden_back * silu_gate).astype(jnp.bfloat16)
    gate_full_grad = contract_rows(normed2, gate_back)
    up_full_grad = contract_rows(normed2, upper_back)
    normed2_back = contract_cols(gate_back, mlp_again[1]) + contract_cols(upper_back, mlp_again[2])
    residual_norm, mlp_gain_term = norm_back(
        residual, scale_two, mlp_again[0].astype(jnp.float32), normed2_back
    )
    mlp_sums = (
        lax.psum_scatter(mlp_gain_term, ("seq", "ctx"), scatter_dimension=0, tiled=True),
        lax.psum_scatter(gate_full_grad, ("seq", "ctx"), scatter_dimension=0, tiled=True),
        lax.psum_scatter(up_full_grad, ("seq", "ctx"), scatter_dimension=0, tiled=True),
    )
    residual_back = out_float + residual_norm
    attn_again = (
        lax.all_gather(attn_gain, ("seq", "ctx"), axis=0, tiled=True),
        lax.all_gather(query_weight, ("seq", "ctx"), axis=0, tiled=True),
        lax.all_gather(key_weight, ("seq", "ctx"), axis=0, tiled=True),
        lax.all_gather(value_weight, ("seq", "ctx"), axis=0, tiled=True),
        lax.all_gather(out_weight, ("seq", "ctx"), axis=0, tiled=True),
    )
    residual_low = residual_back.astype(jnp.bfloat16)
    out_full_grad = contract_rows(attn_low, residual_low)
    attn_back = contract_cols(residual_low, attn_again[4]).astype(jnp.bfloat16)
    grad_mix = attn_back.reshape(row_count, KV_HEADS, group_size, HEAD)
    delta_rows = jnp.transpose(jnp.sum(grad_mix.astype(jnp.float32) * full_mix, axis=-1), (1, 2, 0))

    def grad_step(carry, pieces):
        key_block, value_block, seg_block, block_start = pieces
        allowed = key_mask(seg_block, block_start)

        def compute(acc_query):
            soft_weights = block_soft(key_block, allowed)
            rounded = soft_weights.astype(jnp.bfloat16)
            value_part = jnp.einsum(
                "kgtj,tkgd->jkd", rounded, grad_mix, preferred_element_type=jnp.float32
            )
            soft_back = jnp.einsum(
                "tkgd,jkd->kgtj", grad_mix, value_block, preferred_element_type=jnp.float32
            )
            score_back = (soft_weights * (soft_back - delta_rows[..., None])).astype(jnp.bfloat16)
            acc_query = acc_query + jnp.einsum(
                "kgtj,jkd->tkgd", score_back, key_block, preferred_element_type=jnp.float32
            )
            key_part = jnp.einsum(
                "kgtj,tkgd->jkd", score_back, query_group, preferred_element_type=jnp.float32
            )
            return (acc_query, (key_part, value_part))

        return guarded(compute, carry)

    acc_query, (key_parts, value_parts) = lax.scan(
        grad_step, zero_mix, (key_blocks, value_blocks, seg_blocks, starts)
    )
    key_sums, value_sums = (
        lax.psum_scatter(
            key_parts.reshape(length, KV_HEADS * HEAD).astype(jnp.bfloat16),
            "ctx",
            scatter_dimension=0,
            tiled=True,
        ).astype(jnp.float32),
        lax.psum_scatter(
            value_parts.reshape(length, KV_HEADS * HEAD).astype(jnp.bfloat16),
            "ctx",
            scatter_dimension=0,
            tiled=True,
        ).astype(jnp.float32),
    )
    query_low = (
        rotate((acc_query * score_scale).reshape(row_count, HEADS, HEAD), cosine, -sine_table)
        .astype(jnp.bfloat16)
        .reshape(row_count, HEADS * HEAD)
    )
    key_low = (
        rotate((key_sums * score_scale).reshape(row_count, KV_HEADS, HEAD), cosine, -sine_table)
        .astype(jnp.bfloat16)
        .reshape(row_count, KV_HEADS * HEAD)
    )
    value_low = value_sums.astype(jnp.bfloat16)
    query_full_grad = contract_rows(normed1, query_low)
    key_full_grad = contract_rows(normed1, key_low)
    value_full_grad = contract_rows(normed1, value_low)
    normed1_back = (
        contract_cols(query_low, attn_again[1])
        + contract_cols(key_low, attn_again[2])
        + contract_cols(value_low, attn_again[3])
    )
    input_norm, attn_gain_term = norm_back(
        inputs, scale_one, attn_again[0].astype(jnp.float32), normed1_back
    )
    attn_sums = (
        lax.psum_scatter(attn_gain_term, ("seq", "ctx"), scatter_dimension=0, tiled=True),
        lax.psum_scatter(query_full_grad, ("seq", "ctx"), scatter_dimension=0, tiled=True),
        lax.psum_scatter(key_full_grad, ("seq", "ctx"), scatter_dimension=0, tiled=True),
        lax.psum_scatter(value_full_grad, ("seq", "ctx"), scatter_dimension=0, tiled=True),
        lax.psum_scatter(out_full_grad, ("seq", "ctx"), scatter_dimension=0, tiled=True),
    )
    input_grad = residual_back + input_norm
    return (
        block_output[None],
        input_grad[None],
        attn_sums[0],
        attn_sums[1],
        attn_sums[2],
        attn_sums[3],
        attn_sums[4],
        mlp_sums[0],
        mlp_sums[1],
        mlp_sums[2],
        down_grad,
    )


SEQ_X = [(0, 1), (1, 0), (2, 3), (3, 2)]
SEQ_Y = [(0, 2), (2, 0), (1, 3), (3, 1)]


def gather_ctx(block):
    return lax.all_gather(block, "ctx", axis=0, tiled=True)


def reduce_ctx(partial):
    return lax.psum_scatter(partial, "ctx", scatter_dimension=0, tiled=True)


def exchange_ctx(pieces):
    return lax.all_to_all(pieces, "ctx", 0, 0, tiled=True)


def gather_seq_near(block):
    return lax.ppermute(block, "seq", SEQ_X), lax.ppermute(block, "seq", SEQ_Y)


def gather_seq_far(block, from_x, from_y):
    rows, width = block.shape
    half = rows // 2
    mine = lax.axis_index("seq")
    far_top = lax.ppermute(from_x[:half], "seq", SEQ_Y)
    far_low = lax.ppermute(from_y[half:], "seq", SEQ_X)
    whole = jnp.zeros((4 * rows, width), block.dtype)
    for piece, start in (
        (block, mine * rows),
        (from_x, (mine ^ 1) * rows),
        (from_y, (mine ^ 2) * rows),
        (far_top, (mine ^ 3) * rows),
        (far_low, (mine ^ 3) * rows + half),
    ):
        whole = lax.dynamic_update_slice_in_dim(whole, piece, start, 0)
    return whole


def gather_seq(block):
    return gather_seq_far(block, *gather_seq_near(block))


def seq_part(partials, other, low):
    rows = partials[0].shape[0] // 4
    half = rows // 2
    start = (lax.axis_index("seq") ^ other) * rows + (half if low else 0)
    return jnp.concatenate(
        [lax.dynamic_slice_in_dim(partial, start, half, 0) for partial in partials], axis=1
    )


def seq_parts(partials):
    return (
        seq_part(partials, 3, False),
        seq_part(partials, 3, True),
        seq_part(partials, 1, False),
        seq_part(partials, 2, True),
    )


def send_parts(parts):
    return tuple(
        lax.ppermute(part, "seq", axis) for part, axis in zip(parts, (SEQ_X, SEQ_Y) * 2)
    )


def reduce_seq_near(partials):
    return send_parts(seq_parts(partials))


def add_wide(*terms):
    total = terms[0].astype(jnp.float32)
    for term in terms[1:]:
        total = total + term.astype(jnp.float32)
    return total


def far_sums(partials, top_far, low_far):
    return (
        add_wide(seq_part(partials, 2, False), top_far).astype(jnp.bfloat16),
        add_wide(seq_part(partials, 1, True), low_far).astype(jnp.bfloat16),
    )


def reduce_seq_far(partials, sums, top_near, low_near):
    top_send, low_send = sums
    top_last = lax.ppermute(top_send, "seq", SEQ_Y)
    low_last = lax.ppermute(low_send, "seq", SEQ_X)
    return jnp.concatenate(
        [
            add_wide(seq_part(partials, 0, False), top_near, top_last),
            add_wide(seq_part(partials, 0, True), low_near, low_last),
        ],
        axis=0,
    ).astype(jnp.bfloat16)


def reduce_seq(partials):
    top_far, low_far, *nears = reduce_seq_near(partials)
    return reduce_seq_far(partials, far_sums(partials, top_far, low_far), *nears)


def tie(*values):
    return lax.optimization_barrier(values)


def swap_cores(block):
    return lax.ppermute(block, "ctx", [(device, device ^ 1) for device in range(8)])


def ff_split(width):
    main = width // 8 // 128 * 128
    return main, width // 8 - main


def ff_slices(weight):
    rows, width = weight.shape
    main, tail = ff_split(width)
    return (
        jnp.transpose(weight[:, : 8 * main].reshape(rows, 8, main), (1, 0, 2)),
        jnp.transpose(weight[:, 8 * main :].reshape(rows, 8, tail), (1, 0, 2)),
    )


def ff_rows(main, tail):
    count, rows, width = main.shape
    return jnp.concatenate(
        [
            jnp.transpose(main, (1, 0, 2)).reshape(rows, count * width),
            jnp.transpose(tail, (1, 0, 2)).reshape(rows, count * tail.shape[2]),
        ],
        axis=1,
    )


def head_slices(weight):
    rows = weight.shape[0]
    split = weight.reshape(rows, KV_HEADS, 8, HEAD)
    return jnp.transpose(split, (2, 0, 1, 3)).reshape(8, rows, KV_HEADS * HEAD)


def from_head_slices(pieces):
    rows = pieces.shape[1]
    split = pieces.reshape(8, rows, KV_HEADS, HEAD)
    return jnp.transpose(split, (1, 2, 0, 3)).reshape(rows, HEADS * HEAD)


def attend_mask(edge, first_row, block, span):
    row = first_row + lax.broadcasted_iota(jnp.int32, (block, span), 0)
    column = lax.broadcasted_iota(jnp.int32, (block, span), 1)
    return (column <= row) & (column >= jnp.where(row >= edge, edge, 0))


def soft_rows(query, key, allowed):
    scores = lax.dot_general(
        query, key, (((1,), (1,)), ((), ())), preferred_element_type=jnp.float32
    )
    scores = jnp.where(allowed, scores, MASKED)
    exponents = jnp.exp(scores - jnp.max(scores, axis=-1, keepdims=True))
    return exponents * (1.0 / jnp.sum(exponents, axis=-1, keepdims=True))


def attend_kernel(edge_ref, query_ref, key_ref, value_ref, mix_ref, *, block, blocks):
    step = pl.program_id(1)
    for index in range(blocks):

        @pl.when(step == index)
        def _(index=index):
            span = (index + 1) * block
            allowed = attend_mask(edge_ref[0], index * block, block, span)
            mixed = []
            for head in range(2):
                cut = slice(head * HEAD, (head + 1) * HEAD)
                soft = soft_rows(query_ref[:, cut], key_ref[:span, cut], allowed)
                mixed.append(
                    jnp.dot(
                        soft.astype(jnp.bfloat16),
                        value_ref[:span, cut],
                        preferred_element_type=jnp.float32,
                    )
                )
            mix_ref[...] = jnp.concatenate(mixed, axis=-1).astype(mix_ref.dtype)


def attend_back_kernel(
    edge_ref,
    query_ref,
    key_ref,
    value_ref,
    back_ref,
    query_back_ref,
    key_back_ref,
    value_back_ref,
    *,
    block,
    blocks,
    score_scale,
):
    step = pl.program_id(1)

    @pl.when(step == 0)
    def _():
        key_back_ref[...] = jnp.zeros_like(key_back_ref)
        value_back_ref[...] = jnp.zeros_like(value_back_ref)

    for index in range(blocks):

        @pl.when(step == index)
        def _(index=index):
            span = (index + 1) * block
            allowed = attend_mask(edge_ref[0], index * block, block, span)
            query_parts, key_parts, value_parts = [], [], []
            for head in range(2):
                cut = slice(head * HEAD, (head + 1) * HEAD)
                query, key = query_ref[:, cut], key_ref[:span, cut]
                back = back_ref[:, cut]
                soft = soft_rows(query, key, allowed)
                soft_back = contract_cols(back, value_ref[:span, cut])
                delta = jnp.sum(soft * soft_back, axis=-1, keepdims=True)
                score_back = (soft * (soft_back - delta)).astype(jnp.bfloat16)
                query_parts.append(
                    jnp.dot(score_back, key, preferred_element_type=jnp.float32) * score_scale
                )
                key_parts.append(contract_rows(score_back, query))
                value_parts.append(contract_rows(soft.astype(jnp.bfloat16), back))
            query_back_ref[...] = jnp.concatenate(query_parts, axis=-1)
            key_back_ref[:span, :] += jnp.concatenate(key_parts, axis=-1)
            value_back_ref[:span, :] += jnp.concatenate(value_parts, axis=-1)


def attend_specs(length, block):
    rows = pl.BlockSpec((block, 2 * HEAD), lambda pair, step: (step, pair))
    whole = pl.BlockSpec((length, 2 * HEAD), lambda pair, step: (0, pair))
    edge = pl.BlockSpec(memory_space=pltpu.SMEM)
    return edge, rows, whole


def attend_cost(length, width, products):
    return pl.CostEstimate(
        flops=8 * products * length * length * width,
        transcendentals=length * length * width // HEAD,
        bytes_accessed=(2 * products + 4) * length * width,
    )


def attend(edge, queries, keys, values):
    length, width = queries.shape
    block = 256
    blocks = length // block
    scalar, rows, whole = attend_specs(length, block)

    def body(*refs):
        attend_kernel(*refs, block=block, blocks=blocks)

    return pl.pallas_call(
        body,
        name="attend",
        grid=(width // (2 * HEAD), blocks),
        in_specs=[scalar, rows, whole, whole],
        out_specs=rows,
        out_shape=jax.ShapeDtypeStruct((length, width), jnp.bfloat16),
        cost_estimate=attend_cost(length, width, 2),
    )(edge, queries, keys, values)


def attend_back(edge, queries, keys, values, back, score_scale):
    length, width = queries.shape
    block = 256
    blocks = length // block
    scalar, rows, whole = attend_specs(length, block)

    def body(*refs):
        attend_back_kernel(*refs, block=block, blocks=blocks, score_scale=score_scale)

    shape = jax.ShapeDtypeStruct((length, width), jnp.float32)
    return pl.pallas_call(
        body,
        name="attend_back",
        grid=(width // (2 * HEAD), blocks),
        in_specs=[scalar, rows, whole, whole, rows],
        out_specs=(rows, whole, whole),
        out_shape=(shape, shape, shape),
        cost_estimate=attend_cost(length, width, 5),
    )(edge, queries, keys, values, back)


def turn(values, cosine, sine_table):
    half = HEAD // 2
    lane = lax.broadcasted_iota(jnp.int32, values.shape, 1) % HEAD
    turned = jnp.where(
        lane < half, -jnp.roll(values, -half, axis=1), jnp.roll(values, half, axis=1)
    )
    return values * cosine + turned * sine_table


def local_columns(
    block_input,
    positions,
    segments,
    cotangent,
    attn_gain,
    query_weight,
    key_weight,
    value_weight,
    out_weight,
    mlp_gain,
    gate_weight,
    up_weight,
    down_weight,
):
    f32, bf16 = jnp.float32, jnp.bfloat16
    score_scale = HEAD ** (-0.5)
    length = segments.shape[1]
    rows = query_weight.shape[0]
    head_width = KV_HEADS * HEAD
    inputs = block_input[0].astype(f32)
    out_back = cotangent[0]
    gain_one = attn_gain.astype(f32)[:, None]
    gain_two = mlp_gain.astype(f32)[:, None]

    def fold(weight, gain):
        return (weight.astype(f32) * gain).astype(bf16)

    inputs_all = gather_ctx(block_input[0])
    key_value = jnp.stack([fold(key_weight, gain_one), fold(value_weight, gain_one)])
    attn_pieces = jnp.concatenate(
        [
            head_slices(fold(query_weight, gain_one)),
            jnp.tile(key_value, (4, 1, 1)),
        ],
        axis=2,
    )
    main, tail = ff_split(gate_weight.shape[1])
    both = 2 * (main + tail)
    gate_main, gate_tail = ff_slices(fold(gate_weight, gain_two))
    up_main, up_tail = ff_slices(fold(up_weight, gain_two))
    down_pieces = jnp.concatenate(ff_slices(down_weight), axis=2)
    gate_up_pieces = jnp.concatenate([gate_main, up_main, gate_tail, up_tail], axis=2)
    attn_own = exchange_ctx(attn_pieces).reshape(8 * rows, 2 * head_width)
    edge = jnp.sum((segments[0] == 0).astype(jnp.int32))
    token = jnp.arange(length, dtype=jnp.int32)
    position = jnp.where(token < edge, token + (length - edge), token - edge)
    cosine, sine_table = rope_tables(position, HEAD)
    cosine = jnp.tile(cosine, (1, KV_HEADS))
    sine_table = jnp.tile(sine_table, (1, KV_HEADS))
    edge = edge[None]
    attn_own, down_pieces, gate_up_pieces, cosine, sine_table = tie(
        attn_own, down_pieces, gate_up_pieces, cosine, sine_table
    )
    attn_cols = gather_seq(attn_own)
    core = lax.axis_index("ctx") % 2
    other_cols = swap_cores(attn_cols[:, head_width:])
    out_rows = gather_seq(out_weight)
    down_own = exchange_ctx(down_pieces).reshape(8 * rows, -1)
    down_own, gate_up_pieces = tie(down_own, gate_up_pieces)
    gate_up_own = exchange_ctx(gate_up_pieces).reshape(8 * rows, -1)

    wide = inputs_all.astype(f32)
    shaped_all = (wide * rms_scale(wide)).astype(bf16)
    raw = jnp.dot(shaped_all, attn_cols, preferred_element_type=f32)
    raw_other = jnp.dot(shaped_all, other_cols, preferred_element_type=f32)
    raw, raw_other, down_own = tie(raw, raw_other, down_own)
    raw_own = raw[:, head_width:]
    down_near = gather_seq_near(down_own)
    queries = turn(raw[:, :head_width], cosine, sine_table).astype(bf16)
    keys = turn(jnp.where(core == 0, raw_own, raw_other), cosine, sine_table).astype(bf16)
    values = jnp.where(core == 0, raw_other, raw_own).astype(bf16)
    queries = queries * jnp.asarray(score_scale, bf16)
    attn_low = attend(edge, queries, keys, values)
    attn_low, out_rows, back_late, gate_up_own, *down_near = tie(
        attn_low, out_rows, out_back, gate_up_own, *down_near
    )
    gate_up_near = gather_seq_near(gate_up_own)
    down_cols = gather_seq_far(down_own, *down_near)
    mixed = jnp.dot(attn_low, out_rows, preferred_element_type=f32).astype(bf16)
    mixed_own = reduce_ctx(mixed)
    mixed_own, down_cols, *gate_up_near = tie(mixed_own, down_cols, *gate_up_near)
    residual = inputs + mixed_own.astype(f32)
    scale_two = rms_scale(residual)
    shaped_two = residual * scale_two
    shaped_low = shaped_two.astype(bf16)
    normed_all = gather_ctx(shaped_low)
    shaped_two, back_late = tie(shaped_two, back_late)
    gate_up = gather_seq_far(gate_up_own, *gate_up_near)
    back_all = gather_ctx(back_late)
    proj = jnp.dot(normed_all, gate_up, preferred_element_type=f32)

    def halves(left_tail, right_tail, left, right):
        return jnp.concatenate([left, left_tail], axis=1), jnp.concatenate([right, right_tail], axis=1)

    gate_proj, up_proj = halves(
        proj[:, 2 * main : 2 * main + tail],
        proj[:, 2 * main + tail :],
        proj[:, :main],
        proj[:, main : 2 * main],
    )
    sigmoid_gate = jax.nn.sigmoid(gate_proj)
    silu_gate = gate_proj * sigmoid_gate
    hidden = (silu_gate * up_proj).astype(bf16)
    mixed_out = contract_cols(hidden, down_cols).astype(bf16)
    mixed_out, back_all = tie(mixed_out, back_all)
    out_own = reduce_ctx(mixed_out)
    hidden_back = jnp.dot(back_all, down_cols, preferred_element_type=f32)
    gate_back = (
        hidden_back * up_proj * sigmoid_gate * (1.0 + gate_proj * (1.0 - sigmoid_gate))
    ).astype(bf16)
    upper_back = (hidden_back * silu_gate).astype(bf16)
    gate_up_back = jnp.concatenate(
        [gate_back[:, :main], upper_back[:, :main], gate_back[:, main:], upper_back[:, main:]],
        axis=1,
    )
    weighted = reduce_ctx(contract_cols(gate_up_back, gate_up).astype(bf16))
    gate_up_grad = contract_rows(normed_all, gate_up_back).astype(bf16)
    down_grad = contract_rows(back_all, hidden).astype(bf16)
    mlp_grads = [gate_up_grad, down_grad]
    out_own, *mlp_parts = tie(out_own, *seq_parts(mlp_grads))
    mlp_near = send_parts(mlp_parts)
    weighted, *mlp_near = tie(weighted, *mlp_near)
    weighted = weighted.astype(f32)
    residual_back = out_back.astype(f32) + scale_two * (
        weighted - shaped_two * jnp.mean(weighted * shaped_two, axis=-1, keepdims=True)
    )
    residual_low = residual_back.astype(bf16)
    low_all = gather_ctx(residual_low)
    residual_back, *mlp_near = tie(residual_back, *mlp_near)
    mlp_sums = far_sums(mlp_grads, *mlp_near[:2])
    mlp_grads_own = reduce_seq_far(mlp_grads, mlp_sums, *mlp_near[2:])
    mlp_grad = exchange_ctx(mlp_grads_own.reshape(8, rows, -1))
    attn_back = contract_cols(low_all, out_rows).astype(bf16)
    query_back, key_back, value_back = attend_back(
        edge, queries, keys, values, attn_back, score_scale
    )
    key_low = turn(key_back, cosine, -sine_table).astype(bf16)
    value_low = value_back.astype(bf16)
    other_back = jnp.where(core == 0, value_low, key_low)
    other_part = contract_rows(shaped_all, other_back).astype(bf16)
    heads_back = jnp.concatenate(
        [
            turn(query_back, cosine, -sine_table).astype(bf16),
            jnp.where(core == 0, key_low, value_low),
        ],
        axis=1,
    )
    heads_back, other_part = tie(heads_back, other_part)
    other_part = swap_cores(other_part)
    weighted_part = contract_cols(
        jnp.concatenate([heads_back, other_back], axis=1),
        jnp.concatenate([attn_cols, other_cols], axis=1),
    ).astype(bf16)
    weighted_part, low_all, mlp_grad = tie(weighted_part, low_all, mlp_grad)
    weighted_one = reduce_ctx(weighted_part).astype(f32)
    attn_part = contract_rows(shaped_all, heads_back)
    own_part = attn_part[:, head_width:] + other_part.astype(f32)
    attn_grad_own = reduce_seq(
        [jnp.concatenate([attn_part[:, :head_width].astype(bf16), own_part.astype(bf16)], axis=1)]
    )
    out_grad = reduce_seq([contract_rows(attn_low, low_all).astype(bf16)]).astype(f32)
    attn_grad_own, mlp_grad = tie(attn_grad_own, mlp_grad)
    attn_grad = exchange_ctx(attn_grad_own.reshape(8, rows, -1))

    gate_rows = ff_rows(mlp_grad[:, :, :main], mlp_grad[:, :, 2 * main : 2 * main + tail]).astype(f32)
    up_rows = ff_rows(mlp_grad[:, :, main : 2 * main], mlp_grad[:, :, 2 * main + tail : both])
    up_rows = up_rows.astype(f32)
    down_grad = ff_rows(mlp_grad[:, :, both : both + main], mlp_grad[:, :, both + main :])
    down_grad = down_grad.astype(f32)
    scale_one = rms_scale(inputs)
    shaped_one = inputs * scale_one
    input_grad = residual_back + scale_one * (
        weighted_one - shaped_one * jnp.mean(weighted_one * shaped_one, axis=-1, keepdims=True)
    )
    block_output = (residual + out_own.astype(f32)).astype(bf16)
    attn_grad, out_grad, gate_rows, up_rows, down_grad, input_grad, block_output = tie(
        attn_grad, out_grad, gate_rows, up_rows, down_grad, input_grad, block_output
    )
    query_rows = from_head_slices(attn_grad[:, :, :head_width]).astype(f32)
    pair_rows = jnp.sum(attn_grad[:, :, head_width:].astype(f32).reshape(4, 2, rows, head_width), axis=0)
    key_rows, value_rows = pair_rows[0], pair_rows[1]

    def row_sum(weight, grad):
        return jnp.sum(weight.astype(f32) * grad, axis=1)

    attn_gain_grad = (
        row_sum(query_weight, query_rows)
        + row_sum(key_weight, key_rows)
        + row_sum(value_weight, value_rows)
    )
    mlp_gain_grad = row_sum(gate_weight, gate_rows) + row_sum(up_weight, up_rows)
    return (
        block_output[None],
        input_grad[None],
        attn_gain_grad,
        query_rows * gain_one,
        key_rows * gain_one,
        value_rows * gain_one,
        out_grad,
        mlp_gain_grad,
        gate_rows * gain_two,
        up_rows * gain_two,
        down_grad,
    )


def solution(mesh):
    placed = (
        P("seq", "ctx", None),
        P("seq", "ctx"),
        P("seq", None),
        P("seq", "ctx", None),
        P(("seq", "ctx")),
        P(("seq", "ctx"), None),
        P(("seq", "ctx"), None),
        P(("seq", "ctx"), None),
        P(("seq", "ctx"), None),
        P(("seq", "ctx")),
        P(("seq", "ctx"), None),
        P(("seq", "ctx"), None),
        P(("seq", "ctx"), None),
    )
    seq_count, ctx_count = mesh.shape["seq"], mesh.shape["ctx"]

    def run(*args):
        width = args[0].shape[2]
        fits = (
            seq_count == KV_HEADS == 4
            and ctx_count == HEADS // KV_HEADS == 8
            and width == seq_count * ctx_count * HEAD
        )
        return jax.shard_map(
            local_columns if fits else local_rows,
            mesh=mesh,
            in_specs=placed,
            out_specs=(
                P("seq", "ctx", None),
                P("seq", "ctx", None),
                P(("seq", "ctx")),
                P(("seq", "ctx"), None),
                P(("seq", "ctx"), None),
                P(("seq", "ctx"), None),
                P(("seq", "ctx"), None),
                P(("seq", "ctx")),
                P(("seq", "ctx"), None),
                P(("seq", "ctx"), None),
                P(("seq", "ctx"), None),
            ),
            check_vma=False,
        )(*args)

    return run
```

```python
import jax
import jax.numpy as jnp
from jax import lax
from jax.experimental import pallas as pl
from jax.experimental.pallas import tpu as pltpu
from jax.sharding import PartitionSpec as P

HEADS = 32
KV_HEADS = 4
HEAD = 64


EPSILON = 1e-05
MASKED = -1e30


def rope_tables(position, head_size):
    half_size = head_size // 2
    inverse = 1.0 / 10000.0 ** (jnp.arange(half_size, dtype=jnp.float32) * 2.0 / head_size)
    angles = position.astype(jnp.float32)[:, None] * inverse[None, :]
    cosine = jnp.cos(angles)
    sine_table = jnp.sin(angles)
    return (jnp.concatenate([cosine, cosine], -1), jnp.concatenate([sine_table, sine_table], -1))


def rotate(values, cosine, sine_table):
    half_size = values.shape[-1] // 2
    turned = jnp.concatenate([-values[..., half_size:], values[..., :half_size]], -1)
    return values * cosine[:, None, :] + turned * sine_table[:, None, :]


def rms_scale(inputs):
    return lax.rsqrt(jnp.mean(inputs * inputs, axis=-1, keepdims=True) + EPSILON)


def norm_back(inputs, row_scale, gain, upstream):
    shaped = inputs * row_scale
    weighted = upstream * gain
    gain_term = jnp.sum(upstream * shaped, axis=0)
    return (
        row_scale * (weighted - shaped * jnp.mean(weighted * shaped, axis=-1, keepdims=True)),
        gain_term,
    )


def contract_rows(left, right):
    return lax.dot_general(
        left, right, (((0,), (0,)), ((), ())), preferred_element_type=jnp.float32
    )


def contract_cols(left, right):
    return lax.dot_general(
        left, right, (((1,), (1,)), ((), ())), preferred_element_type=jnp.float32
    )


def local_rows(
    block_input,
    positions,
    segments,
    cotangent,
    attn_gain,
    query_weight,
    key_weight,
    value_weight,
    out_weight,
    mlp_gain,
    gate_weight,
    up_weight,
    down_weight,
):
    row_count = block_input.shape[1]
    group_size = HEADS // KV_HEADS
    score_scale = HEAD ** (-0.5)
    inputs = block_input[0].astype(jnp.float32)
    seg_all = segments[0]
    length = seg_all.shape[0]
    block_size = min(512, length)
    block_count = length // block_size
    first_row = lax.axis_index("ctx") * row_count
    query_index = first_row + jnp.arange(row_count, dtype=jnp.int32)
    seg_rows = lax.dynamic_slice_in_dim(seg_all, first_row, row_count)
    cosine, sine_table = rope_tables(positions[0], HEAD)
    starts = jnp.arange(block_count, dtype=jnp.int32) * block_size
    seg_blocks = seg_all.reshape(block_count, block_size)

    def key_mask(seg_block, block_start):
        key_index = block_start + jnp.arange(block_size, dtype=jnp.int32)
        return (seg_rows[:, None] == seg_block[None, :]) & (
            key_index[None, :] <= query_index[:, None]
        )

    def guarded(compute, running):
        result = compute(running)
        return result

    attn_params = (
        lax.all_gather(attn_gain, ("seq", "ctx"), axis=0, tiled=True),
        lax.all_gather(query_weight, ("seq", "ctx"), axis=0, tiled=True),
        lax.all_gather(key_weight, ("seq", "ctx"), axis=0, tiled=True),
        lax.all_gather(value_weight, ("seq", "ctx"), axis=0, tiled=True),
        lax.all_gather(out_weight, ("seq", "ctx"), axis=0, tiled=True),
    )
    gain_one = attn_params[0].astype(jnp.float32)
    scale_one = rms_scale(inputs)
    normed1 = (inputs * scale_one * gain_one).astype(jnp.bfloat16)
    query_raw = jnp.dot(normed1, attn_params[1], preferred_element_type=jnp.float32)
    key_raw = jnp.dot(normed1, attn_params[2], preferred_element_type=jnp.float32)
    value_raw = jnp.dot(normed1, attn_params[3], preferred_element_type=jnp.float32)
    queries = rotate(query_raw.reshape(row_count, HEADS, HEAD), cosine, sine_table).astype(
        jnp.bfloat16
    )
    keys_local = (
        rotate(key_raw.reshape(row_count, KV_HEADS, HEAD), cosine, sine_table)
        .astype(jnp.bfloat16)
        .reshape(row_count, KV_HEADS * HEAD)
    )
    values_local = value_raw.astype(jnp.bfloat16)
    keys_all, values_all = (
        lax.all_gather(keys_local, "ctx", axis=0, tiled=True),
        lax.all_gather(values_local, "ctx", axis=0, tiled=True),
    )
    key_blocks = keys_all.reshape(block_count, block_size, KV_HEADS, HEAD)
    value_blocks = values_all.reshape(block_count, block_size, KV_HEADS, HEAD)
    query_group = queries.reshape(row_count, KV_HEADS, group_size, HEAD)

    def block_scores(key_block, allowed):
        scores = (
            jnp.einsum("tkgd,jkd->kgtj", query_group, key_block, preferred_element_type=jnp.float32)
            * score_scale
        )
        return jnp.where(allowed[None, None], scores, MASKED)

    def max_step(carry, pieces):
        key_block, seg_block, block_start = pieces
        allowed = key_mask(seg_block, block_start)

        def compute(running):
            run_max, run_sum = running
            scores = block_scores(key_block, allowed)
            new_max = jnp.maximum(run_max, jnp.max(scores, axis=-1))
            exponents = jnp.where(allowed[None, None], jnp.exp(scores - new_max[..., None]), 0.0)
            return (new_max, run_sum * jnp.exp(run_max - new_max) + jnp.sum(exponents, axis=-1))

        return (guarded(compute, carry), None)

    start_max = jnp.full((KV_HEADS, group_size, row_count), MASKED, jnp.float32)
    start_sum = jnp.zeros((KV_HEADS, group_size, row_count), jnp.float32)
    (run_max, run_sum), unused = lax.scan(
        max_step, (start_max, start_sum), (key_blocks, seg_blocks, starts)
    )
    log_sum = run_max + jnp.log(run_sum)

    def block_soft(key_block, allowed):
        scores = block_scores(key_block, allowed)
        return jnp.where(allowed[None, None], jnp.exp(scores - log_sum[..., None]), 0.0)

    def value_step(carry, pieces):
        key_block, value_block, seg_block, block_start = pieces
        allowed = key_mask(seg_block, block_start)

        def compute(running):
            acc_out, acc_fix = running
            soft_weights = block_soft(key_block, allowed)
            rounded = soft_weights.astype(jnp.bfloat16)
            leftover = (soft_weights - rounded.astype(jnp.float32)).astype(jnp.bfloat16)
            acc_out = acc_out + jnp.einsum(
                "kgtj,jkd->tkgd", rounded, value_block, preferred_element_type=jnp.float32
            )
            acc_fix = acc_fix + jnp.einsum(
                "kgtj,jkd->tkgd", leftover, value_block, preferred_element_type=jnp.float32
            )
            return (acc_out, acc_fix)

        return (guarded(compute, carry), None)

    zero_mix = jnp.zeros((row_count, KV_HEADS, group_size, HEAD), jnp.float32)
    (acc_out, acc_fix), unused = lax.scan(
        value_step, (zero_mix, zero_mix), (key_blocks, value_blocks, seg_blocks, starts)
    )
    attn_low = acc_out.reshape(row_count, HEADS * HEAD).astype(jnp.bfloat16)
    full_mix = acc_out + acc_fix
    residual = inputs + jnp.dot(attn_low, attn_params[4], preferred_element_type=jnp.float32)
    mlp_params = (
        lax.all_gather(mlp_gain, ("seq", "ctx"), axis=0, tiled=True),
        lax.all_gather(gate_weight, ("seq", "ctx"), axis=0, tiled=True),
        lax.all_gather(up_weight, ("seq", "ctx"), axis=0, tiled=True),
        lax.all_gather(down_weight, ("seq", "ctx"), axis=0, tiled=True),
    )
    gain_two = mlp_params[0].astype(jnp.float32)
    scale_two = rms_scale(residual)
    normed2 = (residual * scale_two * gain_two).astype(jnp.bfloat16)
    gate_proj = jnp.dot(normed2, mlp_params[1], preferred_element_type=jnp.float32)
    up_proj = jnp.dot(normed2, mlp_params[2], preferred_element_type=jnp.float32)
    sigmoid_gate = jax.nn.sigmoid(gate_proj)
    silu_gate = gate_proj * sigmoid_gate
    hidden = (silu_gate * up_proj).astype(jnp.bfloat16)
    block_output = (residual + contract_cols(hidden, mlp_params[3])).astype(jnp.bfloat16)
    out_back = cotangent[0]
    out_float = out_back.astype(jnp.float32)
    mlp_again = (
        lax.all_gather(mlp_gain, ("seq", "ctx"), axis=0, tiled=True),
        lax.all_gather(gate_weight, ("seq", "ctx"), axis=0, tiled=True),
        lax.all_gather(up_weight, ("seq", "ctx"), axis=0, tiled=True),
        lax.all_gather(down_weight, ("seq", "ctx"), axis=0, tiled=True),
    )
    down_grad = lax.psum_scatter(
        contract_rows(out_back, hidden), ("seq", "ctx"), scatter_dimension=0, tiled=True
    )
    hidden_back = jnp.dot(out_back, mlp_again[3], preferred_element_type=jnp.float32)
    gate_back = (
        hidden_back * up_proj * sigmoid_gate * (1.0 + gate_proj * (1.0 - sigmoid_gate))
    ).astype(jnp.bfloat16)
    upper_back = (hidden_back * silu_gate).astype(jnp.bfloat16)
    gate_full_grad = contract_rows(normed2, gate_back)
    up_full_grad = contract_rows(normed2, upper_back)
    normed2_back = contract_cols(gate_back, mlp_again[1]) + contract_cols(upper_back, mlp_again[2])
    residual_norm, mlp_gain_term = norm_back(
        residual, scale_two, mlp_again[0].astype(jnp.float32), normed2_back
    )
    mlp_sums = (
        lax.psum_scatter(mlp_gain_term, ("seq", "ctx"), scatter_dimension=0, tiled=True),
        lax.psum_scatter(gate_full_grad, ("seq", "ctx"), scatter_dimension=0, tiled=True),
        lax.psum_scatter(up_full_grad, ("seq", "ctx"), scatter_dimension=0, tiled=True),
    )
    residual_back = out_float + residual_norm
    attn_again = (
        lax.all_gather(attn_gain, ("seq", "ctx"), axis=0, tiled=True),
        lax.all_gather(query_weight, ("seq", "ctx"), axis=0, tiled=True),
        lax.all_gather(key_weight, ("seq", "ctx"), axis=0, tiled=True),
        lax.all_gather(value_weight, ("seq", "ctx"), axis=0, tiled=True),
        lax.all_gather(out_weight, ("seq", "ctx"), axis=0, tiled=True),
    )
    residual_low = residual_back.astype(jnp.bfloat16)
    out_full_grad = contract_rows(attn_low, residual_low)
    attn_back = contract_cols(residual_low, attn_again[4]).astype(jnp.bfloat16)
    grad_mix = attn_back.reshape(row_count, KV_HEADS, group_size, HEAD)
    delta_rows = jnp.transpose(jnp.sum(grad_mix.astype(jnp.float32) * full_mix, axis=-1), (1, 2, 0))

    def grad_step(carry, pieces):
        key_block, value_block, seg_block, block_start = pieces
        allowed = key_mask(seg_block, block_start)

        def compute(acc_query):
            soft_weights = block_soft(key_block, allowed)
            rounded = soft_weights.astype(jnp.bfloat16)
            value_part = jnp.einsum(
                "kgtj,tkgd->jkd", rounded, grad_mix, preferred_element_type=jnp.float32
            )
            soft_back = jnp.einsum(
                "tkgd,jkd->kgtj", grad_mix, value_block, preferred_element_type=jnp.float32
            )
            score_back = (soft_weights * (soft_back - delta_rows[..., None])).astype(jnp.bfloat16)
            acc_query = acc_query + jnp.einsum(
                "kgtj,jkd->tkgd", score_back, key_block, preferred_element_type=jnp.float32
            )
            key_part = jnp.einsum(
                "kgtj,tkgd->jkd", score_back, query_group, preferred_element_type=jnp.float32
            )
            return (acc_query, (key_part, value_part))

        return guarded(compute, carry)

    acc_query, (key_parts, value_parts) = lax.scan(
        grad_step, zero_mix, (key_blocks, value_blocks, seg_blocks, starts)
    )
    key_sums, value_sums = (
        lax.psum_scatter(
            key_parts.reshape(length, KV_HEADS * HEAD).astype(jnp.bfloat16),
            "ctx",
            scatter_dimension=0,
            tiled=True,
        ).astype(jnp.float32),
        lax.psum_scatter(
            value_parts.reshape(length, KV_HEADS * HEAD).astype(jnp.bfloat16),
            "ctx",
            scatter_dimension=0,
            tiled=True,
        ).astype(jnp.float32),
    )
    query_low = (
        rotate((acc_query * score_scale).reshape(row_count, HEADS, HEAD), cosine, -sine_table)
        .astype(jnp.bfloat16)
        .reshape(row_count, HEADS * HEAD)
    )
    key_low = (
        rotate((key_sums * score_scale).reshape(row_count, KV_HEADS, HEAD), cosine, -sine_table)
        .astype(jnp.bfloat16)
        .reshape(row_count, KV_HEADS * HEAD)
    )
    value_low = value_sums.astype(jnp.bfloat16)
    query_full_grad = contract_rows(normed1, query_low)
    key_full_grad = contract_rows(normed1, key_low)
    value_full_grad = contract_rows(normed1, value_low)
    normed1_back = (
        contract_cols(query_low, attn_again[1])
        + contract_cols(key_low, attn_again[2])
        + contract_cols(value_low, attn_again[3])
    )
    input_norm, attn_gain_term = norm_back(
        inputs, scale_one, attn_again[0].astype(jnp.float32), normed1_back
    )
    attn_sums = (
        lax.psum_scatter(attn_gain_term, ("seq", "ctx"), scatter_dimension=0, tiled=True),
        lax.psum_scatter(query_full_grad, ("seq", "ctx"), scatter_dimension=0, tiled=True),
        lax.psum_scatter(key_full_grad, ("seq", "ctx"), scatter_dimension=0, tiled=True),
        lax.psum_scatter(value_full_grad, ("seq", "ctx"), scatter_dimension=0, tiled=True),
        lax.psum_scatter(out_full_grad, ("seq", "ctx"), scatter_dimension=0, tiled=True),
    )
    input_grad = residual_back + input_norm
    return (
        block_output[None],
        input_grad[None],
        attn_sums[0],
        attn_sums[1],
        attn_sums[2],
        attn_sums[3],
        attn_sums[4],
        mlp_sums[0],
        mlp_sums[1],
        mlp_sums[2],
        down_grad,
    )


SEQ_X = [(0, 1), (1, 0), (2, 3), (3, 2)]
SEQ_Y = [(0, 2), (2, 0), (1, 3), (3, 1)]


def gather_ctx(block):
    return lax.all_gather(block, "ctx", axis=0, tiled=True)


def reduce_ctx(partial):
    return lax.psum_scatter(partial, "ctx", scatter_dimension=0, tiled=True)


def exchange_ctx(pieces):
    return lax.all_to_all(pieces, "ctx", 0, 0, tiled=True)


def gather_seq_near(block):
    return lax.ppermute(block, "seq", SEQ_X), lax.ppermute(block, "seq", SEQ_Y)


def gather_seq_far(block, from_x, from_y):
    rows, width = block.shape
    half = rows // 2
    mine = lax.axis_index("seq")
    far_top = lax.ppermute(from_x[:half], "seq", SEQ_Y)
    far_low = lax.ppermute(from_y[half:], "seq", SEQ_X)
    whole = jnp.zeros((4 * rows, width), block.dtype)
    for piece, start in (
        (block, mine * rows),
        (from_x, (mine ^ 1) * rows),
        (from_y, (mine ^ 2) * rows),
        (far_top, (mine ^ 3) * rows),
        (far_low, (mine ^ 3) * rows + half),
    ):
        whole = lax.dynamic_update_slice_in_dim(whole, piece, start, 0)
    return whole


def gather_seq(block):
    return gather_seq_far(block, *gather_seq_near(block))


def seq_part(partials, other, low):
    rows = partials[0].shape[0] // 4
    half = rows // 2
    start = (lax.axis_index("seq") ^ other) * rows + (half if low else 0)
    return jnp.concatenate(
        [lax.dynamic_slice_in_dim(partial, start, half, 0) for partial in partials], axis=1
    )


def seq_parts(partials):
    return (
        seq_part(partials, 3, False),
        seq_part(partials, 3, True),
        seq_part(partials, 1, False),
        seq_part(partials, 2, True),
    )


def send_parts(parts):
    return tuple(
        lax.ppermute(part, "seq", axis) for part, axis in zip(parts, (SEQ_X, SEQ_Y) * 2)
    )


def reduce_seq_near(partials):
    return send_parts(seq_parts(partials))


def add_wide(*terms):
    total = terms[0].astype(jnp.float32)
    for term in terms[1:]:
        total = total + term.astype(jnp.float32)
    return total


def far_sums(partials, top_far, low_far):
    return (
        add_wide(seq_part(partials, 2, False), top_far).astype(jnp.bfloat16),
        add_wide(seq_part(partials, 1, True), low_far).astype(jnp.bfloat16),
    )


def reduce_seq_far(partials, sums, top_near, low_near):
    top_send, low_send = sums
    top_last = lax.ppermute(top_send, "seq", SEQ_Y)
    low_last = lax.ppermute(low_send, "seq", SEQ_X)
    return jnp.concatenate(
        [
            add_wide(seq_part(partials, 0, False), top_near, top_last),
            add_wide(seq_part(partials, 0, True), low_near, low_last),
        ],
        axis=0,
    ).astype(jnp.bfloat16)


def reduce_seq(partials):
    top_far, low_far, *nears = reduce_seq_near(partials)
    return reduce_seq_far(partials, far_sums(partials, top_far, low_far), *nears)


def tie(*values):
    return lax.optimization_barrier(values)


def swap_cores(block):
    return lax.ppermute(block, "ctx", [(device, device ^ 1) for device in range(8)])


def ff_split(width):
    main = width // 8 // 128 * 128
    return main, width // 8 - main


def ff_slices(weight):
    rows, width = weight.shape
    main, tail = ff_split(width)
    return (
        jnp.transpose(weight[:, : 8 * main].reshape(rows, 8, main), (1, 0, 2)),
        jnp.transpose(weight[:, 8 * main :].reshape(rows, 8, tail), (1, 0, 2)),
    )


def ff_rows(main, tail):
    count, rows, width = main.shape
    return jnp.concatenate(
        [
            jnp.transpose(main, (1, 0, 2)).reshape(rows, count * width),
            jnp.transpose(tail, (1, 0, 2)).reshape(rows, count * tail.shape[2]),
        ],
        axis=1,
    )


def head_slices(weight):
    rows = weight.shape[0]
    split = weight.reshape(rows, KV_HEADS, 8, HEAD)
    return jnp.transpose(split, (2, 0, 1, 3)).reshape(8, rows, KV_HEADS * HEAD)


def from_head_slices(pieces):
    rows = pieces.shape[1]
    split = pieces.reshape(8, rows, KV_HEADS, HEAD)
    return jnp.transpose(split, (1, 2, 0, 3)).reshape(rows, HEADS * HEAD)


def attend_mask(edge, first_row, block, span):
    row = first_row + lax.broadcasted_iota(jnp.int32, (block, span), 0)
    column = lax.broadcasted_iota(jnp.int32, (block, span), 1)
    return (column <= row) & (column >= jnp.where(row >= edge, edge, 0))


def soft_rows(query, key, allowed):
    scores = lax.dot_general(
        query, key, (((1,), (1,)), ((), ())), preferred_element_type=jnp.float32
    )
    scores = jnp.where(allowed, scores, MASKED)
    exponents = jnp.exp(scores - jnp.max(scores, axis=-1, keepdims=True))
    return exponents * (1.0 / jnp.sum(exponents, axis=-1, keepdims=True))


def attend_kernel(edge_ref, query_ref, key_ref, value_ref, mix_ref, *, block, blocks):
    step = pl.program_id(1)
    for index in range(blocks):

        @pl.when(step == index)
        def _(index=index):
            span = (index + 1) * block
            allowed = attend_mask(edge_ref[0], index * block, block, span)
            mixed = []
            for head in range(2):
                cut = slice(head * HEAD, (head + 1) * HEAD)
                soft = soft_rows(query_ref[:, cut], key_ref[:span, cut], allowed)
                mixed.append(
                    jnp.dot(
                        soft.astype(jnp.bfloat16),
                        value_ref[:span, cut],
                        preferred_element_type=jnp.float32,
                    )
                )
            mix_ref[...] = jnp.concatenate(mixed, axis=-1).astype(mix_ref.dtype)


def attend_back_kernel(
    edge_ref,
    query_ref,
    key_ref,
    value_ref,
    back_ref,
    query_back_ref,
    key_back_ref,
    value_back_ref,
    *,
    block,
    blocks,
    score_scale,
):
    step = pl.program_id(1)

    @pl.when(step == 0)
    def _():
        key_back_ref[...] = jnp.zeros_like(key_back_ref)
        value_back_ref[...] = jnp.zeros_like(value_back_ref)

    for index in range(blocks):

        @pl.when(step == index)
        def _(index=index):
            span = (index + 1) * block
            allowed = attend_mask(edge_ref[0], index * block, block, span)
            query_parts, key_parts, value_parts = [], [], []
            for head in range(2):
                cut = slice(head * HEAD, (head + 1) * HEAD)
                query, key = query_ref[:, cut], key_ref[:span, cut]
                back = back_ref[:, cut]
                soft = soft_rows(query, key, allowed)
                soft_back = contract_cols(back, value_ref[:span, cut])
                delta = jnp.sum(soft * soft_back, axis=-1, keepdims=True)
                score_back = (soft * (soft_back - delta)).astype(jnp.bfloat16)
                query_parts.append(
                    jnp.dot(score_back, key, preferred_element_type=jnp.float32) * score_scale
                )
                key_parts.append(contract_rows(score_back, query))
                value_parts.append(contract_rows(soft.astype(jnp.bfloat16), back))
            query_back_ref[...] = jnp.concatenate(query_parts, axis=-1)
            key_back_ref[:span, :] += jnp.concatenate(key_parts, axis=-1)
            value_back_ref[:span, :] += jnp.concatenate(value_parts, axis=-1)


def attend_specs(length, block):
    rows = pl.BlockSpec((block, 2 * HEAD), lambda pair, step: (step, pair))
    whole = pl.BlockSpec((length, 2 * HEAD), lambda pair, step: (0, pair))
    edge = pl.BlockSpec(memory_space=pltpu.SMEM)
    return edge, rows, whole


def attend_cost(length, width, products):
    return pl.CostEstimate(
        flops=8 * products * length * length * width,
        transcendentals=length * length * width // HEAD,
        bytes_accessed=(2 * products + 4) * length * width,
    )


def attend(edge, queries, keys, values):
    length, width = queries.shape
    block = 256
    blocks = length // block
    scalar, rows, whole = attend_specs(length, block)

    def body(*refs):
        attend_kernel(*refs, block=block, blocks=blocks)

    return pl.pallas_call(
        body,
        name="attend",
        grid=(width // (2 * HEAD), blocks),
        in_specs=[scalar, rows, whole, whole],
        out_specs=rows,
        out_shape=jax.ShapeDtypeStruct((length, width), jnp.bfloat16),
        cost_estimate=attend_cost(length, width, 2),
    )(edge, queries, keys, values)


def attend_back(edge, queries, keys, values, back, score_scale):
    length, width = queries.shape
    block = 256
    blocks = length // block
    scalar, rows, whole = attend_specs(length, block)

    def body(*refs):
        attend_back_kernel(*refs, block=block, blocks=blocks, score_scale=score_scale)

    shape = jax.ShapeDtypeStruct((length, width), jnp.float32)
    return pl.pallas_call(
        body,
        name="attend_back",
        grid=(width // (2 * HEAD), blocks),
        in_specs=[scalar, rows, whole, whole, rows],
        out_specs=(rows, whole, whole),
        out_shape=(shape, shape, shape),
        cost_estimate=attend_cost(length, width, 5),
    )(edge, queries, keys, values, back)


def turn(values, cosine, sine_table):
    half = HEAD // 2
    lane = lax.broadcasted_iota(jnp.int32, values.shape, 1) % HEAD
    turned = jnp.where(
        lane < half, -jnp.roll(values, -half, axis=1), jnp.roll(values, half, axis=1)
    )
    return values * cosine + turned * sine_table


def local_columns(
    block_input,
    positions,
    segments,
    cotangent,
    attn_gain,
    query_weight,
    key_weight,
    value_weight,
    out_weight,
    mlp_gain,
    gate_weight,
    up_weight,
    down_weight,
):
    f32, bf16 = jnp.float32, jnp.bfloat16
    score_scale = HEAD ** (-0.5)
    length = segments.shape[1]
    rows = query_weight.shape[0]
    head_width = KV_HEADS * HEAD
    inputs = block_input[0].astype(f32)
    out_back = cotangent[0]
    gain_one = attn_gain.astype(f32)[:, None]
    gain_two = mlp_gain.astype(f32)[:, None]

    def fold(weight, gain):
        return (weight.astype(f32) * gain).astype(bf16)

    inputs_all = gather_ctx(block_input[0])
    key_value = jnp.stack([fold(key_weight, gain_one), fold(value_weight, gain_one)])
    attn_pieces = jnp.concatenate(
        [
            head_slices(fold(query_weight, gain_one)),
            jnp.tile(key_value, (4, 1, 1)),
        ],
        axis=2,
    )
    main, tail = ff_split(gate_weight.shape[1])
    both = 2 * (main + tail)
    gate_main, gate_tail = ff_slices(fold(gate_weight, gain_two))
    up_main, up_tail = ff_slices(fold(up_weight, gain_two))
    down_pieces = jnp.concatenate(ff_slices(down_weight), axis=2)
    gate_up_pieces = jnp.concatenate([gate_main, up_main, gate_tail, up_tail], axis=2)
    attn_own = exchange_ctx(attn_pieces).reshape(8 * rows, 2 * head_width)
    edge = jnp.sum((segments[0] == 0).astype(jnp.int32))
    token = jnp.arange(length, dtype=jnp.int32)
    position = jnp.where(token < edge, token + (length - edge), token - edge)
    cosine, sine_table = rope_tables(position, HEAD)
    cosine = jnp.tile(cosine, (1, KV_HEADS))
    sine_table = jnp.tile(sine_table, (1, KV_HEADS))
    edge = edge[None]
    attn_own, down_pieces, gate_up_pieces, cosine, sine_table = tie(
        attn_own, down_pieces, gate_up_pieces, cosine, sine_table
    )
    attn_cols = gather_seq(attn_own)
    core = lax.axis_index("ctx") % 2
    other_cols = swap_cores(attn_cols[:, head_width:])
    out_rows = gather_seq(out_weight)
    down_own = exchange_ctx(down_pieces).reshape(8 * rows, -1)
    down_own, gate_up_pieces = tie(down_own, gate_up_pieces)
    gate_up_own = exchange_ctx(gate_up_pieces).reshape(8 * rows, -1)

    wide = inputs_all.astype(f32)
    shaped_all = (wide * rms_scale(wide)).astype(bf16)
    raw = jnp.dot(shaped_all, attn_cols, preferred_element_type=f32)
    raw_other = jnp.dot(shaped_all, other_cols, preferred_element_type=f32)
    raw, raw_other, down_own = tie(raw, raw_other, down_own)
    raw_own = raw[:, head_width:]
    down_near = gather_seq_near(down_own)
    queries = turn(raw[:, :head_width], cosine, sine_table).astype(bf16)
    keys = turn(jnp.where(core == 0, raw_own, raw_other), cosine, sine_table).astype(bf16)
    values = jnp.where(core == 0, raw_other, raw_own).astype(bf16)
    queries = queries * jnp.asarray(score_scale, bf16)
    attn_low = attend(edge, queries, keys, values)
    attn_low, out_rows, back_late, gate_up_own, *down_near = tie(
        attn_low, out_rows, out_back, gate_up_own, *down_near
    )
    gate_up_near = gather_seq_near(gate_up_own)
    down_cols = gather_seq_far(down_own, *down_near)
    mixed = jnp.dot(attn_low, out_rows, preferred_element_type=f32).astype(bf16)
    mixed_own = reduce_ctx(mixed)
    mixed_own, down_cols, *gate_up_near = tie(mixed_own, down_cols, *gate_up_near)
    residual = inputs + mixed_own.astype(f32)
    scale_two = rms_scale(residual)
    shaped_two = residual * scale_two
    shaped_low = shaped_two.astype(bf16)
    normed_all = gather_ctx(shaped_low)
    shaped_two, back_late = tie(shaped_two, back_late)
    gate_up = gather_seq_far(gate_up_own, *gate_up_near)
    back_all = gather_ctx(back_late)
    proj = jnp.dot(normed_all, gate_up, preferred_element_type=f32)

    def halves(left_tail, right_tail, left, right):
        return jnp.concatenate([left, left_tail], axis=1), jnp.concatenate([right, right_tail], axis=1)

    gate_proj, up_proj = halves(
        proj[:, 2 * main : 2 * main + tail],
        proj[:, 2 * main + tail :],
        proj[:, :main],
        proj[:, main : 2 * main],
    )
    sigmoid_gate = jax.nn.sigmoid(gate_proj)
    silu_gate = gate_proj * sigmoid_gate
    hidden = (silu_gate * up_proj).astype(bf16)
    mixed_out = contract_cols(hidden, down_cols).astype(bf16)
    mixed_out, back_all = tie(mixed_out, back_all)
    out_own = reduce_ctx(mixed_out)
    hidden_back = jnp.dot(back_all, down_cols, preferred_element_type=f32)
    gate_back = (
        hidden_back * up_proj * sigmoid_gate * (1.0 + gate_proj * (1.0 - sigmoid_gate))
    ).astype(bf16)
    upper_back = (hidden_back * silu_gate).astype(bf16)
    gate_up_back = jnp.concatenate(
        [gate_back[:, :main], upper_back[:, :main], gate_back[:, main:], upper_back[:, main:]],
        axis=1,
    )
    weighted = reduce_ctx(contract_cols(gate_up_back, gate_up).astype(bf16))
    gate_up_grad = contract_rows(normed_all, gate_up_back).astype(bf16)
    down_grad = contract_rows(back_all, hidden).astype(bf16)
    mlp_grads = [gate_up_grad, down_grad]
    out_own, *mlp_parts = tie(out_own, *seq_parts(mlp_grads))
    mlp_near = send_parts(mlp_parts)
    weighted, *mlp_near = tie(weighted, *mlp_near)
    weighted = weighted.astype(f32)
    residual_back = out_back.astype(f32) + scale_two * (
        weighted - shaped_two * jnp.mean(weighted * shaped_two, axis=-1, keepdims=True)
    )
    residual_low = residual_back.astype(bf16)
    low_all = gather_ctx(residual_low)
    residual_back, *mlp_near = tie(residual_back, *mlp_near)
    mlp_sums = far_sums(mlp_grads, *mlp_near[:2])
    mlp_grads_own = reduce_seq_far(mlp_grads, mlp_sums, *mlp_near[2:])
    mlp_grad = exchange_ctx(mlp_grads_own.reshape(8, rows, -1))
    attn_back = contract_cols(low_all, out_rows).astype(bf16)
    query_back, key_back, value_back = attend_back(
        edge, queries, keys, values, attn_back, score_scale
    )
    key_low = turn(key_back, cosine, -sine_table).astype(bf16)
    value_low = value_back.astype(bf16)
    other_back = jnp.where(core == 0, value_low, key_low)
    other_part = contract_rows(shaped_all, other_back).astype(bf16)
    heads_back = jnp.concatenate(
        [
            turn(query_back, cosine, -sine_table).astype(bf16),
            jnp.where(core == 0, key_low, value_low),
        ],
        axis=1,
    )
    heads_back, other_part = tie(heads_back, other_part)
    other_part = swap_cores(other_part)
    weighted_part = contract_cols(
        jnp.concatenate([heads_back, other_back], axis=1),
        jnp.concatenate([attn_cols, other_cols], axis=1),
    ).astype(bf16)
    weighted_part, low_all, mlp_grad = tie(weighted_part, low_all, mlp_grad)
    weighted_one = reduce_ctx(weighted_part).astype(f32)
    attn_part = contract_rows(shaped_all, heads_back)
    own_part = attn_part[:, head_width:] + other_part.astype(f32)
    attn_grad_own = reduce_seq(
        [jnp.concatenate([attn_part[:, :head_width].astype(bf16), own_part.astype(bf16)], axis=1)]
    )
    out_grad = reduce_seq([contract_rows(attn_low, low_all).astype(bf16)]).astype(f32)
    attn_grad_own, mlp_grad = tie(attn_grad_own, mlp_grad)
    attn_grad = exchange_ctx(attn_grad_own.reshape(8, rows, -1))

    gate_rows = ff_rows(mlp_grad[:, :, :main], mlp_grad[:, :, 2 * main : 2 * main + tail]).astype(f32)
    up_rows = ff_rows(mlp_grad[:, :, main : 2 * main], mlp_grad[:, :, 2 * main + tail : both])
    up_rows = up_rows.astype(f32)
    down_grad = ff_rows(mlp_grad[:, :, both : both + main], mlp_grad[:, :, both + main :])
    down_grad = down_grad.astype(f32)
    scale_one = rms_scale(inputs)
    shaped_one = inputs * scale_one
    input_grad = residual_back + scale_one * (
        weighted_one - shaped_one * jnp.mean(weighted_one * shaped_one, axis=-1, keepdims=True)
    )
    block_output = (residual + out_own.astype(f32)).astype(bf16)
    def row_sum(weight, grad):
        return jnp.sum(weight.astype(f32) * grad, axis=1)

    mlp_gain_grad = row_sum(gate_weight, gate_rows) + row_sum(up_weight, up_rows)
    gate_grad = gate_rows * gain_two
    up_grad = up_rows * gain_two
    attn_grad, out_grad, gate_grad, up_grad, down_grad, input_grad, block_output, mlp_gain_grad = tie(
        attn_grad, out_grad, gate_grad, up_grad, down_grad, input_grad, block_output, mlp_gain_grad
    )
    query_rows = from_head_slices(attn_grad[:, :, :head_width]).astype(f32)
    pair_rows = jnp.sum(attn_grad[:, :, head_width:].astype(f32).reshape(4, 2, rows, head_width), axis=0)
    key_rows, value_rows = pair_rows[0], pair_rows[1]

    attn_gain_grad = (
        row_sum(query_weight, query_rows)
        + row_sum(key_weight, key_rows)
        + row_sum(value_weight, value_rows)
    )
    return (
        block_output[None],
        input_grad[None],
        attn_gain_grad,
        query_rows * gain_one,
        key_rows * gain_one,
        value_rows * gain_one,
        out_grad,
        mlp_gain_grad,
        gate_grad,
        up_grad,
        down_grad,
    )


def solution(mesh):
    placed = (
        P("seq", "ctx", None),
        P("seq", "ctx"),
        P("seq", None),
        P("seq", "ctx", None),
        P(("seq", "ctx")),
        P(("seq", "ctx"), None),
        P(("seq", "ctx"), None),
        P(("seq", "ctx"), None),
        P(("seq", "ctx"), None),
        P(("seq", "ctx")),
        P(("seq", "ctx"), None),
        P(("seq", "ctx"), None),
        P(("seq", "ctx"), None),
    )
    seq_count, ctx_count = mesh.shape["seq"], mesh.shape["ctx"]

    def run(*args):
        width = args[0].shape[2]
        fits = (
            seq_count == KV_HEADS == 4
            and ctx_count == HEADS // KV_HEADS == 8
            and width == seq_count * ctx_count * HEAD
        )
        return jax.shard_map(
            local_columns if fits else local_rows,
            mesh=mesh,
            in_specs=placed,
            out_specs=(
                P("seq", "ctx", None),
                P("seq", "ctx", None),
                P(("seq", "ctx")),
                P(("seq", "ctx"), None),
                P(("seq", "ctx"), None),
                P(("seq", "ctx"), None),
                P(("seq", "ctx"), None),
                P(("seq", "ctx")),
                P(("seq", "ctx"), None),
                P(("seq", "ctx"), None),
                P(("seq", "ctx"), None),
            ),
            check_vma=False,
        )(*args)

    return run
```
